128 devices in a mesh: heads: 4 (over z), seq: 32 (over x, y, core).
Axes of the slice: x: 4, y: 4, z: 4, core: 2. Of those that a mesh axis runs over, the one named last changes fastest.
Arguments:
- queries: bfloat16 [8, 64, 128, 128], P(None, None, 'heads'), may hold values from -12 to 12
- prefix_keys: bfloat16 [192, 128, 8, 128], P('seq', None, 'heads'), may hold values from -6 to 6
- prefix_values: bfloat16 [192, 128, 8, 128], P('seq', None, 'heads'), may hold values from -6 to 6
- block_use: int32 [8, 192], P(None, 'seq'), may hold values 0 or 1
- private_keys: bfloat16 [8, 8192, 8, 128], P(None, 'seq', 'heads'), may hold values from -6 to 6
- private_values: bfloat16 [8, 8192, 8, 128], P(None, 'seq', 'heads'), may hold values from -6 to 6
- private_lengths: int32 [8], replicated, may hold values from 1 to 8192
- draft_keys: bfloat16 [8, 64, 8, 128], P(None, None, 'heads'), may hold values from -10 to 10
- draft_values: bfloat16 [8, 64, 8, 128], P(None, None, 'heads'), may hold values from -6 to 6
- parents: int32 [8, 64], replicated, may hold values from 0 to 62, as said below
- out_weight: bfloat16 [128, 128, 16384], P('heads', None, 'seq'), may hold values from -0.046875 to 0.046875
Outputs:
- mixed: float32 [8, 64, 16384], P('heads', None, 'seq')
The draws below stay inside these ranges and needn't reach their ends.
Inputs may be any that keep to these rules, and one draw needn't show every extreme that they name: parents[r, 0] = 0, parents[r, t] < t for t >= 1, and the parent of token 63 is token 62.
All inputs are finite; a program needn't handle non-finite values. No bound on the sum of `block_use` on one device may be relied on, other than what follows from the above.
Results may differ from the reference program's by a relative error of at most 0.0047.
Values may be sent and summed in bfloat16 or wider, within the bound.
A program may use at most 128 MiB of HBM per device.

```python
import math
import jax
import jax.numpy as jnp
from jax import lax

D = 16384
HQ = 128
KVH = 8
HD = 128
TREE = 64
BLK = 128
R = 8
NBLK = 192
PRIV = 8192


def draw_queries(key, part):
    base = jax.random.normal(jax.random.fold_in(key, 1), (R, TREE, HQ, HD), jnp.float32) * 2.5
    base = jnp.clip(base, -12.0, 12.0)
    return base.astype(jnp.bfloat16)


def draw_prefix_keys(key, part):
    base = jax.random.normal(jax.random.fold_in(key, 2), (NBLK, BLK, KVH, HD), jnp.float32)
    base = jnp.clip(base, -6.0, 6.0)
    return base.astype(jnp.bfloat16)


def draw_parents(key, part):
    places = jnp.arange(TREE, dtype=jnp.int32)
    upper = jnp.maximum(places, 1)
    picks = jax.random.randint(jax.random.fold_in(key, 3), (R, TREE), 0, upper[None, :])
    picks = jnp.where(places[None, :] == TREE - 1, TREE - 2, picks)
    return picks.astype(jnp.int32)


def plant(drawn, rng, smallest, largest):
    longest = drawn.shape.index(max(drawn.shape))
    spots = []
    for shift in (0, 1):
        where = [jax.random.randint(jax.random.fold_in(rng, axis), (), 0, length) for axis, length in enumerate(drawn.shape)]
        where[longest] = (where[longest] + shift) % drawn.shape[longest]
        spots.append(tuple(where))
    return drawn.at[spots[0]].set(smallest).at[spots[1]].set(largest)


def shard_levels(key, shape, cuts, smallest, high):
    gain, own = 1.0, jax.random.fold_in(key, 6)
    for axis_at, parts in cuts:
        heights = jnp.exp(jax.random.uniform(jax.random.fold_in(own, axis_at), (parts,), jnp.float32, smallest / len(cuts), high / len(cuts)))
        gain = gain * jnp.repeat(heights, shape[axis_at] // parts).reshape([-1 if axis == axis_at else 1 for axis in range(len(shape))])
    return gain


def normal_values(stream_key, dims, scale, most, shards=(), held_as=jnp.bfloat16):
    values = scale * jax.random.normal(stream_key, dims, jnp.float32)
    if shards:
        values = values * shard_levels(stream_key, dims, shards, -0.22, 0.18)
    return jnp.clip(values, -most, most).astype(held_as)


def setup_inputs(seed: int = 0) -> dict:
    arg_keys = jax.random.split(jax.random.key(seed), 12)
    queries = draw_queries(jax.random.fold_in(arg_keys[11], 71), 0)
    prefix_keys = draw_prefix_keys(jax.random.fold_in(arg_keys[11], 71), 0)
    prefix_values = normal_values(arg_keys[2], (NBLK, BLK, KVH, HD), 1.0, 6.0, ((0, 32), (2, 4)))
    block_use = plant((jax.random.randint(arg_keys[3], (R, NBLK), 0, 2) < 1).astype(jnp.int32), jax.random.fold_in(arg_keys[3], 1), 0, 1)
    private_keys = normal_values(arg_keys[4], (R, PRIV, KVH, HD), 1.0, 6.0, ((1, 32), (2, 4)))
    private_values = normal_values(arg_keys[5], (R, PRIV, KVH, HD), 1.0, 6.0, ((1, 32), (2, 4)))
    private_lengths = plant(jax.random.randint(arg_keys[6], (R,), 1, PRIV + 1), jax.random.fold_in(arg_keys[6], 1), 1, PRIV).astype(jnp.int32)
    draft_keys = normal_values(arg_keys[7], (R, TREE, KVH, HD), 2.0, 10.0, ((2, 4),))
    draft_values = normal_values(arg_keys[8], (R, TREE, KVH, HD), 1.0, 6.0, ((2, 4),))
    parents = draw_parents(jax.random.fold_in(arg_keys[11], 71), 0)
    out_weight = normal_values(arg_keys[10], (HQ, HD, D), (HQ * HD) ** -0.5, 0.046875, ((0, 4), (2, 32)))
    return {"queries": queries, "prefix_keys": prefix_keys, "prefix_values": prefix_values, "block_use": block_use, "private_keys": private_keys, "private_values": private_values, "private_lengths": private_lengths, "draft_keys": draft_keys, "draft_values": draft_values, "parents": parents, "out_weight": out_weight}


def ancestry(parents):
    tree_size = parents.shape[-1]
    places = jnp.arange(tree_size, dtype=jnp.int32)
    onestep = (parents[..., None] == places).astype(jnp.float32)
    ident = (places[:, None] == places[None, :]).astype(jnp.float32)
    reach = jnp.maximum(onestep, ident)
    for level in range(max(1, (tree_size - 1).bit_length())):
        reach = jnp.minimum(jnp.einsum('rij,rjk->rik', reach, reach, precision=lax.Precision.HIGHEST), 1.0)
    return reach

def reference(queries, prefix_keys, prefix_values, block_use, private_keys, private_values, private_lengths, draft_keys, draft_values, parents, out_weight):
    group_size = HQ // KVH
    scaling = 1.0 / math.sqrt(HD)
    reach = ancestry(parents)
    flat_keys = prefix_keys.reshape(NBLK * BLK, KVH, HD)
    flat_values = prefix_values.reshape(NBLK * BLK, KVH, HD)

    def per_request(item):
        query_rows, use_row, length, own_keys, own_values, tree_keys, tree_values, reach_row = item
        fixed_live = jnp.concatenate([jnp.repeat(use_row == 1, BLK), jnp.arange(PRIV, dtype=jnp.int32) < length])
        keys_all = jnp.concatenate([flat_keys, own_keys, tree_keys], 0)
        values_all = jnp.concatenate([flat_values, own_values, tree_values], 0)
        fixed_count = fixed_live.shape[0]
        live = jnp.concatenate([jnp.broadcast_to(fixed_live[None, None, :], (TREE, group_size, fixed_count)), jnp.broadcast_to((reach_row > 0.5)[:, None, :], (TREE, group_size, TREE))], -1).reshape(TREE * group_size, fixed_count + TREE)

        def per_head(head):
            head_queries = lax.dynamic_slice_in_dim(query_rows, head * group_size, group_size, 1).reshape(TREE * group_size, HD)
            head_keys = lax.dynamic_index_in_dim(keys_all, head, 1, keepdims=False)
            head_values = lax.dynamic_index_in_dim(values_all, head, 1, keepdims=False)
            scores = jnp.dot(head_queries, head_keys.T, preferred_element_type=jnp.float32) * scaling
            scores = jnp.where(live, scores, -1e+30)
            top = lax.optimization_barrier(jnp.max(scores, axis=-1, keepdims=True))
            weights = jnp.where(live, jnp.exp(scores - top), 0.0)
            totals = lax.optimization_barrier(jnp.sum(weights, axis=-1, keepdims=True))
            weighted = jnp.dot(weights.astype(jnp.bfloat16), head_values, preferred_element_type=jnp.float32)
            return (weighted / totals).astype(jnp.bfloat16).reshape(TREE, group_size, HD)
        outputs = lax.map(per_head, jnp.arange(KVH, dtype=jnp.int32))
        return jnp.transpose(outputs, (1, 0, 2, 3)).reshape(TREE, HQ, HD)
    attention = lax.map(per_request, (queries, block_use, private_lengths, private_keys, private_values, draft_keys, draft_values, reach))
    mixed = jnp.dot(attention.reshape(R * TREE, HQ * HD), out_weight.reshape(HQ * HD, D), preferred_element_type=jnp.float32)
    return mixed.reshape(R, TREE, D)
```

```python
import math

import jax
import jax.numpy as jnp
from jax import lax
from jax.sharding import PartitionSpec as P


def ancestry(parents):
    tree_size = parents.shape[-1]
    places = jnp.arange(tree_size, dtype=jnp.int32)
    onestep = (parents[..., None] == places).astype(jnp.float32)
    ident = (places[:, None] == places[None, :]).astype(jnp.float32)
    reach = jnp.maximum(onestep, ident)
    for level in range(max(1, (tree_size - 1).bit_length())):
        reach = jnp.minimum(
            jnp.einsum("rij,rjk->rik", reach, reach, precision=lax.Precision.HIGHEST), 1.0
        )
    return reach


def combine(first, second):
    top = jnp.maximum(first[0], second[0])
    first_factor = jnp.exp(first[0] - top)
    second_factor = jnp.exp(second[0] - top)
    totals = first[1] * first_factor + second[1] * second_factor
    weighted = first[2] * first_factor[..., None] + second[2] * second_factor[..., None]
    return (top, totals, weighted)


def draft_part(row_queries, tree_keys, tree_values, row_reach, scaling):
    requests, rows, heads_dev, head_dim = row_queries.shape
    kv_dev = tree_keys.shape[2]
    group_size = heads_dev // kv_dev
    grouped = row_queries.reshape(requests, rows, kv_dev, group_size, head_dim)
    scores = (
        jnp.einsum("rtkgd,rskd->rtkgs", grouped, tree_keys, preferred_element_type=jnp.float32)
        * scaling
    )
    live = (row_reach > 0.5)[:, :, None, None, :]
    scores = jnp.where(live, scores, -1e30)
    highest = jnp.max(scores, axis=-1)
    weights = jnp.where(live, jnp.exp(scores - highest[..., None]), 0.0)
    totals = jnp.sum(weights, axis=-1)
    weighted = jnp.einsum(
        "rtkgs,rskd->rtkgd",
        weights.astype(jnp.bfloat16),
        tree_values,
        preferred_element_type=jnp.float32,
    )
    return (
        highest.reshape(requests, rows, heads_dev),
        totals.reshape(requests, rows, heads_dev),
        weighted.reshape(requests, rows, heads_dev, head_dim),
    )


def local(
    queries,
    prefix_keys,
    prefix_values,
    block_use,
    private_keys,
    private_values,
    private_lengths,
    draft_keys,
    draft_values,
    parents,
    out_weight,
):
    tree_size = queries.shape[1]
    heads_dev = queries.shape[2]
    head_dim = queries.shape[3]
    kv_dev = prefix_keys.shape[2]
    group_size = heads_dev // kv_dev
    block_count = prefix_keys.shape[0]
    block_len = prefix_keys.shape[1]
    private_dev = private_keys.shape[1]
    scaling = 1.0 / math.sqrt(head_dim)
    shard_index = lax.axis_index("seq")
    prefix_flat_keys = prefix_keys.reshape(block_count * block_len, kv_dev, head_dim)
    prefix_flat_values = prefix_values.reshape(block_count * block_len, kv_dev, head_dim)
    positions = shard_index * private_dev + jnp.arange(private_dev, dtype=jnp.int32)
    reach = ancestry(parents)

    def one_request(item):
        query_rows, use_row, length, own_keys, own_values = item
        grouped = query_rows.reshape(tree_size, kv_dev, group_size, head_dim)
        prefix_live = jnp.repeat(use_row == 1, block_len)
        own_live = positions < length
        prefix_scores = (
            jnp.einsum(
                "tkgd,nkd->tkgn", grouped, prefix_flat_keys, preferred_element_type=jnp.float32
            )
            * scaling
        )
        own_scores = (
            jnp.einsum("tkgd,nkd->tkgn", grouped, own_keys, preferred_element_type=jnp.float32)
            * scaling
        )
        prefix_scores = jnp.where(prefix_live, prefix_scores, -1e30)
        own_scores = jnp.where(own_live, own_scores, -1e30)
        highest = jnp.maximum(jnp.max(prefix_scores, axis=-1), jnp.max(own_scores, axis=-1))
        prefix_weights = jnp.where(prefix_live, jnp.exp(prefix_scores - highest[..., None]), 0.0)
        own_weights = jnp.where(own_live, jnp.exp(own_scores - highest[..., None]), 0.0)
        totals = jnp.sum(prefix_weights, axis=-1) + jnp.sum(own_weights, axis=-1)
        weighted = jnp.einsum(
            "tkgn,nkd->tkgd",
            prefix_weights.astype(jnp.bfloat16),
            prefix_flat_values,
            preferred_element_type=jnp.float32,
        )
        weighted = weighted + jnp.einsum(
            "tkgn,nkd->tkgd",
            own_weights.astype(jnp.bfloat16),
            own_values,
            preferred_element_type=jnp.float32,
        )
        return (
            highest.reshape(tree_size, heads_dev),
            totals.reshape(tree_size, heads_dev),
            weighted.reshape(tree_size, heads_dev, head_dim),
        )

    highest, totals, weighted = lax.map(
        one_request, (queries, block_use, private_lengths, private_keys, private_values)
    )
    requests = queries.shape[0]
    seq_size = lax.axis_size("seq")
    row_count = requests * tree_size
    chunk = row_count // seq_size
    sent = weighted.astype(jnp.bfloat16).reshape(seq_size, chunk, heads_dev, head_dim)
    stats = jnp.stack([highest, totals], 0).reshape(2, seq_size, chunk, heads_dev)
    stats = jnp.transpose(stats, (1, 0, 2, 3))
    got = lax.all_to_all(sent, "seq", 0, 0, tiled=True)
    got_stats = lax.all_to_all(stats, "seq", 0, 0, tiled=True)
    part_top = got_stats[:, 0]
    part_totals = got_stats[:, 1]
    top_all = jnp.max(part_top, axis=0)
    factor = jnp.exp(part_top - top_all[None])
    summed_totals = jnp.sum(part_totals * factor, axis=0)
    summed_weighted = jnp.sum(got.astype(jnp.float32) * factor[..., None], axis=0)
    row0 = shard_index * chunk
    request = row0 // tree_size
    token0 = row0 % tree_size
    my_queries = lax.dynamic_slice_in_dim(
        queries.reshape(row_count, heads_dev, head_dim), row0, chunk, 0
    )[None]
    my_keys = lax.dynamic_index_in_dim(draft_keys, request, 0, keepdims=True)
    my_values = lax.dynamic_index_in_dim(draft_values, request, 0, keepdims=True)
    my_reach = lax.dynamic_slice_in_dim(
        lax.dynamic_index_in_dim(reach, request, 0, keepdims=True), token0, chunk, 1
    )
    draft = draft_part(my_queries, my_keys, my_values, my_reach, scaling)
    draft = (draft[0][0], draft[1][0], draft[2][0])
    final_top, final_totals, final_weighted = combine(
        (top_all, summed_totals, summed_weighted), draft
    )
    attention = (final_weighted / final_totals[..., None]).astype(jnp.bfloat16)
    attention = lax.all_gather(attention, "seq", axis=0, tiled=True)
    attention = attention.reshape(requests, tree_size, heads_dev, head_dim)
    return lax.psum_scatter(
        jnp.einsum("rthd,hde->rte", attention, out_weight, preferred_element_type=jnp.float32),
        "heads",
        scatter_dimension=0,
        tiled=True,
    )


def solution(mesh):
    return jax.shard_map(
        local,
        mesh=mesh,
        in_specs=(
            P(None, None, "heads", None),
            P("seq", None, "heads", None),
            P("seq", None, "heads", None),
            P(None, "seq"),
            P(None, "seq", "heads", None),
            P(None, "seq", "heads", None),
            P(),
            P(None, None, "heads", None),
            P(None, None, "heads", None),
            P(),
            P("heads", None, "seq"),
        ),
        out_specs=P("heads", None, "seq"),
        check_vma=False,
    )
```

```python
import math

import jax
import jax.numpy as jnp
from jax import lax
from jax.experimental import pallas as pl
from jax.experimental.pallas import tpu as pltpu
from jax.sharding import PartitionSpec as P


def ancestry(parents):
    tree_size = parents.shape[-1]
    places = jnp.arange(tree_size, dtype=jnp.int32)
    onestep = (parents[..., None] == places).astype(jnp.float32)
    ident = (places[:, None] == places[None, :]).astype(jnp.float32)
    reach = jnp.maximum(onestep, ident)
    for level in range(max(1, (tree_size - 1).bit_length())):
        reach = jnp.minimum(
            jnp.einsum("rij,rjk->rik", reach, reach, precision=lax.Precision.HIGHEST), 1.0
        )
    return reach


def combine(first, second):
    top = jnp.maximum(first[0], second[0])
    first_factor = jnp.exp(first[0] - top)
    second_factor = jnp.exp(second[0] - top)
    totals = first[1] * first_factor + second[1] * second_factor
    weighted = first[2] * first_factor[..., None] + second[2] * second_factor[..., None]
    return (top, totals, weighted)


def draft_part(row_queries, tree_keys, tree_values, row_reach, scaling):
    requests, rows, heads_dev, head_dim = row_queries.shape
    kv_dev = tree_keys.shape[2]
    group_size = heads_dev // kv_dev
    grouped = row_queries.reshape(requests, rows, kv_dev, group_size, head_dim)
    scores = (
        jnp.einsum("rtkgd,rskd->rtkgs", grouped, tree_keys, preferred_element_type=jnp.float32)
        * scaling
    )
    live = (row_reach > 0.5)[:, :, None, None, :]
    scores = jnp.where(live, scores, -1e30)
    highest = jnp.max(scores, axis=-1)
    weights = jnp.where(live, jnp.exp(scores - highest[..., None]), 0.0)
    totals = jnp.sum(weights, axis=-1)
    weighted = jnp.einsum(
        "rtkgs,rskd->rtkgd",
        weights.astype(jnp.bfloat16),
        tree_values,
        preferred_element_type=jnp.float32,
    )
    return (
        highest.reshape(requests, rows, heads_dev),
        totals.reshape(requests, rows, heads_dev),
        weighted.reshape(requests, rows, heads_dev, head_dim),
    )


def context_kernel(use_ref, len_ref, q_ref, kp_ref, vp_ref, ko_ref, vo_ref, acc_ref, st_ref):
    r = pl.program_id(1)
    scaling = 1.0 / math.sqrt(q_ref.shape[-1])
    q = q_ref[0].reshape(-1, q_ref.shape[-1])
    kp = kp_ref[0]
    ko = ko_ref[0, 0]
    dims = (((1,), (1,)), ((), ()))
    s_pre = lax.dot_general(kp, q, dims, preferred_element_type=jnp.float32) * scaling
    s_own = lax.dot_general(ko, q, dims, preferred_element_type=jnp.float32) * scaling
    n_pre = kp.shape[0]
    n_own = ko.shape[0]
    block_len = n_pre // use_ref.shape[1]
    block_id = lax.broadcasted_iota(jnp.int32, (n_pre, 1), 0) // block_len
    pre_live = jnp.zeros((n_pre, 1), jnp.bool_)
    for b in range(use_ref.shape[1]):
        pre_live = jnp.logical_or(pre_live, jnp.logical_and(block_id == b, use_ref[r, b] == 1))
    own_live = lax.broadcasted_iota(jnp.int32, (n_own, 1), 0) < len_ref[r]
    s_pre = jnp.where(pre_live, s_pre, -1e30)
    s_own = jnp.where(own_live, s_own, -1e30)
    top = jnp.maximum(
        jnp.max(s_pre, axis=0, keepdims=True), jnp.max(s_own, axis=0, keepdims=True)
    )
    w_pre = jnp.where(pre_live, jnp.exp(s_pre - top), 0.0)
    w_own = jnp.where(own_live, jnp.exp(s_own - top), 0.0)
    totals = jnp.sum(w_pre, axis=0, keepdims=True) + jnp.sum(w_own, axis=0, keepdims=True)
    acc = jnp.dot(vp_ref[0], w_pre.astype(jnp.bfloat16), preferred_element_type=jnp.float32)
    acc = acc + jnp.dot(
        vo_ref[0, 0], w_own.astype(jnp.bfloat16), preferred_element_type=jnp.float32
    )
    pieces = acc_ref.shape[1]
    width = acc_ref.shape[-1]
    for c in range(pieces):
        acc_ref[0, c, 0] = acc[:, c * width : (c + 1) * width].astype(acc_ref.dtype)
    st_ref[0, 0] = jnp.zeros(st_ref.shape[2:], jnp.float32)
    st_ref[0, 0, 0:1, :] = top
    st_ref[0, 0, 1:2, :] = totals


def context_part(queries, prefix_keys, prefix_values, use_rows, own_lengths, own_keys, own_values, pieces):
    requests, tree_size, heads_dev, head_dim = queries.shape
    block_count, block_len, kv_dev, _ = prefix_keys.shape
    group_size = heads_dev // kv_dev
    private_dev = own_keys.shape[1]
    n_pre = block_count * block_len
    rows = tree_size * group_size
    width = rows // pieces
    kp = jnp.transpose(prefix_keys.reshape(n_pre, kv_dev, head_dim), (1, 0, 2))
    vp = jnp.transpose(prefix_values.reshape(n_pre, kv_dev, head_dim), (1, 2, 0))
    ko = jnp.transpose(own_keys, (0, 2, 1, 3))
    vo = jnp.transpose(own_values, (0, 2, 3, 1))
    grid_spec = pltpu.PrefetchScalarGridSpec(
        num_scalar_prefetch=2,
        grid=(kv_dev, requests),
        in_specs=[
            pl.BlockSpec((1, tree_size, group_size, head_dim), lambda k, r, u, n: (r, 0, k, 0)),
            pl.BlockSpec((1, n_pre, head_dim), lambda k, r, u, n: (k, 0, 0)),
            pl.BlockSpec((1, head_dim, n_pre), lambda k, r, u, n: (k, 0, 0)),
            pl.BlockSpec((1, 1, private_dev, head_dim), lambda k, r, u, n: (r, k, 0, 0)),
            pl.BlockSpec((1, 1, head_dim, private_dev), lambda k, r, u, n: (r, k, 0, 0)),
        ],
        out_specs=[
            pl.BlockSpec((1, pieces, 1, head_dim, width), lambda k, r, u, n: (r, 0, k, 0, 0)),
            pl.BlockSpec((1, 1, 8, rows), lambda k, r, u, n: (r, k, 0, 0)),
        ],
    )
    acc, st = pl.pallas_call(
        context_kernel,
        grid_spec=grid_spec,
        out_shape=[
            jax.ShapeDtypeStruct((requests, pieces, kv_dev, head_dim, width), jnp.bfloat16),
            jax.ShapeDtypeStruct((requests, kv_dev, 8, rows), jnp.float32),
        ],
    )(use_rows, own_lengths, queries, kp, vp, ko, vo)
    return acc, st


def local(
    queries,
    prefix_keys,
    prefix_values,
    block_use,
    private_keys,
    private_values,
    private_lengths,
    draft_keys,
    draft_values,
    parents,
    out_weight,
):
    requests, tree_size, heads_dev, head_dim = queries.shape
    kv_dev = prefix_keys.shape[2]
    group_size = heads_dev // kv_dev
    private_dev = private_keys.shape[1]
    scaling = 1.0 / math.sqrt(head_dim)
    shard_index = lax.axis_index("seq")
    seq_size = lax.axis_size("seq")
    reach = ancestry(parents)
    row_count = requests * tree_size
    chunk = row_count // seq_size
    pieces = tree_size // chunk
    own_lengths = jnp.clip(private_lengths - shard_index * private_dev, 0, private_dev)
    acc, st = context_part(
        queries, prefix_keys, prefix_values, block_use, own_lengths, private_keys, private_values, pieces
    )
    width = chunk * group_size
    sent = acc.reshape(seq_size, kv_dev, head_dim, width)
    stats = st[:, :, :2, :].reshape(requests, kv_dev, 2, pieces, width)
    stats = jnp.transpose(stats, (0, 3, 2, 1, 4)).reshape(seq_size, 2, kv_dev, width)
    got = lax.all_to_all(sent, "seq", 0, 0, tiled=True)
    got_stats = lax.all_to_all(stats, "seq", 0, 0, tiled=True)
    part_top = got_stats[:, 0]
    part_totals = got_stats[:, 1]
    top_all = jnp.max(part_top, axis=0)
    factor = jnp.exp(part_top - top_all[None])
    summed_totals = jnp.sum(part_totals * factor, axis=0)
    summed_weighted = jnp.sum(got.astype(jnp.float32) * factor[:, :, None, :], axis=0)
    top_all = jnp.transpose(top_all.reshape(kv_dev, chunk, group_size), (1, 0, 2)).reshape(chunk, heads_dev)
    summed_totals = jnp.transpose(
        summed_totals.reshape(kv_dev, chunk, group_size), (1, 0, 2)
    ).reshape(chunk, heads_dev)
    summed_weighted = jnp.transpose(
        summed_weighted.reshape(kv_dev, head_dim, chunk, group_size), (2, 0, 3, 1)
    ).reshape(chunk, heads_dev, head_dim)
    row0 = shard_index * chunk
    request = row0 // tree_size
    token0 = row0 % tree_size
    my_queries = lax.dynamic_slice_in_dim(
        queries.reshape(row_count, heads_dev, head_dim), row0, chunk, 0
    )[None]
    my_keys = lax.dynamic_index_in_dim(draft_keys, request, 0, keepdims=True)
    my_values = lax.dynamic_index_in_dim(draft_values, request, 0, keepdims=True)
    my_reach = lax.dynamic_slice_in_dim(
        lax.dynamic_index_in_dim(reach, request, 0, keepdims=True), token0, chunk, 1
    )
    draft = draft_part(my_queries, my_keys, my_values, my_reach, scaling)
    draft = (draft[0][0], draft[1][0], draft[2][0])
    final_top, final_totals, final_weighted = combine(
        (top_all, summed_totals, summed_weighted), draft
    )
    attention = (final_weighted / final_totals[..., None]).astype(jnp.bfloat16)
    attention = lax.all_gather(attention, "seq", axis=0, tiled=True)
    attention = attention.reshape(requests, tree_size, heads_dev, head_dim)
    return lax.psum_scatter(
        jnp.einsum("rthd,hde->rte", attention, out_weight, preferred_element_type=jnp.float32),
        "heads",
        scatter_dimension=0,
        tiled=True,
    )


def solution(mesh):
    return jax.shard_map(
        local,
        mesh=mesh,
        in_specs=(
            P(None, None, "heads", None),
            P("seq", None, "heads", None),
            P("seq", None, "heads", None),
            P(None, "seq"),
            P(None, "seq", "heads", None),
            P(None, "seq", "heads", None),
            P(),
            P(None, None, "heads", None),
            P(None, None, "heads", None),
            P(),
            P("heads", None, "seq"),
        ),
        out_specs=P("heads", None, "seq"),
        check_vma=False,
    )
```

```python
import math

import jax
import jax.numpy as jnp
from jax import lax
from jax.experimental import pallas as pl
from jax.experimental.pallas import tpu as pltpu
from jax.sharding import PartitionSpec as P


def ancestry(parents):
    tree_size = parents.shape[-1]
    places = jnp.arange(tree_size, dtype=jnp.int32)
    onestep = (parents[..., None] == places).astype(jnp.float32)
    ident = (places[:, None] == places[None, :]).astype(jnp.float32)
    reach = jnp.maximum(onestep, ident)
    for level in range(max(1, (tree_size - 1).bit_length())):
        reach = jnp.minimum(
            jnp.einsum("rij,rjk->rik", reach, reach, precision=lax.Precision.HIGHEST), 1.0
        )
    return reach


def combine(first, second):
    top = jnp.maximum(first[0], second[0])
    first_factor = jnp.exp(first[0] - top)
    second_factor = jnp.exp(second[0] - top)
    totals = first[1] * first_factor + second[1] * second_factor
    weighted = first[2] * first_factor[..., None] + second[2] * second_factor[..., None]
    return (top, totals, weighted)


def draft_part(row_queries, tree_keys, tree_values, row_reach, scaling):
    requests, rows, heads_dev, head_dim = row_queries.shape
    kv_dev = tree_keys.shape[2]
    group_size = heads_dev // kv_dev
    grouped = row_queries.reshape(requests, rows, kv_dev, group_size, head_dim)
    scores = (
        jnp.einsum("rtkgd,rskd->rtkgs", grouped, tree_keys, preferred_element_type=jnp.float32)
        * scaling
    )
    live = (row_reach > 0.5)[:, :, None, None, :]
    scores = jnp.where(live, scores, -1e30)
    highest = jnp.max(scores, axis=-1)
    weights = jnp.where(live, jnp.exp(scores - highest[..., None]), 0.0)
    totals = jnp.sum(weights, axis=-1)
    weighted = jnp.einsum(
        "rtkgs,rskd->rtkgd",
        weights.astype(jnp.bfloat16),
        tree_values,
        preferred_element_type=jnp.float32,
    )
    return (
        highest.reshape(requests, rows, heads_dev),
        totals.reshape(requests, rows, heads_dev),
        weighted.reshape(requests, rows, heads_dev, head_dim),
    )


def context_kernel(use_ref, len_ref, q_ref, kp_ref, vp_ref, ko_ref, vo_ref, acc_ref):
    r = pl.program_id(1)
    scaling = 1.0 / math.sqrt(q_ref.shape[-1])
    q = q_ref[0].reshape(-1, q_ref.shape[-1])
    kp = kp_ref[0]
    ko = ko_ref[0, 0]
    dims = (((1,), (1,)), ((), ()))
    s_pre = lax.dot_general(kp, q, dims, preferred_element_type=jnp.float32) * scaling
    s_own = lax.dot_general(ko, q, dims, preferred_element_type=jnp.float32) * scaling
    n_pre = kp.shape[0]
    n_own = ko.shape[0]
    block_len = n_pre // use_ref.shape[1]
    block_id = lax.broadcasted_iota(jnp.int32, (n_pre, 1), 0) // block_len
    pre_live = jnp.zeros((n_pre, 1), jnp.bool_)
    for b in range(use_ref.shape[1]):
        pre_live = jnp.logical_or(pre_live, jnp.logical_and(block_id == b, use_ref[r, b] == 1))
    own_live = lax.broadcasted_iota(jnp.int32, (n_own, 1), 0) < len_ref[r]
    s_pre = jnp.where(pre_live, s_pre, -1e30)
    s_own = jnp.where(own_live, s_own, -1e30)
    top = jnp.maximum(
        jnp.max(s_pre, axis=0, keepdims=True), jnp.max(s_own, axis=0, keepdims=True)
    )
    top = jnp.maximum(top, -1e29).astype(jnp.bfloat16).astype(jnp.float32)
    w_pre = jnp.exp(s_pre - top)
    w_own = jnp.exp(s_own - top)
    totals = jnp.sum(w_pre, axis=0, keepdims=True) + jnp.sum(w_own, axis=0, keepdims=True)
    acc = jnp.dot(vp_ref[0], w_pre.astype(jnp.bfloat16), preferred_element_type=jnp.float32)
    acc = acc + jnp.dot(
        vo_ref[0, 0], w_own.astype(jnp.bfloat16), preferred_element_type=jnp.float32
    )
    head_dim = acc.shape[0]
    pieces = acc_ref.shape[1]
    width = acc_ref.shape[-1]
    extra = acc_ref.shape[3] - head_dim
    high = totals.astype(jnp.bfloat16).astype(jnp.float32)
    low = totals - high
    row_id = lax.broadcasted_iota(jnp.int32, (extra, totals.shape[1]), 0)
    stats = jnp.where(row_id == 0, top, jnp.where(row_id == 1, high, jnp.where(row_id == 2, low, 0.0)))
    for c in range(pieces):
        acc_ref[0, c, 0, 0:head_dim, :] = acc[:, c * width : (c + 1) * width].astype(acc_ref.dtype)
        acc_ref[0, c, 0, head_dim:, :] = stats[:, c * width : (c + 1) * width].astype(acc_ref.dtype)


def context_part(queries, prefix_keys, prefix_values, use_rows, own_lengths, own_keys, own_values, pieces):
    requests, tree_size, heads_dev, head_dim = queries.shape
    block_count, block_len, kv_dev, _ = prefix_keys.shape
    group_size = heads_dev // kv_dev
    private_dev = own_keys.shape[1]
    n_pre = block_count * block_len
    rows = tree_size * group_size
    width = rows // pieces
    kp = jnp.transpose(prefix_keys.reshape(n_pre, kv_dev, head_dim), (1, 0, 2))
    vp = jnp.transpose(prefix_values.reshape(n_pre, kv_dev, head_dim), (1, 2, 0))
    ko = jnp.transpose(own_keys, (0, 2, 1, 3))
    vo = jnp.transpose(own_values, (0, 2, 3, 1))
    grid_spec = pltpu.PrefetchScalarGridSpec(
        num_scalar_prefetch=2,
        grid=(kv_dev, requests),
        in_specs=[
            pl.BlockSpec((1, tree_size, group_size, head_dim), lambda k, r, u, n: (r, 0, k, 0)),
            pl.BlockSpec((1, n_pre, head_dim), lambda k, r, u, n: (k, 0, 0)),
            pl.BlockSpec((1, head_dim, n_pre), lambda k, r, u, n: (k, 0, 0)),
            pl.BlockSpec((1, 1, private_dev, head_dim), lambda k, r, u, n: (r, k, 0, 0)),
            pl.BlockSpec((1, 1, head_dim, private_dev), lambda k, r, u, n: (r, k, 0, 0)),
        ],
        out_specs=pl.BlockSpec(
            (1, pieces, 1, head_dim + 16, width), lambda k, r, u, n: (r, 0, k, 0, 0)
        ),
    )
    return pl.pallas_call(
        context_kernel,
        grid_spec=grid_spec,
        out_shape=jax.ShapeDtypeStruct(
            (requests, pieces, kv_dev, head_dim + 16, width), jnp.bfloat16
        ),
    )(use_rows, own_lengths, queries, kp, vp, ko, vo)


def local(
    queries,
    prefix_keys,
    prefix_values,
    block_use,
    private_keys,
    private_values,
    private_lengths,
    draft_keys,
    draft_values,
    parents,
    out_weight,
):
    requests, tree_size, heads_dev, head_dim = queries.shape
    kv_dev = prefix_keys.shape[2]
    group_size = heads_dev // kv_dev
    private_dev = private_keys.shape[1]
    scaling = 1.0 / math.sqrt(head_dim)
    shard_index = lax.axis_index("seq")
    seq_size = lax.axis_size("seq")
    reach = ancestry(parents)
    row_count = requests * tree_size
    chunk = row_count // seq_size
    pieces = tree_size // chunk
    own_lengths = jnp.clip(private_lengths - shard_index * private_dev, 0, private_dev)
    acc = context_part(
        queries, prefix_keys, prefix_values, block_use, own_lengths, private_keys, private_values, pieces
    )
    width = chunk * group_size
    sent = acc.reshape(seq_size, kv_dev, head_dim + 16, width)
    got = lax.all_to_all(sent, "seq", 0, 0, tiled=True)
    part_top = got[:, :, head_dim].astype(jnp.float32)
    part_totals = got[:, :, head_dim + 1].astype(jnp.float32) + got[:, :, head_dim + 2].astype(
        jnp.float32
    )
    top_all = jnp.max(part_top, axis=0)
    factor = jnp.exp(part_top - top_all[None])
    summed_totals = jnp.sum(part_totals * factor, axis=0)
    summed_weighted = jnp.sum(
        got[:, :, :head_dim].astype(jnp.float32) * factor[:, :, None, :], axis=0
    )
    top_all = jnp.transpose(top_all.reshape(kv_dev, chunk, group_size), (1, 0, 2)).reshape(chunk, heads_dev)
    summed_totals = jnp.transpose(
        summed_totals.reshape(kv_dev, chunk, group_size), (1, 0, 2)
    ).reshape(chunk, heads_dev)
    summed_weighted = jnp.transpose(
        summed_weighted.reshape(kv_dev, head_dim, chunk, group_size), (2, 0, 3, 1)
    ).reshape(chunk, heads_dev, head_dim)
    row0 = shard_index * chunk
    request = row0 // tree_size
    token0 = row0 % tree_size
    my_queries = lax.dynamic_slice_in_dim(
        queries.reshape(row_count, heads_dev, head_dim), row0, chunk, 0
    )[None]
    my_keys = lax.dynamic_index_in_dim(draft_keys, request, 0, keepdims=True)
    my_values = lax.dynamic_index_in_dim(draft_values, request, 0, keepdims=True)
    my_reach = lax.dynamic_slice_in_dim(
        lax.dynamic_index_in_dim(reach, request, 0, keepdims=True), token0, chunk, 1
    )
    draft = draft_part(my_queries, my_keys, my_values, my_reach, scaling)
    draft = (draft[0][0], draft[1][0], draft[2][0])
    final_top, final_totals, final_weighted = combine(
        (top_all, summed_totals, summed_weighted), draft
    )
    attention = (final_weighted / final_totals[..., None]).astype(jnp.bfloat16)
    attention = lax.all_gather(attention, "seq", axis=0, tiled=True)
    attention = attention.reshape(requests, tree_size, heads_dev, head_dim)
    heads_size = lax.axis_size("heads")
    partial = jnp.einsum("rthd,hde->rte", attention, out_weight, preferred_element_type=jnp.float32)
    partial = partial.reshape(heads_size, requests // heads_size, tree_size, partial.shape[-1])
    return jnp.sum(lax.all_to_all(partial, "heads", 0, 0, tiled=True), axis=0)


def solution(mesh):
    return jax.shard_map(
        local,
        mesh=mesh,
        in_specs=(
            P(None, None, "heads", None),
            P("seq", None, "heads", None),
            P("seq", None, "heads", None),
            P(None, "seq"),
            P(None, "seq", "heads", None),
            P(None, "seq", "heads", None),
            P(),
            P(None, None, "heads", None),
            P(None, None, "heads", None),
            P(),
            P("heads", None, "seq"),
        ),
        out_specs=P("heads", None, "seq"),
        check_vma=False,
    )
```

```python
import math

import jax
import jax.numpy as jnp
from jax import lax
from jax.experimental import pallas as pl
from jax.experimental.pallas import tpu as pltpu
from jax.sharding import Mesh, PartitionSpec as P
import numpy as np


def ancestry(parents):
    tree_size = parents.shape[-1]
    places = jnp.arange(tree_size, dtype=jnp.int32)
    onestep = (parents[..., None] == places).astype(jnp.float32)
    ident = (places[:, None] == places[None, :]).astype(jnp.float32)
    reach = jnp.maximum(onestep, ident)
    for level in range(max(1, (tree_size - 1).bit_length())):
        reach = jnp.minimum(
            jnp.einsum("rij,rjk->rik", reach, reach, precision=lax.Precision.HIGHEST), 1.0
        )
    return reach


def combine(first, second):
    top = jnp.maximum(first[0], second[0])
    first_factor = jnp.exp(first[0] - top)
    second_factor = jnp.exp(second[0] - top)
    totals = first[1] * first_factor + second[1] * second_factor
    weighted = first[2] * first_factor[..., None] + second[2] * second_factor[..., None]
    return (top, totals, weighted)


def draft_part(row_queries, tree_keys, tree_values, row_reach, scaling):
    requests, rows, heads_dev, head_dim = row_queries.shape
    kv_dev = tree_keys.shape[2]
    group_size = heads_dev // kv_dev
    grouped = row_queries.reshape(requests, rows, kv_dev, group_size, head_dim)
    scores = (
        jnp.einsum("rtkgd,rskd->rtkgs", grouped, tree_keys, preferred_element_type=jnp.float32)
        * scaling
    )
    live = (row_reach > 0.5)[:, :, None, None, :]
    scores = jnp.where(live, scores, -1e30)
    highest = jnp.max(scores, axis=-1)
    weights = jnp.where(live, jnp.exp(scores - highest[..., None]), 0.0)
    totals = jnp.sum(weights, axis=-1)
    weighted = jnp.einsum(
        "rtkgs,rskd->rtkgd",
        weights.astype(jnp.bfloat16),
        tree_values,
        preferred_element_type=jnp.float32,
    )
    return (
        highest.reshape(requests, rows, heads_dev),
        totals.reshape(requests, rows, heads_dev),
        weighted.reshape(requests, rows, heads_dev, head_dim),
    )


def context_kernel(use_ref, len_ref, q_ref, kp_ref, vp_ref, ko_ref, vo_ref, acc_ref):
    r = pl.program_id(1)
    scaling = 1.0 / math.sqrt(q_ref.shape[-1])
    q = q_ref[0].reshape(-1, q_ref.shape[-1])
    kp = kp_ref[0]
    ko = ko_ref[0, 0]
    dims = (((1,), (1,)), ((), ()))
    s_pre = lax.dot_general(kp, q, dims, preferred_element_type=jnp.float32) * scaling
    s_own = lax.dot_general(ko, q, dims, preferred_element_type=jnp.float32) * scaling
    n_pre = kp.shape[0]
    n_own = ko.shape[0]
    block_len = n_pre // use_ref.shape[1]
    block_id = lax.broadcasted_iota(jnp.int32, (n_pre, 1), 0) // block_len
    pre_live = jnp.zeros((n_pre, 1), jnp.bool_)
    for b in range(use_ref.shape[1]):
        pre_live = jnp.logical_or(pre_live, jnp.logical_and(block_id == b, use_ref[r, b] == 1))
    own_live = lax.broadcasted_iota(jnp.int32, (n_own, 1), 0) < len_ref[r]
    s_pre = jnp.where(pre_live, s_pre, -1e30)
    s_own = jnp.where(own_live, s_own, -1e30)
    top = jnp.maximum(
        jnp.max(s_pre, axis=0, keepdims=True), jnp.max(s_own, axis=0, keepdims=True)
    )
    top = jnp.maximum(top, -1e29).astype(jnp.bfloat16).astype(jnp.float32)
    w_pre = jnp.exp(s_pre - top)
    w_own = jnp.exp(s_own - top)
    totals = jnp.sum(w_pre, axis=0, keepdims=True) + jnp.sum(w_own, axis=0, keepdims=True)
    acc = jnp.dot(vp_ref[0], w_pre.astype(jnp.bfloat16), preferred_element_type=jnp.float32)
    acc = acc + jnp.dot(
        vo_ref[0, 0], w_own.astype(jnp.bfloat16), preferred_element_type=jnp.float32
    )
    head_dim = acc.shape[0]
    pieces = acc_ref.shape[1]
    width = acc_ref.shape[-1]
    extra = acc_ref.shape[3] - head_dim
    high = totals.astype(jnp.bfloat16).astype(jnp.float32)
    low = totals - high
    row_id = lax.broadcasted_iota(jnp.int32, (extra, totals.shape[1]), 0)
    stats = jnp.where(row_id == 0, top, jnp.where(row_id == 1, high, jnp.where(row_id == 2, low, 0.0)))
    for c in range(pieces):
        acc_ref[0, c, 0, 0:head_dim, :] = acc[:, c * width : (c + 1) * width].astype(acc_ref.dtype)
        acc_ref[0, c, 0, head_dim:, :] = stats[:, c * width : (c + 1) * width].astype(acc_ref.dtype)


def context_part(queries, prefix_keys, prefix_values, use_rows, own_lengths, own_keys, own_values, pieces):
    requests, tree_size, heads_dev, head_dim = queries.shape
    block_count, block_len, kv_dev, _ = prefix_keys.shape
    group_size = heads_dev // kv_dev
    private_dev = own_keys.shape[1]
    n_pre = block_count * block_len
    rows = tree_size * group_size
    width = rows // pieces
    kp = jnp.transpose(prefix_keys.reshape(n_pre, kv_dev, head_dim), (1, 0, 2))
    vp = jnp.transpose(prefix_values.reshape(n_pre, kv_dev, head_dim), (1, 2, 0))
    ko = jnp.transpose(own_keys, (0, 2, 1, 3))
    vo = jnp.transpose(own_values, (0, 2, 3, 1))
    grid_spec = pltpu.PrefetchScalarGridSpec(
        num_scalar_prefetch=2,
        grid=(kv_dev, requests),
        in_specs=[
            pl.BlockSpec((1, tree_size, group_size, head_dim), lambda k, r, u, n: (r, 0, k, 0)),
            pl.BlockSpec((1, n_pre, head_dim), lambda k, r, u, n: (k, 0, 0)),
            pl.BlockSpec((1, head_dim, n_pre), lambda k, r, u, n: (k, 0, 0)),
            pl.BlockSpec((1, 1, private_dev, head_dim), lambda k, r, u, n: (r, k, 0, 0)),
            pl.BlockSpec((1, 1, head_dim, private_dev), lambda k, r, u, n: (r, k, 0, 0)),
        ],
        out_specs=pl.BlockSpec(
            (1, pieces, 1, head_dim + 16, width), lambda k, r, u, n: (r, 0, k, 0, 0)
        ),
    )
    return pl.pallas_call(
        context_kernel,
        grid_spec=grid_spec,
        out_shape=jax.ShapeDtypeStruct(
            (requests, pieces, kv_dev, head_dim + 16, width), jnp.bfloat16
        ),
    )(use_rows, own_lengths, queries, kp, vp, ko, vo)


SEQ = ("sx", "sy", "sc")


def unpack(parts, head_dim, axis):
    top = parts[:, :, :, head_dim] if axis == 1 else parts[:, :, head_dim]
    high = parts[:, :, :, head_dim + 1] if axis == 1 else parts[:, :, head_dim + 1]
    low = parts[:, :, :, head_dim + 2] if axis == 1 else parts[:, :, head_dim + 2]
    weighted = parts[:, :, :, :head_dim] if axis == 1 else parts[:, :, :head_dim]
    totals = high.astype(jnp.float32) + low.astype(jnp.float32)
    return top.astype(jnp.float32), totals, weighted.astype(jnp.float32)


def local(
    queries,
    prefix_keys,
    prefix_values,
    block_use,
    private_keys,
    private_values,
    private_lengths,
    draft_keys,
    draft_values,
    parents,
    out_weight,
):
    requests, tree_size, heads_dev, head_dim = queries.shape
    kv_dev = prefix_keys.shape[2]
    group_size = heads_dev // kv_dev
    private_dev = private_keys.shape[1]
    scaling = 1.0 / math.sqrt(head_dim)
    shard_index = lax.axis_index(SEQ)
    seq_size = lax.axis_size(SEQ)
    reach = ancestry(parents)
    row_count = requests * tree_size
    chunk = row_count // seq_size
    pieces = tree_size // chunk
    own_lengths = jnp.clip(private_lengths - shard_index * private_dev, 0, private_dev)
    acc = context_part(
        queries, prefix_keys, prefix_values, block_use, own_lengths, private_keys, private_values, pieces
    )
    width = chunk * group_size
    pair = lax.axis_size("sc")
    core = lax.axis_index("sc")
    parts = acc.reshape(seq_size // pair, pair, kv_dev, head_dim + 16, width)
    parts = lax.all_to_all(parts, "sc", 1, 1, tiled=True)
    part_top, part_totals, part_weighted = unpack(parts, head_dim, 1)
    pair_top = jnp.max(part_top, axis=1)
    factor = jnp.exp(part_top - pair_top[:, None])
    pair_totals = jnp.sum(part_totals * factor, axis=1)
    pair_weighted = jnp.sum(part_weighted * factor[:, :, :, None, :], axis=1)
    high = pair_totals.astype(jnp.bfloat16)
    low = (pair_totals - high.astype(jnp.float32)).astype(jnp.bfloat16)
    zeros = jnp.zeros(pair_top.shape[:2] + (13,) + pair_top.shape[2:], jnp.bfloat16)
    sent = jnp.concatenate(
        [
            pair_weighted.astype(jnp.bfloat16),
            pair_top.astype(jnp.bfloat16)[:, :, None],
            high[:, :, None],
            low[:, :, None],
            zeros,
        ],
        axis=2,
    )
    got = lax.all_to_all(sent, ("sx", "sy"), 0, 0, tiled=True)
    part_top, part_totals, part_weighted = unpack(got, head_dim, 0)
    top_all = jnp.max(part_top, axis=0)
    factor = jnp.exp(part_top - top_all[None])
    summed_totals = jnp.sum(part_totals * factor, axis=0)
    summed_weighted = jnp.sum(part_weighted * factor[:, :, None, :], axis=0)
    top_all = jnp.transpose(top_all.reshape(kv_dev, chunk, group_size), (1, 0, 2)).reshape(chunk, heads_dev)
    summed_totals = jnp.transpose(
        summed_totals.reshape(kv_dev, chunk, group_size), (1, 0, 2)
    ).reshape(chunk, heads_dev)
    summed_weighted = jnp.transpose(
        summed_weighted.reshape(kv_dev, head_dim, chunk, group_size), (2, 0, 3, 1)
    ).reshape(chunk, heads_dev, head_dim)
    row0 = shard_index * chunk
    request = row0 // tree_size
    token0 = row0 % tree_size
    my_queries = lax.dynamic_slice_in_dim(
        queries.reshape(row_count, heads_dev, head_dim), row0, chunk, 0
    )[None]
    my_keys = lax.dynamic_index_in_dim(draft_keys, request, 0, keepdims=True)
    my_values = lax.dynamic_index_in_dim(draft_values, request, 0, keepdims=True)
    my_reach = lax.dynamic_slice_in_dim(
        lax.dynamic_index_in_dim(reach, request, 0, keepdims=True), token0, chunk, 1
    )
    draft = draft_part(my_queries, my_keys, my_values, my_reach, scaling)
    draft = (draft[0][0], draft[1][0], draft[2][0])
    final_top, final_totals, final_weighted = combine(
        (top_all, summed_totals, summed_weighted), draft
    )
    attention = (final_weighted / final_totals[..., None]).astype(jnp.bfloat16)
    attention = lax.all_gather(attention, ("sx", "sy"), axis=0, tiled=False)
    other = lax.ppermute(attention, "sc", [(i, (i + 1) % pair) for i in range(pair)])
    first = jnp.where(core == 0, attention, other)
    second = jnp.where(core == 0, other, attention)
    attention = jnp.stack([first, second], 1)
    attention = attention.reshape(requests, tree_size, heads_dev, head_dim)
    heads_size = lax.axis_size("heads")
    partial = jnp.einsum("rthd,hde->rte", attention, out_weight, preferred_element_type=jnp.float32)
    partial = partial.reshape(heads_size, requests // heads_size, tree_size, partial.shape[-1])
    return jnp.sum(lax.all_to_all(partial, "heads", 0, 0, tiled=True), axis=0)


def solution(mesh):
    heads_size = mesh.shape["heads"]
    sizes = [mesh.shape["seq"] // 8, 4, 2]
    fine = Mesh(np.asarray(mesh.devices).reshape([heads_size] + sizes), ("heads",) + SEQ)
    return jax.shard_map(
        local,
        mesh=fine,
        in_specs=(
            P(None, None, "heads", None),
            P(SEQ, None, "heads", None),
            P(SEQ, None, "heads", None),
            P(None, SEQ),
            P(None, SEQ, "heads", None),
            P(None, SEQ, "heads", None),
            P(),
            P(None, None, "heads", None),
            P(None, None, "heads", None),
            P(),
            P("heads", None, SEQ),
        ),
        out_specs=P("heads", None, SEQ),
        check_vma=False,
    )
```

```python
import math

import jax
import jax.numpy as jnp
from jax import lax
from jax.experimental import pallas as pl
from jax.experimental.pallas import tpu as pltpu
from jax.sharding import Mesh, PartitionSpec as P
import numpy as np


def ancestry(parents):
    tree_size = parents.shape[-1]
    places = jnp.arange(tree_size, dtype=jnp.int32)
    onestep = (parents[..., None] == places).astype(jnp.float32)
    ident = (places[:, None] == places[None, :]).astype(jnp.float32)
    reach = jnp.maximum(onestep, ident)
    for level in range(max(1, (tree_size - 1).bit_length())):
        reach = jnp.minimum(
            jnp.einsum("rij,rjk->rik", reach, reach, precision=lax.Precision.HIGHEST), 1.0
        )
    return reach


def combine(first, second):
    top = jnp.maximum(first[0], second[0])
    first_factor = jnp.exp(first[0] - top)
    second_factor = jnp.exp(second[0] - top)
    totals = first[1] * first_factor + second[1] * second_factor
    weighted = first[2] * first_factor[..., None] + second[2] * second_factor[..., None]
    return (top, totals, weighted)


def draft_part(row_queries, tree_keys, tree_values, row_reach, scaling):
    requests, rows, heads_dev, head_dim = row_queries.shape
    kv_dev = tree_keys.shape[2]
    group_size = heads_dev // kv_dev
    grouped = row_queries.reshape(requests, rows, kv_dev, group_size, head_dim)
    scores = (
        jnp.einsum("rtkgd,rskd->rtkgs", grouped, tree_keys, preferred_element_type=jnp.float32)
        * scaling
    )
    live = (row_reach > 0.5)[:, :, None, None, :]
    scores = jnp.where(live, scores, -1e30)
    highest = jnp.max(scores, axis=-1)
    weights = jnp.where(live, jnp.exp(scores - highest[..., None]), 0.0)
    totals = jnp.sum(weights, axis=-1)
    weighted = jnp.einsum(
        "rtkgs,rskd->rtkgd",
        weights.astype(jnp.bfloat16),
        tree_values,
        preferred_element_type=jnp.float32,
    )
    return (
        highest.reshape(requests, rows, heads_dev),
        totals.reshape(requests, rows, heads_dev),
        weighted.reshape(requests, rows, heads_dev, head_dim),
    )


def context_kernel(use_ref, len_ref, q_ref, kp_ref, vp_ref, ko_ref, vo_ref, acc_ref):
    r = pl.program_id(1)
    scaling = 1.0 / math.sqrt(q_ref.shape[-1])
    q = q_ref[0].reshape(-1, q_ref.shape[-1])
    kp = kp_ref[0]
    ko = ko_ref[0, 0]
    dims = (((1,), (1,)), ((), ()))
    s_pre = lax.dot_general(kp, q, dims, preferred_element_type=jnp.float32) * scaling
    s_own = lax.dot_general(ko, q, dims, preferred_element_type=jnp.float32) * scaling
    n_pre = kp.shape[0]
    n_own = ko.shape[0]
    block_len = n_pre // use_ref.shape[1]
    block_id = lax.broadcasted_iota(jnp.int32, (n_pre, 1), 0) // block_len
    pre_live = jnp.zeros((n_pre, 1), jnp.bool_)
    for b in range(use_ref.shape[1]):
        pre_live = jnp.logical_or(pre_live, jnp.logical_and(block_id == b, use_ref[r, b] == 1))
    own_live = lax.broadcasted_iota(jnp.int32, (n_own, 1), 0) < len_ref[r]
    s_pre = jnp.where(pre_live, s_pre, -1e30)
    s_own = jnp.where(own_live, s_own, -1e30)
    top = jnp.maximum(
        jnp.max(s_pre, axis=0, keepdims=True), jnp.max(s_own, axis=0, keepdims=True)
    )
    top = jnp.maximum(top, -1e29).astype(jnp.bfloat16).astype(jnp.float32)
    w_pre = jnp.exp(s_pre - top)
    w_own = jnp.exp(s_own - top)
    totals = jnp.sum(w_pre, axis=0, keepdims=True) + jnp.sum(w_own, axis=0, keepdims=True)
    acc = jnp.dot(vp_ref[0], w_pre.astype(jnp.bfloat16), preferred_element_type=jnp.float32)
    acc = acc + jnp.dot(
        vo_ref[0, 0], w_own.astype(jnp.bfloat16), preferred_element_type=jnp.float32
    )
    head_dim = acc.shape[0]
    pieces = acc_ref.shape[1]
    width = acc_ref.shape[-1]
    extra = acc_ref.shape[3] - head_dim
    high = totals.astype(jnp.bfloat16).astype(jnp.float32)
    low = totals - high
    row_id = lax.broadcasted_iota(jnp.int32, (extra, totals.shape[1]), 0)
    stats = jnp.where(row_id == 0, top, jnp.where(row_id == 1, high, jnp.where(row_id == 2, low, 0.0)))
    for c in range(pieces):
        acc_ref[0, c, 0, 0:head_dim, :] = acc[:, c * width : (c + 1) * width].astype(acc_ref.dtype)
        acc_ref[0, c, 0, head_dim:, :] = stats[:, c * width : (c + 1) * width].astype(acc_ref.dtype)


def context_part(queries, prefix_keys, prefix_values, use_rows, own_lengths, own_keys, own_values, pieces):
    requests, tree_size, heads_dev, head_dim = queries.shape
    block_count, block_len, kv_dev, _ = prefix_keys.shape
    group_size = heads_dev // kv_dev
    private_dev = own_keys.shape[1]
    n_pre = block_count * block_len
    rows = tree_size * group_size
    width = rows // pieces
    kp = jnp.transpose(prefix_keys.reshape(n_pre, kv_dev, head_dim), (1, 0, 2))
    vp = jnp.transpose(prefix_values.reshape(n_pre, kv_dev, head_dim), (1, 2, 0))
    ko = jnp.transpose(own_keys, (0, 2, 1, 3))
    vo = jnp.transpose(own_values, (0, 2, 3, 1))
    grid_spec = pltpu.PrefetchScalarGridSpec(
        num_scalar_prefetch=2,
        grid=(kv_dev, requests),
        in_specs=[
            pl.BlockSpec((1, tree_size, group_size, head_dim), lambda k, r, u, n: (r, 0, k, 0)),
            pl.BlockSpec((1, n_pre, head_dim), lambda k, r, u, n: (k, 0, 0)),
            pl.BlockSpec((1, head_dim, n_pre), lambda k, r, u, n: (k, 0, 0)),
            pl.BlockSpec((1, 1, private_dev, head_dim), lambda k, r, u, n: (r, k, 0, 0)),
            pl.BlockSpec((1, 1, head_dim, private_dev), lambda k, r, u, n: (r, k, 0, 0)),
        ],
        out_specs=pl.BlockSpec(
            (1, pieces, 1, head_dim + 16, width), lambda k, r, u, n: (r, 0, k, 0, 0)
        ),
    )
    return pl.pallas_call(
        context_kernel,
        grid_spec=grid_spec,
        out_shape=jax.ShapeDtypeStruct(
            (requests, pieces, kv_dev, head_dim + 16, width), jnp.bfloat16
        ),
    )(use_rows, own_lengths, queries, kp, vp, ko, vo)


SEQ = ("sx", "sy", "sc")


def unpack(parts, head_dim, axis):
    top = parts[:, :, :, head_dim] if axis == 1 else parts[:, :, head_dim]
    high = parts[:, :, :, head_dim + 1] if axis == 1 else parts[:, :, head_dim + 1]
    low = parts[:, :, :, head_dim + 2] if axis == 1 else parts[:, :, head_dim + 2]
    weighted = parts[:, :, :, :head_dim] if axis == 1 else parts[:, :, :head_dim]
    totals = high.astype(jnp.float32) + low.astype(jnp.float32)
    return top.astype(jnp.float32), totals, weighted.astype(jnp.float32)


def local(
    queries,
    prefix_keys,
    prefix_values,
    block_use,
    private_keys,
    private_values,
    private_lengths,
    draft_keys,
    draft_values,
    parents,
    out_weight,
):
    requests, tree_size, heads_dev, head_dim = queries.shape
    kv_dev = prefix_keys.shape[2]
    group_size = heads_dev // kv_dev
    private_dev = private_keys.shape[1]
    scaling = 1.0 / math.sqrt(head_dim)
    shard_index = lax.axis_index(SEQ)
    seq_size = lax.axis_size(SEQ)
    reach = ancestry(parents)
    row_count = requests * tree_size
    chunk = row_count // seq_size
    pieces = tree_size // chunk
    own_lengths = jnp.clip(private_lengths - shard_index * private_dev, 0, private_dev)
    acc = context_part(
        queries, prefix_keys, prefix_values, block_use, own_lengths, private_keys, private_values, pieces
    )
    width = chunk * group_size
    pair = lax.axis_size("sc")
    core = lax.axis_index("sc")
    parts = acc.reshape(seq_size // pair, pair, kv_dev, head_dim + 16, width)
    parts = lax.all_to_all(parts, "sc", 1, 1, tiled=True)
    part_top, part_totals, part_weighted = unpack(parts, head_dim, 1)
    pair_top = jnp.max(part_top, axis=1)
    factor = jnp.exp(part_top - pair_top[:, None])
    pair_totals = jnp.sum(part_totals * factor, axis=1)
    pair_weighted = jnp.sum(part_weighted * factor[:, :, :, None, :], axis=1)
    high = pair_totals.astype(jnp.bfloat16)
    low = (pair_totals - high.astype(jnp.float32)).astype(jnp.bfloat16)
    zeros = jnp.zeros(pair_top.shape[:2] + (13,) + pair_top.shape[2:], jnp.bfloat16)
    sent = jnp.concatenate(
        [
            pair_weighted.astype(jnp.bfloat16),
            pair_top.astype(jnp.bfloat16)[:, :, None],
            high[:, :, None],
            low[:, :, None],
            zeros,
        ],
        axis=2,
    )
    got = lax.all_to_all(sent, ("sx", "sy"), 0, 0, tiled=True)
    part_top, part_totals, part_weighted = unpack(got, head_dim, 0)
    top_all = jnp.max(part_top, axis=0)
    factor = jnp.exp(part_top - top_all[None])
    summed_totals = jnp.sum(part_totals * factor, axis=0)
    summed_weighted = jnp.sum(part_weighted * factor[:, :, None, :], axis=0)
    top_all = jnp.transpose(top_all.reshape(kv_dev, chunk, group_size), (1, 0, 2)).reshape(chunk, heads_dev)
    summed_totals = jnp.transpose(
        summed_totals.reshape(kv_dev, chunk, group_size), (1, 0, 2)
    ).reshape(chunk, heads_dev)
    summed_weighted = jnp.transpose(
        summed_weighted.reshape(kv_dev, head_dim, chunk, group_size), (2, 0, 3, 1)
    ).reshape(chunk, heads_dev, head_dim)
    row0 = shard_index * chunk
    request = row0 // tree_size
    token0 = row0 % tree_size
    my_queries = lax.dynamic_slice_in_dim(
        queries.reshape(row_count, heads_dev, head_dim), row0, chunk, 0
    )[None]
    my_keys = lax.dynamic_index_in_dim(draft_keys, request, 0, keepdims=True)
    my_values = lax.dynamic_index_in_dim(draft_values, request, 0, keepdims=True)
    my_reach = lax.dynamic_slice_in_dim(
        lax.dynamic_index_in_dim(reach, request, 0, keepdims=True), token0, chunk, 1
    )
    draft = draft_part(my_queries, my_keys, my_values, my_reach, scaling)
    draft = (draft[0][0], draft[1][0], draft[2][0])
    final_top, final_totals, final_weighted = combine(
        (top_all, summed_totals, summed_weighted), draft
    )
    attention = (final_weighted / final_totals[..., None]).astype(jnp.bfloat16)
    peers = seq_size // pair
    attention = jnp.broadcast_to(attention[None], (peers,) + attention.shape)
    attention = lax.all_to_all(attention, ("sx", "sy"), 0, 0, tiled=True)
    other = lax.ppermute(attention, "sc", [(i, (i + 1) % pair) for i in range(pair)])
    first = jnp.where(core == 0, attention, other)
    second = jnp.where(core == 0, other, attention)
    attention = jnp.stack([first, second], 1)
    attention = attention.reshape(requests, tree_size, heads_dev, head_dim)
    heads_size = lax.axis_size("heads")
    partial = jnp.einsum("rthd,hde->rte", attention, out_weight, preferred_element_type=jnp.float32)
    partial = partial.reshape(heads_size, requests // heads_size, tree_size, partial.shape[-1])
    return jnp.sum(lax.all_to_all(partial, "heads", 0, 0, tiled=True), axis=0)


def solution(mesh):
    heads_size = mesh.shape["heads"]
    sizes = [mesh.shape["seq"] // 8, 4, 2]
    fine = Mesh(np.asarray(mesh.devices).reshape([heads_size] + sizes), ("heads",) + SEQ)
    return jax.shard_map(
        local,
        mesh=fine,
        in_specs=(
            P(None, None, "heads", None),
            P(SEQ, None, "heads", None),
            P(SEQ, None, "heads", None),
            P(None, SEQ),
            P(None, SEQ, "heads", None),
            P(None, SEQ, "heads", None),
            P(),
            P(None, None, "heads", None),
            P(None, None, "heads", None),
            P(),
            P("heads", None, SEQ),
        ),
        out_specs=P("heads", None, SEQ),
        check_vma=False,
    )
```

```python
import math

import jax
import jax.numpy as jnp
from jax import lax
from jax.experimental import pallas as pl
from jax.experimental.pallas import tpu as pltpu
from jax.sharding import Mesh, PartitionSpec as P
import numpy as np


def ancestry(parents):
    tree_size = parents.shape[-1]
    places = jnp.arange(tree_size, dtype=jnp.int32)
    onestep = (parents[..., None] == places).astype(jnp.float32)
    ident = (places[:, None] == places[None, :]).astype(jnp.float32)
    reach = jnp.maximum(onestep, ident)
    for level in range(max(1, (tree_size - 1).bit_length())):
        reach = jnp.minimum(
            jnp.einsum("rij,rjk->rik", reach, reach, precision=lax.Precision.HIGHEST), 1.0
        )
    return reach


def combine(first, second):
    top = jnp.maximum(first[0], second[0])
    first_factor = jnp.exp(first[0] - top)
    second_factor = jnp.exp(second[0] - top)
    totals = first[1] * first_factor + second[1] * second_factor
    weighted = first[2] * first_factor[..., None] + second[2] * second_factor[..., None]
    return (top, totals, weighted)


def draft_part(row_queries, tree_keys, tree_values, row_reach, scaling):
    requests, rows, heads_dev, head_dim = row_queries.shape
    kv_dev = tree_keys.shape[2]
    group_size = heads_dev // kv_dev
    grouped = row_queries.reshape(requests, rows, kv_dev, group_size, head_dim)
    scores = (
        jnp.einsum("rtkgd,rskd->rtkgs", grouped, tree_keys, preferred_element_type=jnp.float32)
        * scaling
    )
    live = (row_reach > 0.5)[:, :, None, None, :]
    scores = jnp.where(live, scores, -1e30)
    highest = jnp.max(scores, axis=-1)
    weights = jnp.where(live, jnp.exp(scores - highest[..., None]), 0.0)
    totals = jnp.sum(weights, axis=-1)
    weighted = jnp.einsum(
        "rtkgs,rskd->rtkgd",
        weights.astype(jnp.bfloat16),
        tree_values,
        preferred_element_type=jnp.float32,
    )
    return (
        highest.reshape(requests, rows, heads_dev),
        totals.reshape(requests, rows, heads_dev),
        weighted.reshape(requests, rows, heads_dev, head_dim),
    )


def context_kernel(use_ref, len_ref, q_ref, kp_ref, vp_ref, ko_ref, vo_ref, acc_ref):
    r = pl.program_id(1)
    scaling = 1.0 / math.sqrt(q_ref.shape[-1])
    q = q_ref[0].reshape(-1, q_ref.shape[-1])
    kp = kp_ref[0]
    ko = ko_ref[0, 0]
    dims = (((1,), (1,)), ((), ()))
    s_pre = lax.dot_general(kp, q, dims, preferred_element_type=jnp.float32) * scaling
    s_own = lax.dot_general(ko, q, dims, preferred_element_type=jnp.float32) * scaling
    n_pre = kp.shape[0]
    n_own = ko.shape[0]
    block_len = n_pre // use_ref.shape[1]
    block_id = lax.broadcasted_iota(jnp.int32, (n_pre, 1), 0) // block_len
    pre_live = jnp.zeros((n_pre, 1), jnp.bool_)
    for b in range(use_ref.shape[1]):
        pre_live = jnp.logical_or(pre_live, jnp.logical_and(block_id == b, use_ref[r, b] == 1))
    own_live = lax.broadcasted_iota(jnp.int32, (n_own, 1), 0) < len_ref[r]
    s_pre = jnp.where(pre_live, s_pre, -1e30)
    s_own = jnp.where(own_live, s_own, -1e30)
    top = jnp.maximum(
        jnp.max(s_pre, axis=0, keepdims=True), jnp.max(s_own, axis=0, keepdims=True)
    )
    top = jnp.maximum(top, -1e29).astype(jnp.bfloat16).astype(jnp.float32)
    w_pre = jnp.exp(s_pre - top)
    w_own = jnp.exp(s_own - top)
    totals = jnp.sum(w_pre, axis=0, keepdims=True) + jnp.sum(w_own, axis=0, keepdims=True)
    acc = jnp.dot(vp_ref[0], w_pre.astype(jnp.bfloat16), preferred_element_type=jnp.float32)
    acc = acc + jnp.dot(
        vo_ref[0, 0], w_own.astype(jnp.bfloat16), preferred_element_type=jnp.float32
    )
    head_dim = acc.shape[0]
    pieces = acc_ref.shape[0] * acc_ref.shape[2]
    width = acc_ref.shape[-1]
    extra = acc_ref.shape[-2] - head_dim
    high = totals.astype(jnp.bfloat16).astype(jnp.float32)
    low = totals - high
    row_id = lax.broadcasted_iota(jnp.int32, (extra, totals.shape[1]), 0)
    stats = jnp.where(row_id == 0, top, jnp.where(row_id == 1, high, jnp.where(row_id == 2, low, 0.0)))
    pair = acc_ref.shape[0]
    for c in range(pieces):
        spot = (c % pair, 0, c // pair, 0)
        acc_ref[spot + (slice(0, head_dim),)] = acc[:, c * width : (c + 1) * width].astype(
            acc_ref.dtype
        )
        acc_ref[spot + (slice(head_dim, None),)] = stats[:, c * width : (c + 1) * width].astype(
            acc_ref.dtype
        )


def context_part(queries, prefix_keys, prefix_values, use_rows, own_lengths, own_keys, own_values, pieces, pair):
    requests, tree_size, heads_dev, head_dim = queries.shape
    block_count, block_len, kv_dev, _ = prefix_keys.shape
    group_size = heads_dev // kv_dev
    private_dev = own_keys.shape[1]
    n_pre = block_count * block_len
    rows = tree_size * group_size
    width = rows // pieces
    kp = jnp.transpose(prefix_keys.reshape(n_pre, kv_dev, head_dim), (1, 0, 2))
    vp = jnp.transpose(prefix_values.reshape(n_pre, kv_dev, head_dim), (1, 2, 0))
    ko = jnp.transpose(own_keys, (0, 2, 1, 3))
    vo = jnp.transpose(own_values, (0, 2, 3, 1))
    grid_spec = pltpu.PrefetchScalarGridSpec(
        num_scalar_prefetch=2,
        grid=(kv_dev, requests),
        in_specs=[
            pl.BlockSpec((1, tree_size, group_size, head_dim), lambda k, r, u, n: (r, 0, k, 0)),
            pl.BlockSpec((1, n_pre, head_dim), lambda k, r, u, n: (k, 0, 0)),
            pl.BlockSpec((1, head_dim, n_pre), lambda k, r, u, n: (k, 0, 0)),
            pl.BlockSpec((1, 1, private_dev, head_dim), lambda k, r, u, n: (r, k, 0, 0)),
            pl.BlockSpec((1, 1, head_dim, private_dev), lambda k, r, u, n: (r, k, 0, 0)),
        ],
        out_specs=pl.BlockSpec(
            (pair, 1, pieces // pair, 1, head_dim + 16, width),
            lambda k, r, u, n: (0, r, 0, k, 0, 0),
        ),
    )
    return pl.pallas_call(
        context_kernel,
        grid_spec=grid_spec,
        out_shape=jax.ShapeDtypeStruct(
            (pair, requests, pieces // pair, kv_dev, head_dim + 16, width), jnp.bfloat16
        ),
    )(use_rows, own_lengths, queries, kp, vp, ko, vo)


SEQ = ("sx", "sy", "sc")


def unpack(parts, head_dim, axis):
    top = parts[:, :, :, head_dim] if axis == 1 else parts[:, :, head_dim]
    high = parts[:, :, :, head_dim + 1] if axis == 1 else parts[:, :, head_dim + 1]
    low = parts[:, :, :, head_dim + 2] if axis == 1 else parts[:, :, head_dim + 2]
    weighted = parts[:, :, :, :head_dim] if axis == 1 else parts[:, :, :head_dim]
    totals = high.astype(jnp.float32) + low.astype(jnp.float32)
    return top.astype(jnp.float32), totals, weighted.astype(jnp.float32)


def local(
    queries,
    prefix_keys,
    prefix_values,
    block_use,
    private_keys,
    private_values,
    private_lengths,
    draft_keys,
    draft_values,
    parents,
    out_weight,
):
    requests, tree_size, heads_dev, head_dim = queries.shape
    kv_dev = prefix_keys.shape[2]
    group_size = heads_dev // kv_dev
    private_dev = private_keys.shape[1]
    scaling = 1.0 / math.sqrt(head_dim)
    shard_index = lax.axis_index(SEQ)
    seq_size = lax.axis_size(SEQ)
    reach = ancestry(parents)
    row_count = requests * tree_size
    chunk = row_count // seq_size
    pieces = tree_size // chunk
    pair = lax.axis_size("sc")
    core = lax.axis_index("sc")
    own_lengths = jnp.clip(private_lengths - shard_index * private_dev, 0, private_dev)
    acc = context_part(
        queries, prefix_keys, prefix_values, block_use, own_lengths, private_keys, private_values, pieces, pair
    )
    width = chunk * group_size
    parts = acc.reshape(pair, seq_size // pair, kv_dev, head_dim + 16, width)
    parts = lax.all_to_all(parts, "sc", 0, 0, tiled=True).astype(jnp.float32)
    part_top = parts[:, :, :, head_dim : head_dim + 1]
    pair_top = jnp.max(part_top, axis=0)
    factor = jnp.exp(part_top - pair_top[None])
    scaled = jnp.sum(parts * factor, axis=0)
    pair_totals = scaled[:, :, head_dim + 1 : head_dim + 2] + scaled[:, :, head_dim + 2 : head_dim + 3]
    high = pair_totals.astype(jnp.bfloat16).astype(jnp.float32)
    low = pair_totals - high
    row = lax.broadcasted_iota(jnp.int32, scaled.shape, 2)
    sent = jnp.where(
        row < head_dim,
        scaled,
        jnp.where(
            row == head_dim,
            pair_top,
            jnp.where(row == head_dim + 1, high, jnp.where(row == head_dim + 2, low, 0.0)),
        ),
    ).astype(jnp.bfloat16)
    got = lax.all_to_all(sent, ("sx", "sy"), 0, 0, tiled=True)
    part_top, part_totals, part_weighted = unpack(got, head_dim, 0)
    top_all = jnp.max(part_top, axis=0)
    factor = jnp.exp(part_top - top_all[None])
    summed_totals = jnp.sum(part_totals * factor, axis=0)
    summed_weighted = jnp.sum(part_weighted * factor[:, :, None, :], axis=0)
    top_all = jnp.transpose(top_all.reshape(kv_dev, chunk, group_size), (1, 0, 2)).reshape(chunk, heads_dev)
    summed_totals = jnp.transpose(
        summed_totals.reshape(kv_dev, chunk, group_size), (1, 0, 2)
    ).reshape(chunk, heads_dev)
    summed_weighted = jnp.transpose(
        summed_weighted.reshape(kv_dev, head_dim, chunk, group_size), (2, 0, 3, 1)
    ).reshape(chunk, heads_dev, head_dim)
    row0 = shard_index * chunk
    request = row0 // tree_size
    token0 = row0 % tree_size
    my_queries = lax.dynamic_slice_in_dim(
        queries.reshape(row_count, heads_dev, head_dim), row0, chunk, 0
    )[None]
    my_keys = lax.dynamic_index_in_dim(draft_keys, request, 0, keepdims=True)
    my_values = lax.dynamic_index_in_dim(draft_values, request, 0, keepdims=True)
    my_reach = lax.dynamic_slice_in_dim(
        lax.dynamic_index_in_dim(reach, request, 0, keepdims=True), token0, chunk, 1
    )
    draft = draft_part(my_queries, my_keys, my_values, my_reach, scaling)
    draft = (draft[0][0], draft[1][0], draft[2][0])
    final_top, final_totals, final_weighted = combine(
        (top_all, summed_totals, summed_weighted), draft
    )
    attention = (final_weighted / final_totals[..., None]).astype(jnp.bfloat16)
    peers = seq_size // pair
    attention = jnp.broadcast_to(attention[None], (peers,) + attention.shape)
    attention = lax.all_to_all(attention, ("sx", "sy"), 0, 0, tiled=True)
    other = lax.ppermute(attention, "sc", [(i, (i + 1) % pair) for i in range(pair)])
    first = jnp.where(core == 0, attention, other)
    second = jnp.where(core == 0, other, attention)
    attention = jnp.stack([first, second], 1)
    attention = attention.reshape(requests, tree_size, heads_dev, head_dim)
    heads_size = lax.axis_size("heads")
    partial = jnp.einsum("rthd,hde->rte", attention, out_weight, preferred_element_type=jnp.float32)
    partial = partial.reshape(heads_size, requests // heads_size, tree_size, partial.shape[-1])
    return jnp.sum(lax.all_to_all(partial, "heads", 0, 0, tiled=True), axis=0)


def solution(mesh):
    heads_size = mesh.shape["heads"]
    sizes = [mesh.shape["seq"] // 8, 4, 2]
    fine = Mesh(np.asarray(mesh.devices).reshape([heads_size] + sizes), ("heads",) + SEQ)
    return jax.shard_map(
        local,
        mesh=fine,
        in_specs=(
            P(None, None, "heads", None),
            P(SEQ, None, "heads", None),
            P(SEQ, None, "heads", None),
            P(None, SEQ),
            P(None, SEQ, "heads", None),
            P(None, SEQ, "heads", None),
            P(),
            P(None, None, "heads", None),
            P(None, None, "heads", None),
            P(),
            P("heads", None, SEQ),
        ),
        out_specs=P("heads", None, SEQ),
        check_vma=False,
    )
```

```python
import math

import jax
import jax.numpy as jnp
from jax import lax
from jax.experimental import pallas as pl
from jax.experimental.pallas import tpu as pltpu
from jax.sharding import Mesh, PartitionSpec as P
import numpy as np


def ancestry(parents):
    tree_size = parents.shape[-1]
    places = jnp.arange(tree_size, dtype=jnp.int32)
    onestep = (parents[..., None] == places).astype(jnp.float32)
    ident = (places[:, None] == places[None, :]).astype(jnp.float32)
    reach = jnp.maximum(onestep, ident)
    for level in range(max(1, (tree_size - 1).bit_length())):
        reach = jnp.minimum(
            jnp.einsum("rij,rjk->rik", reach, reach, precision=lax.Precision.HIGHEST), 1.0
        )
    return reach


def combine(first, second):
    top = jnp.maximum(first[0], second[0])
    first_factor = jnp.exp(first[0] - top)
    second_factor = jnp.exp(second[0] - top)
    totals = first[1] * first_factor + second[1] * second_factor
    weighted = first[2] * first_factor[..., None] + second[2] * second_factor[..., None]
    return (top, totals, weighted)


def draft_part(row_queries, tree_keys, tree_values, row_reach, scaling):
    requests, rows, heads_dev, head_dim = row_queries.shape
    kv_dev = tree_keys.shape[2]
    group_size = heads_dev // kv_dev
    grouped = row_queries.reshape(requests, rows, kv_dev, group_size, head_dim)
    scores = (
        jnp.einsum("rtkgd,rskd->rtkgs", grouped, tree_keys, preferred_element_type=jnp.float32)
        * scaling
    )
    live = (row_reach > 0.5)[:, :, None, None, :]
    scores = jnp.where(live, scores, -1e30)
    highest = jnp.max(scores, axis=-1)
    weights = jnp.where(live, jnp.exp(scores - highest[..., None]), 0.0)
    totals = jnp.sum(weights, axis=-1)
    weighted = jnp.einsum(
        "rtkgs,rskd->rtkgd",
        weights.astype(jnp.bfloat16),
        tree_values,
        preferred_element_type=jnp.float32,
    )
    return (
        highest.reshape(requests, rows, heads_dev),
        totals.reshape(requests, rows, heads_dev),
        weighted.reshape(requests, rows, heads_dev, head_dim),
    )


def context_kernel(use_ref, len_ref, q_ref, kp_ref, vp_ref, ko_ref, vo_ref, acc_ref):
    r = pl.program_id(1)
    scaling = 1.0 / math.sqrt(q_ref.shape[-1])
    q = q_ref[0].reshape(-1, q_ref.shape[-1])
    kp = kp_ref[0]
    ko = ko_ref[0, 0]
    dims = (((1,), (1,)), ((), ()))
    s_pre = lax.dot_general(kp, q, dims, preferred_element_type=jnp.float32) * scaling
    s_own = lax.dot_general(ko, q, dims, preferred_element_type=jnp.float32) * scaling
    n_pre = kp.shape[0]
    n_own = ko.shape[0]
    block_len = n_pre // use_ref.shape[1]
    block_id = lax.broadcasted_iota(jnp.int32, (n_pre, 1), 0) // block_len
    pre_live = jnp.zeros((n_pre, 1), jnp.bool_)
    for b in range(use_ref.shape[1]):
        pre_live = jnp.logical_or(pre_live, jnp.logical_and(block_id == b, use_ref[r, b] == 1))
    own_live = lax.broadcasted_iota(jnp.int32, (n_own, 1), 0) < len_ref[r]
    s_pre = jnp.where(pre_live, s_pre, -1e30)
    s_own = jnp.where(own_live, s_own, -1e30)
    top = jnp.maximum(
        jnp.max(s_pre, axis=0, keepdims=True), jnp.max(s_own, axis=0, keepdims=True)
    )
    top = jnp.maximum(top, -1e29).astype(jnp.bfloat16).astype(jnp.float32)
    w_pre = jnp.exp(s_pre - top)
    w_own = jnp.exp(s_own - top)
    totals = jnp.sum(w_pre, axis=0, keepdims=True) + jnp.sum(w_own, axis=0, keepdims=True)
    acc = jnp.dot(vp_ref[0], w_pre.astype(jnp.bfloat16), preferred_element_type=jnp.float32)
    acc = acc + jnp.dot(
        vo_ref[0, 0], w_own.astype(jnp.bfloat16), preferred_element_type=jnp.float32
    )
    head_dim = acc.shape[0]
    pieces = acc_ref.shape[0] * acc_ref.shape[2]
    width = acc_ref.shape[-1]
    extra = acc_ref.shape[-2] - head_dim
    high = totals.astype(jnp.bfloat16).astype(jnp.float32)
    low = totals - high
    row_id = lax.broadcasted_iota(jnp.int32, (extra, totals.shape[1]), 0)
    stats = jnp.where(row_id == 0, top, jnp.where(row_id == 1, high, jnp.where(row_id == 2, low, 0.0)))
    pair = acc_ref.shape[0]
    for c in range(pieces):
        spot = (c % pair, 0, c // pair, 0)
        acc_ref[spot + (slice(0, head_dim),)] = acc[:, c * width : (c + 1) * width].astype(
            acc_ref.dtype
        )
        acc_ref[spot + (slice(head_dim, None),)] = stats[:, c * width : (c + 1) * width].astype(
            acc_ref.dtype
        )


def context_part(queries, prefix_keys, prefix_values, use_rows, own_lengths, own_keys, own_values, pieces, pair):
    requests, tree_size, heads_dev, head_dim = queries.shape
    block_count, block_len, kv_dev, _ = prefix_keys.shape
    group_size = heads_dev // kv_dev
    private_dev = own_keys.shape[1]
    n_pre = block_count * block_len
    rows = tree_size * group_size
    width = rows // pieces
    kp = jnp.transpose(prefix_keys.reshape(n_pre, kv_dev, head_dim), (1, 0, 2))
    vp = jnp.transpose(prefix_values.reshape(n_pre, kv_dev, head_dim), (1, 2, 0))
    ko = jnp.transpose(own_keys, (0, 2, 1, 3))
    vo = jnp.transpose(own_values, (0, 2, 3, 1))
    grid_spec = pltpu.PrefetchScalarGridSpec(
        num_scalar_prefetch=2,
        grid=(kv_dev, requests),
        in_specs=[
            pl.BlockSpec((1, tree_size, group_size, head_dim), lambda k, r, u, n: (r, 0, k, 0)),
            pl.BlockSpec((1, n_pre, head_dim), lambda k, r, u, n: (k, 0, 0)),
            pl.BlockSpec((1, head_dim, n_pre), lambda k, r, u, n: (k, 0, 0)),
            pl.BlockSpec((1, 1, private_dev, head_dim), lambda k, r, u, n: (r, k, 0, 0)),
            pl.BlockSpec((1, 1, head_dim, private_dev), lambda k, r, u, n: (r, k, 0, 0)),
        ],
        out_specs=pl.BlockSpec(
            (pair, 1, pieces // pair, 1, head_dim + 16, width),
            lambda k, r, u, n: (0, r, 0, k, 0, 0),
        ),
    )
    return pl.pallas_call(
        context_kernel,
        grid_spec=grid_spec,
        out_shape=jax.ShapeDtypeStruct(
            (pair, requests, pieces // pair, kv_dev, head_dim + 16, width), jnp.bfloat16
        ),
    )(use_rows, own_lengths, queries, kp, vp, ko, vo)


SEQ = ("sx", "sy", "sc")


def unpack(parts, head_dim, axis):
    top = parts[:, :, :, head_dim] if axis == 1 else parts[:, :, head_dim]
    high = parts[:, :, :, head_dim + 1] if axis == 1 else parts[:, :, head_dim + 1]
    low = parts[:, :, :, head_dim + 2] if axis == 1 else parts[:, :, head_dim + 2]
    weighted = parts[:, :, :, :head_dim] if axis == 1 else parts[:, :, :head_dim]
    totals = high.astype(jnp.float32) + low.astype(jnp.float32)
    return top.astype(jnp.float32), totals, weighted.astype(jnp.float32)


def local(
    queries,
    prefix_keys,
    prefix_values,
    block_use,
    private_keys,
    private_values,
    private_lengths,
    draft_keys,
    draft_values,
    parents,
    out_weight,
):
    requests, tree_size, heads_dev, head_dim = queries.shape
    kv_dev = prefix_keys.shape[2]
    group_size = heads_dev // kv_dev
    private_dev = private_keys.shape[1]
    scaling = 1.0 / math.sqrt(head_dim)
    shard_index = lax.axis_index(SEQ)
    seq_size = lax.axis_size(SEQ)
    reach = ancestry(parents)
    row_count = requests * tree_size
    chunk = row_count // seq_size
    pieces = tree_size // chunk
    pair = lax.axis_size("sc")
    core = lax.axis_index("sc")
    own_lengths = jnp.clip(private_lengths - shard_index * private_dev, 0, private_dev)
    acc = context_part(
        queries, prefix_keys, prefix_values, block_use, own_lengths, private_keys, private_values, pieces, pair
    )
    width = chunk * group_size
    parts = acc.reshape(pair, seq_size // pair, kv_dev, head_dim + 16, width)
    parts = lax.all_to_all(parts, "sc", 0, 0, tiled=True).astype(jnp.float32)
    part_top = parts[:, :, :, head_dim : head_dim + 1]
    pair_top = jnp.max(part_top, axis=0)
    factor = jnp.exp(part_top - pair_top[None])
    scaled = jnp.sum(parts * factor, axis=0)
    pair_totals = scaled[:, :, head_dim + 1 : head_dim + 2] + scaled[:, :, head_dim + 2 : head_dim + 3]
    high = pair_totals.astype(jnp.bfloat16).astype(jnp.float32)
    low = pair_totals - high
    row = lax.broadcasted_iota(jnp.int32, scaled.shape, 2)
    sent = jnp.where(
        row < head_dim,
        scaled,
        jnp.where(
            row == head_dim,
            pair_top,
            jnp.where(row == head_dim + 1, high, jnp.where(row == head_dim + 2, low, 0.0)),
        ),
    ).astype(jnp.bfloat16)
    got = lax.all_to_all(sent, ("sx", "sy"), 0, 0, tiled=True)
    part_top, part_totals, part_weighted = unpack(got, head_dim, 0)
    top_all = jnp.max(part_top, axis=0)
    factor = jnp.exp(part_top - top_all[None])
    summed_totals = jnp.sum(part_totals * factor, axis=0)
    summed_weighted = jnp.sum(part_weighted * factor[:, :, None, :], axis=0)
    top_all = jnp.transpose(top_all.reshape(kv_dev, chunk, group_size), (1, 0, 2)).reshape(chunk, heads_dev)
    summed_totals = jnp.transpose(
        summed_totals.reshape(kv_dev, chunk, group_size), (1, 0, 2)
    ).reshape(chunk, heads_dev)
    summed_weighted = jnp.transpose(
        summed_weighted.reshape(kv_dev, head_dim, chunk, group_size), (2, 0, 3, 1)
    ).reshape(chunk, heads_dev, head_dim)
    row0 = shard_index * chunk
    request = row0 // tree_size
    token0 = row0 % tree_size
    my_queries = lax.dynamic_slice_in_dim(
        queries.reshape(row_count, heads_dev, head_dim), row0, chunk, 0
    )[None]
    my_keys = lax.dynamic_index_in_dim(draft_keys, request, 0, keepdims=True)
    my_values = lax.dynamic_index_in_dim(draft_values, request, 0, keepdims=True)
    my_reach = lax.dynamic_slice_in_dim(
        lax.dynamic_index_in_dim(reach, request, 0, keepdims=True), token0, chunk, 1
    )
    draft = draft_part(my_queries, my_keys, my_values, my_reach, scaling)
    draft = (draft[0][0], draft[1][0], draft[2][0])
    final_top, final_totals, final_weighted = combine(
        (top_all, summed_totals, summed_weighted), draft
    )
    attention = (final_weighted / final_totals[..., None]).astype(jnp.bfloat16)
    peers = seq_size // pair
    attention = jnp.broadcast_to(attention[None], (peers,) + attention.shape)
    attention = lax.all_to_all(attention, ("sx", "sy"), 0, 0, tiled=True)
    other = lax.ppermute(attention, "sc", [(i, (i + 1) % pair) for i in range(pair)])
    mine = jnp.einsum("xshd,hde->xse", attention, out_weight, preferred_element_type=jnp.float32)
    theirs = jnp.einsum("xshd,hde->xse", other, out_weight, preferred_element_type=jnp.float32)
    first = jnp.where(core == 0, mine, theirs)
    second = jnp.where(core == 0, theirs, mine)
    partial = jnp.stack([first, second], 1)
    heads_size = lax.axis_size("heads")
    partial = partial.reshape(heads_size, requests // heads_size, tree_size, partial.shape[-1])
    return jnp.sum(lax.all_to_all(partial, "heads", 0, 0, tiled=True), axis=0)


def solution(mesh):
    heads_size = mesh.shape["heads"]
    sizes = [mesh.shape["seq"] // 8, 4, 2]
    fine = Mesh(np.asarray(mesh.devices).reshape([heads_size] + sizes), ("heads",) + SEQ)
    return jax.shard_map(
        local,
        mesh=fine,
        in_specs=(
            P(None, None, "heads", None),
            P(SEQ, None, "heads", None),
            P(SEQ, None, "heads", None),
            P(None, SEQ),
            P(None, SEQ, "heads", None),
            P(None, SEQ, "heads", None),
            P(),
            P(None, None, "heads", None),
            P(None, None, "heads", None),
            P(),
            P("heads", None, SEQ),
        ),
        out_specs=P("heads", None, SEQ),
        check_vma=False,
    )
```

```python
import math

import jax
import jax.numpy as jnp
from jax import lax
from jax.experimental import pallas as pl
from jax.experimental.pallas import tpu as pltpu
from jax.sharding import Mesh, PartitionSpec as P
import numpy as np


def ancestry(parents):
    tree_size = parents.shape[-1]
    places = jnp.arange(tree_size, dtype=jnp.int32)
    onestep = (parents[..., None] == places).astype(jnp.float32)
    ident = (places[:, None] == places[None, :]).astype(jnp.float32)
    reach = jnp.maximum(onestep, ident)
    for level in range(max(1, (tree_size - 1).bit_length())):
        reach = jnp.minimum(
            jnp.einsum("rij,rjk->rik", reach, reach, precision=lax.Precision.HIGHEST), 1.0
        )
    return reach


def combine(first, second):
    top = jnp.maximum(first[0], second[0])
    first_factor = jnp.exp(first[0] - top)
    second_factor = jnp.exp(second[0] - top)
    totals = first[1] * first_factor + second[1] * second_factor
    weighted = first[2] * first_factor[..., None] + second[2] * second_factor[..., None]
    return (top, totals, weighted)


def draft_part(row_queries, tree_keys, tree_values, row_reach, scaling):
    requests, rows, heads_dev, head_dim = row_queries.shape
    kv_dev = tree_keys.shape[2]
    group_size = heads_dev // kv_dev
    grouped = row_queries.reshape(requests, rows, kv_dev, group_size, head_dim)
    scores = (
        jnp.einsum("rtkgd,rskd->rtkgs", grouped, tree_keys, preferred_element_type=jnp.float32)
        * scaling
    )
    live = (row_reach > 0.5)[:, :, None, None, :]
    scores = jnp.where(live, scores, -1e30)
    highest = jnp.max(scores, axis=-1)
    weights = jnp.where(live, jnp.exp(scores - highest[..., None]), 0.0)
    totals = jnp.sum(weights, axis=-1)
    weighted = jnp.einsum(
        "rtkgs,rskd->rtkgd",
        weights.astype(jnp.bfloat16),
        tree_values,
        preferred_element_type=jnp.float32,
    )
    return (
        highest.reshape(requests, rows, heads_dev),
        totals.reshape(requests, rows, heads_dev),
        weighted.reshape(requests, rows, heads_dev, head_dim),
    )


def context_kernel(use_ref, len_ref, q_ref, kp_ref, vp_ref, ko_ref, vo_ref, acc_ref):
    r = pl.program_id(1)
    scaling = 1.0 / math.sqrt(q_ref.shape[-1])
    q = q_ref[0].reshape(-1, q_ref.shape[-1])
    kp = kp_ref[0]
    ko = ko_ref[0, 0]
    dims = (((1,), (1,)), ((), ()))
    s_pre = lax.dot_general(kp, q, dims, preferred_element_type=jnp.float32) * scaling
    s_own = lax.dot_general(ko, q, dims, preferred_element_type=jnp.float32) * scaling
    n_pre = kp.shape[0]
    n_own = ko.shape[0]
    block_len = n_pre // use_ref.shape[1]
    block_id = lax.broadcasted_iota(jnp.int32, (n_pre, 1), 0) // block_len
    pre_live = jnp.zeros((n_pre, 1), jnp.bool_)
    for b in range(use_ref.shape[1]):
        pre_live = jnp.logical_or(pre_live, jnp.logical_and(block_id == b, use_ref[r, b] == 1))
    own_live = lax.broadcasted_iota(jnp.int32, (n_own, 1), 0) < len_ref[r]
    s_pre = jnp.where(pre_live, s_pre, -1e30)
    s_own = jnp.where(own_live, s_own, -1e30)
    top = jnp.maximum(
        jnp.max(s_pre, axis=0, keepdims=True), jnp.max(s_own, axis=0, keepdims=True)
    )
    top = jnp.maximum(top, -1e29).astype(jnp.bfloat16).astype(jnp.float32)
    w_pre = jnp.exp(s_pre - top)
    w_own = jnp.exp(s_own - top)
    totals = jnp.sum(w_pre, axis=0, keepdims=True) + jnp.sum(w_own, axis=0, keepdims=True)
    acc = jnp.dot(vp_ref[0], w_pre.astype(jnp.bfloat16), preferred_element_type=jnp.float32)
    acc = acc + jnp.dot(
        vo_ref[0, 0], w_own.astype(jnp.bfloat16), preferred_element_type=jnp.float32
    )
    head_dim = acc.shape[0]
    pieces = acc_ref.shape[0] * acc_ref.shape[2]
    width = acc_ref.shape[-1]
    extra = acc_ref.shape[-2] - head_dim
    high = totals.astype(jnp.bfloat16).astype(jnp.float32)
    low = totals - high
    row_id = lax.broadcasted_iota(jnp.int32, (extra, totals.shape[1]), 0)
    stats = jnp.where(row_id == 0, top, jnp.where(row_id == 1, high, jnp.where(row_id == 2, low, 0.0)))
    pair = acc_ref.shape[0]
    for c in range(pieces):
        spot = (c % pair, 0, c // pair, 0)
        acc_ref[spot + (slice(0, head_dim),)] = acc[:, c * width : (c + 1) * width].astype(
            acc_ref.dtype
        )
        acc_ref[spot + (slice(head_dim, None),)] = stats[:, c * width : (c + 1) * width].astype(
            acc_ref.dtype
        )


def context_part(queries, prefix_keys, prefix_values, use_rows, own_lengths, own_keys, own_values, pieces, pair):
    requests, tree_size, heads_dev, head_dim = queries.shape
    block_count, block_len, kv_dev, _ = prefix_keys.shape
    group_size = heads_dev // kv_dev
    private_dev = own_keys.shape[1]
    n_pre = block_count * block_len
    rows = tree_size * group_size
    width = rows // pieces
    kp = jnp.transpose(prefix_keys.reshape(n_pre, kv_dev, head_dim), (1, 0, 2))
    vp = jnp.transpose(prefix_values.reshape(n_pre, kv_dev, head_dim), (1, 2, 0))
    ko = jnp.transpose(own_keys, (0, 2, 1, 3))
    vo = jnp.transpose(own_values, (0, 2, 3, 1))
    grid_spec = pltpu.PrefetchScalarGridSpec(
        num_scalar_prefetch=2,
        grid=(kv_dev, requests),
        in_specs=[
            pl.BlockSpec((1, tree_size, group_size, head_dim), lambda k, r, u, n: (r, 0, k, 0)),
            pl.BlockSpec((1, n_pre, head_dim), lambda k, r, u, n: (k, 0, 0)),
            pl.BlockSpec((1, head_dim, n_pre), lambda k, r, u, n: (k, 0, 0)),
            pl.BlockSpec((1, 1, private_dev, head_dim), lambda k, r, u, n: (r, k, 0, 0)),
            pl.BlockSpec((1, 1, head_dim, private_dev), lambda k, r, u, n: (r, k, 0, 0)),
        ],
        out_specs=pl.BlockSpec(
            (pair, 1, pieces // pair, 1, head_dim + 16, width),
            lambda k, r, u, n: (0, r, 0, k, 0, 0),
        ),
    )
    return pl.pallas_call(
        context_kernel,
        grid_spec=grid_spec,
        out_shape=jax.ShapeDtypeStruct(
            (pair, requests, pieces // pair, kv_dev, head_dim + 16, width), jnp.bfloat16
        ),
    )(use_rows, own_lengths, queries, kp, vp, ko, vo)


SEQ = ("sx", "sy", "sc")


def exchange(x, axis_name):
    flat = lax.all_to_all(x.reshape(x.shape[0], -1), axis_name, 0, 0, tiled=True)
    return flat.reshape(x.shape)


def unpack(parts, head_dim, axis):
    top = parts[:, :, :, head_dim] if axis == 1 else parts[:, :, head_dim]
    high = parts[:, :, :, head_dim + 1] if axis == 1 else parts[:, :, head_dim + 1]
    low = parts[:, :, :, head_dim + 2] if axis == 1 else parts[:, :, head_dim + 2]
    weighted = parts[:, :, :, :head_dim] if axis == 1 else parts[:, :, :head_dim]
    totals = high.astype(jnp.float32) + low.astype(jnp.float32)
    return top.astype(jnp.float32), totals, weighted.astype(jnp.float32)


def local(
    queries,
    prefix_keys,
    prefix_values,
    block_use,
    private_keys,
    private_values,
    private_lengths,
    draft_keys,
    draft_values,
    parents,
    out_weight,
):
    requests, tree_size, heads_dev, head_dim = queries.shape
    kv_dev = prefix_keys.shape[2]
    group_size = heads_dev // kv_dev
    private_dev = private_keys.shape[1]
    scaling = 1.0 / math.sqrt(head_dim)
    shard_index = lax.axis_index(SEQ)
    seq_size = lax.axis_size(SEQ)
    reach = ancestry(parents)
    row_count = requests * tree_size
    chunk = row_count // seq_size
    pieces = tree_size // chunk
    pair = lax.axis_size("sc")
    core = lax.axis_index("sc")
    own_lengths = jnp.clip(private_lengths - shard_index * private_dev, 0, private_dev)
    acc = context_part(
        queries, prefix_keys, prefix_values, block_use, own_lengths, private_keys, private_values, pieces, pair
    )
    width = chunk * group_size
    parts = acc.reshape(pair, seq_size // pair, kv_dev, head_dim + 16, width)
    parts = lax.all_to_all(parts, "sc", 0, 0, tiled=True).astype(jnp.float32)
    part_top = parts[:, :, :, head_dim : head_dim + 1]
    pair_top = jnp.max(part_top, axis=0)
    factor = jnp.exp(part_top - pair_top[None])
    scaled = jnp.sum(parts * factor, axis=0)
    pair_totals = scaled[:, :, head_dim + 1 : head_dim + 2] + scaled[:, :, head_dim + 2 : head_dim + 3]
    high = pair_totals.astype(jnp.bfloat16).astype(jnp.float32)
    low = pair_totals - high
    row = lax.broadcasted_iota(jnp.int32, scaled.shape, 2)
    sent = jnp.where(
        row < head_dim,
        scaled,
        jnp.where(
            row == head_dim,
            pair_top,
            jnp.where(row == head_dim + 1, high, jnp.where(row == head_dim + 2, low, 0.0)),
        ),
    ).astype(jnp.bfloat16)
    got = exchange(sent, ("sx", "sy"))
    part_top, part_totals, part_weighted = unpack(got, head_dim, 0)
    top_all = jnp.max(part_top, axis=0)
    factor = jnp.exp(part_top - top_all[None])
    summed_totals = jnp.sum(part_totals * factor, axis=0)
    summed_weighted = jnp.sum(part_weighted * factor[:, :, None, :], axis=0)
    top_all = jnp.transpose(top_all.reshape(kv_dev, chunk, group_size), (1, 0, 2)).reshape(chunk, heads_dev)
    summed_totals = jnp.transpose(
        summed_totals.reshape(kv_dev, chunk, group_size), (1, 0, 2)
    ).reshape(chunk, heads_dev)
    summed_weighted = jnp.transpose(
        summed_weighted.reshape(kv_dev, head_dim, chunk, group_size), (2, 0, 3, 1)
    ).reshape(chunk, heads_dev, head_dim)
    row0 = shard_index * chunk
    request = row0 // tree_size
    token0 = row0 % tree_size
    my_queries = lax.dynamic_slice_in_dim(
        queries.reshape(row_count, heads_dev, head_dim), row0, chunk, 0
    )[None]
    my_keys = lax.dynamic_index_in_dim(draft_keys, request, 0, keepdims=True)
    my_values = lax.dynamic_index_in_dim(draft_values, request, 0, keepdims=True)
    my_reach = lax.dynamic_slice_in_dim(
        lax.dynamic_index_in_dim(reach, request, 0, keepdims=True), token0, chunk, 1
    )
    draft = draft_part(my_queries, my_keys, my_values, my_reach, scaling)
    draft = (draft[0][0], draft[1][0], draft[2][0])
    final_top, final_totals, final_weighted = combine(
        (top_all, summed_totals, summed_weighted), draft
    )
    attention = (final_weighted / final_totals[..., None]).astype(jnp.bfloat16)
    peers = seq_size // pair
    attention = jnp.broadcast_to(attention[None], (peers,) + attention.shape)
    attention = lax.all_to_all(attention, ("sx", "sy"), 0, 0, tiled=True)
    other = lax.ppermute(attention, "sc", [(i, (i + 1) % pair) for i in range(pair)])
    mine = jnp.einsum("xshd,hde->xse", attention, out_weight, preferred_element_type=jnp.float32)
    theirs = jnp.einsum("xshd,hde->xse", other, out_weight, preferred_element_type=jnp.float32)
    first = jnp.where(core == 0, mine, theirs)
    second = jnp.where(core == 0, theirs, mine)
    partial = jnp.stack([first, second], 1)
    heads_size = lax.axis_size("heads")
    partial = partial.reshape(heads_size, requests // heads_size, tree_size, partial.shape[-1])
    return jnp.sum(lax.all_to_all(partial, "heads", 0, 0, tiled=True), axis=0)


def solution(mesh):
    heads_size = mesh.shape["heads"]
    sizes = [mesh.shape["seq"] // 8, 4, 2]
    fine = Mesh(np.asarray(mesh.devices).reshape([heads_size] + sizes), ("heads",) + SEQ)
    return jax.shard_map(
        local,
        mesh=fine,
        in_specs=(
            P(None, None, "heads", None),
            P(SEQ, None, "heads", None),
            P(SEQ, None, "heads", None),
            P(None, SEQ),
            P(None, SEQ, "heads", None),
            P(None, SEQ, "heads", None),
            P(),
            P(None, None, "heads", None),
            P(None, None, "heads", None),
            P(),
            P("heads", None, SEQ),
        ),
        out_specs=P("heads", None, SEQ),
        check_vma=False,
    )
```

```python
import math

import jax
import jax.numpy as jnp
from jax import lax
from jax.experimental import pallas as pl
from jax.experimental.pallas import tpu as pltpu
from jax.sharding import Mesh, PartitionSpec as P
import numpy as np


def ancestry(parents):
    tree_size = parents.shape[-1]
    places = jnp.arange(tree_size, dtype=jnp.int32)
    onestep = (parents[..., None] == places).astype(jnp.float32)
    ident = (places[:, None] == places[None, :]).astype(jnp.float32)
    reach = jnp.maximum(onestep, ident)
    for level in range(max(1, (tree_size - 1).bit_length())):
        reach = jnp.minimum(
            jnp.einsum("rij,rjk->rik", reach, reach, precision=lax.Precision.HIGHEST), 1.0
        )
    return reach


def combine(first, second):
    top = jnp.maximum(first[0], second[0])
    first_factor = jnp.exp(first[0] - top)
    second_factor = jnp.exp(second[0] - top)
    totals = first[1] * first_factor + second[1] * second_factor
    weighted = first[2] * first_factor[..., None] + second[2] * second_factor[..., None]
    return (top, totals, weighted)


def draft_part(row_queries, tree_keys, tree_values, row_reach, scaling):
    requests, rows, heads_dev, head_dim = row_queries.shape
    kv_dev = tree_keys.shape[2]
    group_size = heads_dev // kv_dev
    grouped = row_queries.reshape(requests, rows, kv_dev, group_size, head_dim)
    scores = (
        jnp.einsum("rtkgd,rskd->rtkgs", grouped, tree_keys, preferred_element_type=jnp.float32)
        * scaling
    )
    live = (row_reach > 0.5)[:, :, None, None, :]
    scores = jnp.where(live, scores, -1e30)
    highest = jnp.max(scores, axis=-1)
    weights = jnp.where(live, jnp.exp(scores - highest[..., None]), 0.0)
    totals = jnp.sum(weights, axis=-1)
    weighted = jnp.einsum(
        "rtkgs,rskd->rtkgd",
        weights.astype(jnp.bfloat16),
        tree_values,
        preferred_element_type=jnp.float32,
    )
    return (
        highest.reshape(requests, rows, heads_dev),
        totals.reshape(requests, rows, heads_dev),
        weighted.reshape(requests, rows, heads_dev, head_dim),
    )


def pick(ref, k):
    heads = ref.shape[-2]
    rows = [ref[..., j, :].reshape(-1, ref.shape[-1]) for j in range(heads)]
    picked = rows[0]
    for j in range(1, heads):
        picked = jnp.where(k == j, rows[j], picked)
    return picked


def context_kernel(use_ref, len_ref, q_ref, kp_ref, vp_ref, ko_ref, vo_ref, acc_ref):
    r = pl.program_id(0)
    k = pl.program_id(1)
    scaling = 1.0 / math.sqrt(q_ref.shape[-1])
    q = q_ref[0].reshape(-1, q_ref.shape[-1])
    kp = pick(kp_ref, k)
    ko = pick(ko_ref, k)
    vp = pick(vp_ref, k)
    vo = pick(vo_ref, k)
    dims = (((1,), (1,)), ((), ()))
    s_pre = lax.dot_general(kp, q, dims, preferred_element_type=jnp.float32) * scaling
    s_own = lax.dot_general(ko, q, dims, preferred_element_type=jnp.float32) * scaling
    n_pre = kp.shape[0]
    n_own = ko.shape[0]
    block_len = n_pre // use_ref.shape[1]
    block_id = lax.broadcasted_iota(jnp.int32, (n_pre, 1), 0) // block_len
    pre_live = jnp.zeros((n_pre, 1), jnp.bool_)
    for b in range(use_ref.shape[1]):
        pre_live = jnp.logical_or(pre_live, jnp.logical_and(block_id == b, use_ref[r, b] == 1))
    own_live = lax.broadcasted_iota(jnp.int32, (n_own, 1), 0) < len_ref[r]
    s_pre = jnp.where(pre_live, s_pre, -1e30)
    s_own = jnp.where(own_live, s_own, -1e30)
    top = jnp.maximum(
        jnp.max(s_pre, axis=0, keepdims=True), jnp.max(s_own, axis=0, keepdims=True)
    )
    top = jnp.maximum(top, -1e29).astype(jnp.bfloat16).astype(jnp.float32)
    w_pre = jnp.exp(s_pre - top)
    w_own = jnp.exp(s_own - top)
    totals = jnp.sum(w_pre, axis=0, keepdims=True) + jnp.sum(w_own, axis=0, keepdims=True)
    lead = (((0,), (0,)), ((), ()))
    acc = lax.dot_general(vp, w_pre.astype(jnp.bfloat16), lead, preferred_element_type=jnp.float32)
    acc = acc + lax.dot_general(
        vo, w_own.astype(jnp.bfloat16), lead, preferred_element_type=jnp.float32
    )
    head_dim = acc.shape[0]
    pieces = acc_ref.shape[0] * acc_ref.shape[2]
    width = acc_ref.shape[-1]
    extra = acc_ref.shape[-2] - head_dim
    high = totals.astype(jnp.bfloat16).astype(jnp.float32)
    low = totals - high
    row_id = lax.broadcasted_iota(jnp.int32, (extra, totals.shape[1]), 0)
    stats = jnp.where(row_id == 0, top, jnp.where(row_id == 1, high, jnp.where(row_id == 2, low, 0.0)))
    pair = acc_ref.shape[0]
    for c in range(pieces):
        spot = (c % pair, 0, c // pair, 0)
        acc_ref[spot + (slice(0, head_dim),)] = acc[:, c * width : (c + 1) * width].astype(
            acc_ref.dtype
        )
        acc_ref[spot + (slice(head_dim, None),)] = stats[:, c * width : (c + 1) * width].astype(
            acc_ref.dtype
        )


def context_part(queries, prefix_keys, prefix_values, use_rows, own_lengths, own_keys, own_values, pieces, pair):
    requests, tree_size, heads_dev, head_dim = queries.shape
    block_count, block_len, kv_dev, _ = prefix_keys.shape
    group_size = heads_dev // kv_dev
    private_dev = own_keys.shape[1]
    n_pre = block_count * block_len
    rows = tree_size * group_size
    width = rows // pieces
    grid_spec = pltpu.PrefetchScalarGridSpec(
        num_scalar_prefetch=2,
        grid=(requests, kv_dev),
        in_specs=[
            pl.BlockSpec((1, tree_size, group_size, head_dim), lambda r, k, u, n: (r, 0, k, 0)),
            pl.BlockSpec((block_count, block_len, kv_dev, head_dim), lambda r, k, u, n: (0, 0, 0, 0)),
            pl.BlockSpec((block_count, block_len, kv_dev, head_dim), lambda r, k, u, n: (0, 0, 0, 0)),
            pl.BlockSpec((1, private_dev, kv_dev, head_dim), lambda r, k, u, n: (r, 0, 0, 0)),
            pl.BlockSpec((1, private_dev, kv_dev, head_dim), lambda r, k, u, n: (r, 0, 0, 0)),
        ],
        out_specs=pl.BlockSpec(
            (pair, 1, pieces // pair, 1, head_dim + 16, width),
            lambda r, k, u, n: (0, r, 0, k, 0, 0),
        ),
    )
    return pl.pallas_call(
        context_kernel,
        grid_spec=grid_spec,
        out_shape=jax.ShapeDtypeStruct(
            (pair, requests, pieces // pair, kv_dev, head_dim + 16, width), jnp.bfloat16
        ),
    )(use_rows, own_lengths, queries, prefix_keys, prefix_values, own_keys, own_values)


SEQ = ("sx", "sy", "sc")


def unpack(parts, head_dim, axis):
    top = parts[:, :, :, head_dim] if axis == 1 else parts[:, :, head_dim]
    high = parts[:, :, :, head_dim + 1] if axis == 1 else parts[:, :, head_dim + 1]
    low = parts[:, :, :, head_dim + 2] if axis == 1 else parts[:, :, head_dim + 2]
    weighted = parts[:, :, :, :head_dim] if axis == 1 else parts[:, :, :head_dim]
    totals = high.astype(jnp.float32) + low.astype(jnp.float32)
    return top.astype(jnp.float32), totals, weighted.astype(jnp.float32)


def local(
    queries,
    prefix_keys,
    prefix_values,
    block_use,
    private_keys,
    private_values,
    private_lengths,
    draft_keys,
    draft_values,
    parents,
    out_weight,
):
    requests, tree_size, heads_dev, head_dim = queries.shape
    kv_dev = prefix_keys.shape[2]
    group_size = heads_dev // kv_dev
    private_dev = private_keys.shape[1]
    scaling = 1.0 / math.sqrt(head_dim)
    shard_index = lax.axis_index(SEQ)
    seq_size = lax.axis_size(SEQ)
    reach = ancestry(parents)
    row_count = requests * tree_size
    chunk = row_count // seq_size
    pieces = tree_size // chunk
    pair = lax.axis_size("sc")
    core = lax.axis_index("sc")
    own_lengths = jnp.clip(private_lengths - shard_index * private_dev, 0, private_dev)
    acc = context_part(
        queries, prefix_keys, prefix_values, block_use, own_lengths, private_keys, private_values, pieces, pair
    )
    width = chunk * group_size
    parts = acc.reshape(pair, seq_size // pair, kv_dev, head_dim + 16, width)
    parts = lax.all_to_all(parts, "sc", 0, 0, tiled=True).astype(jnp.float32)
    part_top = parts[:, :, :, head_dim : head_dim + 1]
    pair_top = jnp.max(part_top, axis=0)
    factor = jnp.exp(part_top - pair_top[None])
    scaled = jnp.sum(parts * factor, axis=0)
    pair_totals = scaled[:, :, head_dim + 1 : head_dim + 2] + scaled[:, :, head_dim + 2 : head_dim + 3]
    high = pair_totals.astype(jnp.bfloat16).astype(jnp.float32)
    low = pair_totals - high
    row = lax.broadcasted_iota(jnp.int32, scaled.shape, 2)
    sent = jnp.where(
        row < head_dim,
        scaled,
        jnp.where(
            row == head_dim,
            pair_top,
            jnp.where(row == head_dim + 1, high, jnp.where(row == head_dim + 2, low, 0.0)),
        ),
    ).astype(jnp.bfloat16)
    got = lax.all_to_all(sent, ("sx", "sy"), 0, 0, tiled=True)
    part_top, part_totals, part_weighted = unpack(got, head_dim, 0)
    top_all = jnp.max(part_top, axis=0)
    factor = jnp.exp(part_top - top_all[None])
    summed_totals = jnp.sum(part_totals * factor, axis=0)
    summed_weighted = jnp.sum(part_weighted * factor[:, :, None, :], axis=0)
    top_all = jnp.transpose(top_all.reshape(kv_dev, chunk, group_size), (1, 0, 2)).reshape(chunk, heads_dev)
    summed_totals = jnp.transpose(
        summed_totals.reshape(kv_dev, chunk, group_size), (1, 0, 2)
    ).reshape(chunk, heads_dev)
    summed_weighted = jnp.transpose(
        summed_weighted.reshape(kv_dev, head_dim, chunk, group_size), (2, 0, 3, 1)
    ).reshape(chunk, heads_dev, head_dim)
    row0 = shard_index * chunk
    request = row0 // tree_size
    token0 = row0 % tree_size
    my_queries = lax.dynamic_slice_in_dim(
        queries.reshape(row_count, heads_dev, head_dim), row0, chunk, 0
    )[None]
    my_keys = lax.dynamic_index_in_dim(draft_keys, request, 0, keepdims=True)
    my_values = lax.dynamic_index_in_dim(draft_values, request, 0, keepdims=True)
    my_reach = lax.dynamic_slice_in_dim(
        lax.dynamic_index_in_dim(reach, request, 0, keepdims=True), token0, chunk, 1
    )
    draft = draft_part(my_queries, my_keys, my_values, my_reach, scaling)
    draft = (draft[0][0], draft[1][0], draft[2][0])
    final_top, final_totals, final_weighted = combine(
        (top_all, summed_totals, summed_weighted), draft
    )
    attention = (final_weighted / final_totals[..., None]).astype(jnp.bfloat16)
    peers = seq_size // pair
    attention = jnp.broadcast_to(attention[None], (peers,) + attention.shape)
    attention = lax.all_to_all(attention, ("sx", "sy"), 0, 0, tiled=True)
    other = lax.ppermute(attention, "sc", [(i, (i + 1) % pair) for i in range(pair)])
    mine = jnp.einsum("xshd,hde->xse", attention, out_weight, preferred_element_type=jnp.float32)
    theirs = jnp.einsum("xshd,hde->xse", other, out_weight, preferred_element_type=jnp.float32)
    first = jnp.where(core == 0, mine, theirs)
    second = jnp.where(core == 0, theirs, mine)
    partial = jnp.stack([first, second], 1)
    heads_size = lax.axis_size("heads")
    partial = partial.reshape(heads_size, requests // heads_size, tree_size, partial.shape[-1])
    return jnp.sum(lax.all_to_all(partial, "heads", 0, 0, tiled=True), axis=0)


def solution(mesh):
    heads_size = mesh.shape["heads"]
    sizes = [mesh.shape["seq"] // 8, 4, 2]
    fine = Mesh(np.asarray(mesh.devices).reshape([heads_size] + sizes), ("heads",) + SEQ)
    return jax.shard_map(
        local,
        mesh=fine,
        in_specs=(
            P(None, None, "heads", None),
            P(SEQ, None, "heads", None),
            P(SEQ, None, "heads", None),
            P(None, SEQ),
            P(None, SEQ, "heads", None),
            P(None, SEQ, "heads", None),
            P(),
            P(None, None, "heads", None),
            P(None, None, "heads", None),
            P(),
            P("heads", None, SEQ),
        ),
        out_specs=P("heads", None, SEQ),
        check_vma=False,
    )
```

```python
import math

import jax
import jax.numpy as jnp
from jax import lax
from jax.experimental import pallas as pl
from jax.experimental.pallas import tpu as pltpu
from jax.sharding import Mesh, PartitionSpec as P
import numpy as np


def ancestry(parents):
    tree_size = parents.shape[-1]
    places = jnp.arange(tree_size, dtype=jnp.int32)
    onestep = (parents[..., None] == places).astype(jnp.float32)
    ident = (places[:, None] == places[None, :]).astype(jnp.float32)
    reach = jnp.maximum(onestep, ident)
    for level in range(max(1, (tree_size - 1).bit_length())):
        reach = jnp.minimum(
            jnp.einsum("rij,rjk->rik", reach, reach, precision=lax.Precision.HIGHEST), 1.0
        )
    return reach


def combine(first, second):
    top = jnp.maximum(first[0], second[0])
    first_factor = jnp.exp(first[0] - top)
    second_factor = jnp.exp(second[0] - top)
    totals = first[1] * first_factor + second[1] * second_factor
    weighted = first[2] * first_factor[..., None] + second[2] * second_factor[..., None]
    return (top, totals, weighted)


def draft_part(row_queries, tree_keys, tree_values, row_reach, scaling):
    requests, rows, heads_dev, head_dim = row_queries.shape
    kv_dev = tree_keys.shape[2]
    group_size = heads_dev // kv_dev
    grouped = row_queries.reshape(requests, rows, kv_dev, group_size, head_dim)
    scores = (
        jnp.einsum("rtkgd,rskd->rtkgs", grouped, tree_keys, preferred_element_type=jnp.float32)
        * scaling
    )
    live = (row_reach > 0.5)[:, :, None, None, :]
    scores = jnp.where(live, scores, -1e30)
    highest = jnp.max(scores, axis=-1)
    weights = jnp.where(live, jnp.exp(scores - highest[..., None]), 0.0)
    totals = jnp.sum(weights, axis=-1)
    weighted = jnp.einsum(
        "rtkgs,rskd->rtkgd",
        weights.astype(jnp.bfloat16),
        tree_values,
        preferred_element_type=jnp.float32,
    )
    return (
        highest.reshape(requests, rows, heads_dev),
        totals.reshape(requests, rows, heads_dev),
        weighted.reshape(requests, rows, heads_dev, head_dim),
    )


def context_kernel(use_ref, len_ref, q_ref, kp_ref, vp_ref, ko_ref, vo_ref, acc_ref):
    r = pl.program_id(1)
    scaling = 1.0 / math.sqrt(q_ref.shape[-1])
    q = q_ref[0].reshape(-1, q_ref.shape[-1])
    kp = kp_ref[0]
    ko = ko_ref[0, 0]
    dims = (((1,), (1,)), ((), ()))
    s_pre = lax.dot_general(kp, q, dims, preferred_element_type=jnp.float32) * scaling
    s_own = lax.dot_general(ko, q, dims, preferred_element_type=jnp.float32) * scaling
    n_pre = kp.shape[0]
    n_own = ko.shape[0]
    block_len = n_pre // use_ref.shape[1]
    block_id = lax.broadcasted_iota(jnp.int32, (n_pre, 1), 0) // block_len
    pre_live = jnp.zeros((n_pre, 1), jnp.bool_)
    for b in range(use_ref.shape[1]):
        pre_live = jnp.logical_or(pre_live, jnp.logical_and(block_id == b, use_ref[r, b] == 1))
    own_live = lax.broadcasted_iota(jnp.int32, (n_own, 1), 0) < len_ref[r]
    s_pre = jnp.where(pre_live, s_pre, -1e30)
    s_own = jnp.where(own_live, s_own, -1e30)
    top = jnp.maximum(
        jnp.max(s_pre, axis=0, keepdims=True), jnp.max(s_own, axis=0, keepdims=True)
    )
    top = jnp.maximum(top, -1e29).astype(jnp.bfloat16).astype(jnp.float32)
    w_pre = jnp.exp(s_pre - top)
    w_own = jnp.exp(s_own - top)
    totals = jnp.sum(w_pre, axis=0, keepdims=True) + jnp.sum(w_own, axis=0, keepdims=True)
    acc = jnp.dot(vp_ref[0], w_pre.astype(jnp.bfloat16), preferred_element_type=jnp.float32)
    acc = acc + jnp.dot(
        vo_ref[0, 0], w_own.astype(jnp.bfloat16), preferred_element_type=jnp.float32
    )
    head_dim = acc.shape[0]
    pieces = acc_ref.shape[0] * acc_ref.shape[2]
    width = acc_ref.shape[-1]
    extra = acc_ref.shape[-2] - head_dim
    high = totals.astype(jnp.bfloat16).astype(jnp.float32)
    low = totals - high
    row_id = lax.broadcasted_iota(jnp.int32, (extra, totals.shape[1]), 0)
    stats = jnp.where(row_id == 0, top, jnp.where(row_id == 1, high, jnp.where(row_id == 2, low, 0.0)))
    pair = acc_ref.shape[0]
    for c in range(pieces):
        spot = (c % pair, 0, c // pair, 0)
        acc_ref[spot + (slice(0, head_dim),)] = acc[:, c * width : (c + 1) * width].astype(
            acc_ref.dtype
        )
        acc_ref[spot + (slice(head_dim, None),)] = stats[:, c * width : (c + 1) * width].astype(
            acc_ref.dtype
        )


def context_part(queries, prefix_keys, prefix_values, use_rows, own_lengths, own_keys, own_values, pieces, pair):
    requests, tree_size, heads_dev, head_dim = queries.shape
    block_count, block_len, kv_dev, _ = prefix_keys.shape
    group_size = heads_dev // kv_dev
    private_dev = own_keys.shape[1]
    n_pre = block_count * block_len
    rows = tree_size * group_size
    width = rows // pieces
    kp = jnp.transpose(prefix_keys.reshape(n_pre, kv_dev, head_dim), (1, 0, 2))
    vp = jnp.transpose(prefix_values.reshape(n_pre, kv_dev, head_dim), (1, 2, 0))
    ko = jnp.transpose(own_keys, (0, 2, 1, 3))
    vo = jnp.transpose(own_values, (0, 2, 3, 1))
    grid_spec = pltpu.PrefetchScalarGridSpec(
        num_scalar_prefetch=2,
        grid=(kv_dev, requests),
        in_specs=[
            pl.BlockSpec((1, tree_size, group_size, head_dim), lambda k, r, u, n: (r, 0, k, 0)),
            pl.BlockSpec((1, n_pre, head_dim), lambda k, r, u, n: (k, 0, 0)),
            pl.BlockSpec((1, head_dim, n_pre), lambda k, r, u, n: (k, 0, 0)),
            pl.BlockSpec((1, 1, private_dev, head_dim), lambda k, r, u, n: (r, k, 0, 0)),
            pl.BlockSpec((1, 1, head_dim, private_dev), lambda k, r, u, n: (r, k, 0, 0)),
        ],
        out_specs=pl.BlockSpec(
            (pair, 1, pieces // pair, 1, head_dim + 16, width),
            lambda k, r, u, n: (0, r, 0, k, 0, 0),
        ),
    )
    return pl.pallas_call(
        context_kernel,
        grid_spec=grid_spec,
        out_shape=jax.ShapeDtypeStruct(
            (pair, requests, pieces // pair, kv_dev, head_dim + 16, width), jnp.bfloat16
        ),
    )(use_rows, own_lengths, queries, kp, vp, ko, vo)


SEQ = ("sx", "sy", "sc")


def unpack(parts, head_dim, axis):
    top = parts[:, :, :, head_dim] if axis == 1 else parts[:, :, head_dim]
    high = parts[:, :, :, head_dim + 1] if axis == 1 else parts[:, :, head_dim + 1]
    low = parts[:, :, :, head_dim + 2] if axis == 1 else parts[:, :, head_dim + 2]
    weighted = parts[:, :, :, :head_dim] if axis == 1 else parts[:, :, :head_dim]
    totals = high.astype(jnp.float32) + low.astype(jnp.float32)
    return top.astype(jnp.float32), totals, weighted.astype(jnp.float32)


def local(
    queries,
    prefix_keys,
    prefix_values,
    block_use,
    private_keys,
    private_values,
    private_lengths,
    draft_keys,
    draft_values,
    parents,
    out_weight,
):
    requests, tree_size, heads_dev, head_dim = queries.shape
    kv_dev = prefix_keys.shape[2]
    group_size = heads_dev // kv_dev
    private_dev = private_keys.shape[1]
    scaling = 1.0 / math.sqrt(head_dim)
    shard_index = lax.axis_index(SEQ)
    seq_size = lax.axis_size(SEQ)
    reach = ancestry(parents)
    row_count = requests * tree_size
    chunk = row_count // seq_size
    pieces = tree_size // chunk
    pair = lax.axis_size("sc")
    core = lax.axis_index("sc")
    own_lengths = jnp.clip(private_lengths - shard_index * private_dev, 0, private_dev)
    acc = context_part(
        queries, prefix_keys, prefix_values, block_use, own_lengths, private_keys, private_values, pieces, pair
    )
    width = chunk * group_size
    parts = acc.reshape(pair, seq_size // pair, kv_dev, head_dim + 16, width)
    keep = lax.dynamic_index_in_dim(parts, core, 0, keepdims=False)
    send = lax.dynamic_index_in_dim(parts, pair - 1 - core, 0, keepdims=False)
    recv = lax.ppermute(send, "sc", [(i, (i + 1) % pair) for i in range(pair)])
    keep = keep.astype(jnp.float32)
    recv = recv.astype(jnp.float32)
    keep_top = keep[:, :, head_dim : head_dim + 1]
    recv_top = recv[:, :, head_dim : head_dim + 1]
    pair_top = jnp.maximum(keep_top, recv_top)
    scaled = keep * jnp.exp(keep_top - pair_top) + recv * jnp.exp(recv_top - pair_top)
    pair_totals = scaled[:, :, head_dim + 1 : head_dim + 2] + scaled[:, :, head_dim + 2 : head_dim + 3]
    high = pair_totals.astype(jnp.bfloat16).astype(jnp.float32)
    low = pair_totals - high
    row = lax.broadcasted_iota(jnp.int32, scaled.shape, 2)
    sent = jnp.where(
        row < head_dim,
        scaled,
        jnp.where(
            row == head_dim,
            pair_top,
            jnp.where(row == head_dim + 1, high, jnp.where(row == head_dim + 2, low, 0.0)),
        ),
    ).astype(jnp.bfloat16)
    got = lax.all_to_all(sent, ("sx", "sy"), 0, 0, tiled=True)
    part_top, part_totals, part_weighted = unpack(got, head_dim, 0)
    top_all = jnp.max(part_top, axis=0)
    factor = jnp.exp(part_top - top_all[None])
    summed_totals = jnp.sum(part_totals * factor, axis=0)
    summed_weighted = jnp.sum(part_weighted * factor[:, :, None, :], axis=0)
    top_all = jnp.transpose(top_all.reshape(kv_dev, chunk, group_size), (1, 0, 2)).reshape(chunk, heads_dev)
    summed_totals = jnp.transpose(
        summed_totals.reshape(kv_dev, chunk, group_size), (1, 0, 2)
    ).reshape(chunk, heads_dev)
    summed_weighted = jnp.transpose(
        summed_weighted.reshape(kv_dev, head_dim, chunk, group_size), (2, 0, 3, 1)
    ).reshape(chunk, heads_dev, head_dim)
    row0 = shard_index * chunk
    request = row0 // tree_size
    token0 = row0 % tree_size
    my_queries = lax.dynamic_slice_in_dim(
        queries.reshape(row_count, heads_dev, head_dim), row0, chunk, 0
    )[None]
    my_keys = lax.dynamic_index_in_dim(draft_keys, request, 0, keepdims=True)
    my_values = lax.dynamic_index_in_dim(draft_values, request, 0, keepdims=True)
    my_reach = lax.dynamic_slice_in_dim(
        lax.dynamic_index_in_dim(reach, request, 0, keepdims=True), token0, chunk, 1
    )
    draft = draft_part(my_queries, my_keys, my_values, my_reach, scaling)
    draft = (draft[0][0], draft[1][0], draft[2][0])
    final_top, final_totals, final_weighted = combine(
        (top_all, summed_totals, summed_weighted), draft
    )
    attention = (final_weighted / final_totals[..., None]).astype(jnp.bfloat16)
    peers = seq_size // pair
    attention = jnp.broadcast_to(attention[None], (peers,) + attention.shape)
    attention = lax.all_to_all(attention, ("sx", "sy"), 0, 0, tiled=True)
    other = lax.ppermute(attention, "sc", [(i, (i + 1) % pair) for i in range(pair)])
    mine = jnp.einsum("xshd,hde->xse", attention, out_weight, preferred_element_type=jnp.float32)
    theirs = jnp.einsum("xshd,hde->xse", other, out_weight, preferred_element_type=jnp.float32)
    first = jnp.where(core == 0, mine, theirs)
    second = jnp.where(core == 0, theirs, mine)
    partial = jnp.stack([first, second], 1)
    heads_size = lax.axis_size("heads")
    partial = partial.reshape(heads_size, requests // heads_size, tree_size, partial.shape[-1])
    return jnp.sum(lax.all_to_all(partial, "heads", 0, 0, tiled=True), axis=0)


def solution(mesh):
    heads_size = mesh.shape["heads"]
    sizes = [mesh.shape["seq"] // 8, 4, 2]
    fine = Mesh(np.asarray(mesh.devices).reshape([heads_size] + sizes), ("heads",) + SEQ)
    return jax.shard_map(
        local,
        mesh=fine,
        in_specs=(
            P(None, None, "heads", None),
            P(SEQ, None, "heads", None),
            P(SEQ, None, "heads", None),
            P(None, SEQ),
            P(None, SEQ, "heads", None),
            P(None, SEQ, "heads", None),
            P(),
            P(None, None, "heads", None),
            P(None, None, "heads", None),
            P(),
            P("heads", None, SEQ),
        ),
        out_specs=P("heads", None, SEQ),
        check_vma=False,
    )
```

```python
import math

import jax
import jax.numpy as jnp
from jax import lax
from jax.experimental import pallas as pl
from jax.experimental.pallas import tpu as pltpu
from jax.sharding import Mesh, PartitionSpec as P
import numpy as np


def ancestry(parents):
    tree_size = parents.shape[-1]
    places = jnp.arange(tree_size, dtype=jnp.int32)
    onestep = (parents[..., None] == places).astype(jnp.float32)
    ident = (places[:, None] == places[None, :]).astype(jnp.float32)
    reach = jnp.maximum(onestep, ident)
    for level in range(max(1, (tree_size - 1).bit_length())):
        reach = jnp.minimum(
            jnp.einsum("rij,rjk->rik", reach, reach, precision=lax.Precision.HIGHEST), 1.0
        )
    return reach


def combine(first, second):
    top = jnp.maximum(first[0], second[0])
    first_factor = jnp.exp(first[0] - top)
    second_factor = jnp.exp(second[0] - top)
    totals = first[1] * first_factor + second[1] * second_factor
    weighted = first[2] * first_factor[..., None] + second[2] * second_factor[..., None]
    return (top, totals, weighted)


def draft_part(row_queries, tree_keys, tree_values, row_reach, scaling):
    requests, rows, heads_dev, head_dim = row_queries.shape
    kv_dev = tree_keys.shape[2]
    group_size = heads_dev // kv_dev
    grouped = row_queries.reshape(requests, rows, kv_dev, group_size, head_dim)
    scores = (
        jnp.einsum("rtkgd,rskd->rtkgs", grouped, tree_keys, preferred_element_type=jnp.float32)
        * scaling
    )
    live = (row_reach > 0.5)[:, :, None, None, :]
    scores = jnp.where(live, scores, -1e30)
    highest = jnp.max(scores, axis=-1)
    weights = jnp.where(live, jnp.exp(scores - highest[..., None]), 0.0)
    totals = jnp.sum(weights, axis=-1)
    weighted = jnp.einsum(
        "rtkgs,rskd->rtkgd",
        weights.astype(jnp.bfloat16),
        tree_values,
        preferred_element_type=jnp.float32,
    )
    return (
        highest.reshape(requests, rows, heads_dev),
        totals.reshape(requests, rows, heads_dev),
        weighted.reshape(requests, rows, heads_dev, head_dim),
    )


def context_kernel(use_ref, len_ref, q_ref, kp_ref, vp_ref, ko_ref, vo_ref, acc_ref):
    r = pl.program_id(1)
    scaling = 1.0 / math.sqrt(q_ref.shape[-1])
    q = q_ref[0].reshape(-1, q_ref.shape[-1])
    kp = kp_ref[0]
    ko = ko_ref[0, 0]
    dims = (((1,), (1,)), ((), ()))
    s_pre = lax.dot_general(kp, q, dims, preferred_element_type=jnp.float32) * scaling
    s_own = lax.dot_general(ko, q, dims, preferred_element_type=jnp.float32) * scaling
    n_pre = kp.shape[0]
    n_own = ko.shape[0]
    block_len = n_pre // use_ref.shape[1]
    block_id = lax.broadcasted_iota(jnp.int32, (n_pre, 1), 0) // block_len
    pre_live = jnp.zeros((n_pre, 1), jnp.bool_)
    for b in range(use_ref.shape[1]):
        pre_live = jnp.logical_or(pre_live, jnp.logical_and(block_id == b, use_ref[r, b] == 1))
    own_live = lax.broadcasted_iota(jnp.int32, (n_own, 1), 0) < len_ref[r]
    s_pre = jnp.where(pre_live, s_pre, -1e30)
    s_own = jnp.where(own_live, s_own, -1e30)
    top = jnp.maximum(
        jnp.max(s_pre, axis=0, keepdims=True), jnp.max(s_own, axis=0, keepdims=True)
    )
    top = jnp.maximum(top, -1e29).astype(jnp.bfloat16).astype(jnp.float32)
    w_pre = jnp.exp(s_pre - top)
    w_own = jnp.exp(s_own - top)
    totals = jnp.sum(w_pre, axis=0, keepdims=True) + jnp.sum(w_own, axis=0, keepdims=True)
    acc = jnp.dot(vp_ref[0], w_pre.astype(jnp.bfloat16), preferred_element_type=jnp.float32)
    acc = acc + jnp.dot(
        vo_ref[0, 0], w_own.astype(jnp.bfloat16), preferred_element_type=jnp.float32
    )
    head_dim = acc.shape[0]
    pieces = acc_ref.shape[0] * acc_ref.shape[2]
    width = acc_ref.shape[-1]
    extra = acc_ref.shape[-2] - head_dim
    high = totals.astype(jnp.bfloat16).astype(jnp.float32)
    low = totals - high
    row_id = lax.broadcasted_iota(jnp.int32, (extra, totals.shape[1]), 0)
    stats = jnp.where(row_id == 0, top, jnp.where(row_id == 1, high, jnp.where(row_id == 2, low, 0.0)))
    pair = acc_ref.shape[0]
    for c in range(pieces):
        spot = (c % pair, 0, c // pair, 0)
        acc_ref[spot + (slice(0, head_dim),)] = acc[:, c * width : (c + 1) * width].astype(
            acc_ref.dtype
        )
        acc_ref[spot + (slice(head_dim, None),)] = stats[:, c * width : (c + 1) * width].astype(
            acc_ref.dtype
        )


def context_part(queries, prefix_keys, prefix_values, use_rows, own_lengths, own_keys, own_values, pieces, pair):
    requests, tree_size, heads_dev, head_dim = queries.shape
    block_count, block_len, kv_dev, _ = prefix_keys.shape
    group_size = heads_dev // kv_dev
    private_dev = own_keys.shape[1]
    n_pre = block_count * block_len
    rows = tree_size * group_size
    width = rows // pieces
    kp = jnp.transpose(prefix_keys.reshape(n_pre, kv_dev, head_dim), (1, 0, 2))
    vp = jnp.transpose(prefix_values.reshape(n_pre, kv_dev, head_dim), (1, 2, 0))
    ko = jnp.transpose(own_keys, (0, 2, 1, 3))
    vo = jnp.transpose(own_values, (0, 2, 3, 1))
    grid_spec = pltpu.PrefetchScalarGridSpec(
        num_scalar_prefetch=2,
        grid=(kv_dev, requests),
        in_specs=[
            pl.BlockSpec((1, tree_size, group_size, head_dim), lambda k, r, u, n: (r, 0, k, 0)),
            pl.BlockSpec((1, n_pre, head_dim), lambda k, r, u, n: (k, 0, 0)),
            pl.BlockSpec((1, head_dim, n_pre), lambda k, r, u, n: (k, 0, 0)),
            pl.BlockSpec((1, 1, private_dev, head_dim), lambda k, r, u, n: (r, k, 0, 0)),
            pl.BlockSpec((1, 1, head_dim, private_dev), lambda k, r, u, n: (r, k, 0, 0)),
        ],
        out_specs=pl.BlockSpec(
            (pair, 1, pieces // pair, 1, head_dim + 16, width),
            lambda k, r, u, n: (0, r, 0, k, 0, 0),
        ),
    )
    return pl.pallas_call(
        context_kernel,
        grid_spec=grid_spec,
        out_shape=jax.ShapeDtypeStruct(
            (pair, requests, pieces // pair, kv_dev, head_dim + 16, width), jnp.bfloat16
        ),
    )(use_rows, own_lengths, queries, kp, vp, ko, vo)


SEQ = ("sx", "sy", "sc")


def unpack(parts, head_dim, axis):
    top = parts[:, :, :, head_dim] if axis == 1 else parts[:, :, head_dim]
    high = parts[:, :, :, head_dim + 1] if axis == 1 else parts[:, :, head_dim + 1]
    low = parts[:, :, :, head_dim + 2] if axis == 1 else parts[:, :, head_dim + 2]
    weighted = parts[:, :, :, :head_dim] if axis == 1 else parts[:, :, :head_dim]
    totals = high.astype(jnp.float32) + low.astype(jnp.float32)
    return top.astype(jnp.float32), totals, weighted.astype(jnp.float32)


def local(
    queries,
    prefix_keys,
    prefix_values,
    block_use,
    private_keys,
    private_values,
    private_lengths,
    draft_keys,
    draft_values,
    parents,
    out_weight,
):
    requests, tree_size, heads_dev, head_dim = queries.shape
    kv_dev = prefix_keys.shape[2]
    group_size = heads_dev // kv_dev
    private_dev = private_keys.shape[1]
    scaling = 1.0 / math.sqrt(head_dim)
    shard_index = lax.axis_index(SEQ)
    seq_size = lax.axis_size(SEQ)
    reach = ancestry(parents)
    row_count = requests * tree_size
    chunk = row_count // seq_size
    pieces = tree_size // chunk
    pair = lax.axis_size("sc")
    core = lax.axis_index("sc")
    own_lengths = jnp.clip(private_lengths - shard_index * private_dev, 0, private_dev)
    acc = context_part(
        queries, prefix_keys, prefix_values, block_use, own_lengths, private_keys, private_values, pieces, pair
    )
    width = chunk * group_size
    parts = acc.reshape(pair, seq_size // pair, kv_dev, head_dim + 16, width)
    keep = lax.dynamic_index_in_dim(parts, core, 0, keepdims=False)
    recv = lax.ppermute(parts, "sc", [(i, (i + 1) % pair) for i in range(pair)])
    recv = lax.dynamic_index_in_dim(recv, core, 0, keepdims=False)
    keep = keep.astype(jnp.float32)
    recv = recv.astype(jnp.float32)
    keep_top = keep[:, :, head_dim : head_dim + 1]
    recv_top = recv[:, :, head_dim : head_dim + 1]
    pair_top = jnp.maximum(keep_top, recv_top)
    scaled = keep * jnp.exp(keep_top - pair_top) + recv * jnp.exp(recv_top - pair_top)
    pair_totals = scaled[:, :, head_dim + 1 : head_dim + 2] + scaled[:, :, head_dim + 2 : head_dim + 3]
    high = pair_totals.astype(jnp.bfloat16).astype(jnp.float32)
    low = pair_totals - high
    row = lax.broadcasted_iota(jnp.int32, scaled.shape, 2)
    sent = jnp.where(
        row < head_dim,
        scaled,
        jnp.where(
            row == head_dim,
            pair_top,
            jnp.where(row == head_dim + 1, high, jnp.where(row == head_dim + 2, low, 0.0)),
        ),
    ).astype(jnp.bfloat16)
    got = lax.all_to_all(sent, ("sx", "sy"), 0, 0, tiled=True)
    part_top, part_totals, part_weighted = unpack(got, head_dim, 0)
    top_all = jnp.max(part_top, axis=0)
    factor = jnp.exp(part_top - top_all[None])
    summed_totals = jnp.sum(part_totals * factor, axis=0)
    summed_weighted = jnp.sum(part_weighted * factor[:, :, None, :], axis=0)
    top_all = jnp.transpose(top_all.reshape(kv_dev, chunk, group_size), (1, 0, 2)).reshape(chunk, heads_dev)
    summed_totals = jnp.transpose(
        summed_totals.reshape(kv_dev, chunk, group_size), (1, 0, 2)
    ).reshape(chunk, heads_dev)
    summed_weighted = jnp.transpose(
        summed_weighted.reshape(kv_dev, head_dim, chunk, group_size), (2, 0, 3, 1)
    ).reshape(chunk, heads_dev, head_dim)
    row0 = shard_index * chunk
    request = row0 // tree_size
    token0 = row0 % tree_size
    my_queries = lax.dynamic_slice_in_dim(
        queries.reshape(row_count, heads_dev, head_dim), row0, chunk, 0
    )[None]
    my_keys = lax.dynamic_index_in_dim(draft_keys, request, 0, keepdims=True)
    my_values = lax.dynamic_index_in_dim(draft_values, request, 0, keepdims=True)
    my_reach = lax.dynamic_slice_in_dim(
        lax.dynamic_index_in_dim(reach, request, 0, keepdims=True), token0, chunk, 1
    )
    draft = draft_part(my_queries, my_keys, my_values, my_reach, scaling)
    draft = (draft[0][0], draft[1][0], draft[2][0])
    final_top, final_totals, final_weighted = combine(
        (top_all, summed_totals, summed_weighted), draft
    )
    attention = (final_weighted / final_totals[..., None]).astype(jnp.bfloat16)
    peers = seq_size // pair
    attention = jnp.broadcast_to(attention[None], (peers,) + attention.shape)
    attention = lax.all_to_all(attention, ("sx", "sy"), 0, 0, tiled=True)
    other = lax.ppermute(attention, "sc", [(i, (i + 1) % pair) for i in range(pair)])
    mine = jnp.einsum("xshd,hde->xse", attention, out_weight, preferred_element_type=jnp.float32)
    theirs = jnp.einsum("xshd,hde->xse", other, out_weight, preferred_element_type=jnp.float32)
    first = jnp.where(core == 0, mine, theirs)
    second = jnp.where(core == 0, theirs, mine)
    partial = jnp.stack([first, second], 1)
    heads_size = lax.axis_size("heads")
    partial = partial.reshape(heads_size, requests // heads_size, tree_size, partial.shape[-1])
    return jnp.sum(lax.all_to_all(partial, "heads", 0, 0, tiled=True), axis=0)


def solution(mesh):
    heads_size = mesh.shape["heads"]
    sizes = [mesh.shape["seq"] // 8, 4, 2]
    fine = Mesh(np.asarray(mesh.devices).reshape([heads_size] + sizes), ("heads",) + SEQ)
    return jax.shard_map(
        local,
        mesh=fine,
        in_specs=(
            P(None, None, "heads", None),
            P(SEQ, None, "heads", None),
            P(SEQ, None, "heads", None),
            P(None, SEQ),
            P(None, SEQ, "heads", None),
            P(None, SEQ, "heads", None),
            P(),
            P(None, None, "heads", None),
            P(None, None, "heads", None),
            P(),
            P("heads", None, SEQ),
        ),
        out_specs=P("heads", None, SEQ),
        check_vma=False,
    )
```

```python
import math

import jax
import jax.numpy as jnp
from jax import lax
from jax.experimental import pallas as pl
from jax.experimental.pallas import tpu as pltpu
from jax.sharding import Mesh, PartitionSpec as P
import numpy as np


def ancestry(parents):
    tree_size = parents.shape[-1]
    places = jnp.arange(tree_size, dtype=jnp.int32)
    onestep = (parents[..., None] == places).astype(jnp.float32)
    ident = (places[:, None] == places[None, :]).astype(jnp.float32)
    reach = jnp.maximum(onestep, ident)
    for level in range(max(1, (tree_size - 1).bit_length())):
        reach = jnp.minimum(
            jnp.einsum("rij,rjk->rik", reach, reach, precision=lax.Precision.HIGHEST), 1.0
        )
    return reach


def combine(first, second):
    top = jnp.maximum(first[0], second[0])
    first_factor = jnp.exp(first[0] - top)
    second_factor = jnp.exp(second[0] - top)
    totals = first[1] * first_factor + second[1] * second_factor
    weighted = first[2] * first_factor[..., None] + second[2] * second_factor[..., None]
    return (top, totals, weighted)


def draft_part(row_queries, tree_keys, tree_values, row_reach, scaling):
    requests, rows, heads_dev, head_dim = row_queries.shape
    kv_dev = tree_keys.shape[2]
    group_size = heads_dev // kv_dev
    grouped = row_queries.reshape(requests, rows, kv_dev, group_size, head_dim)
    scores = (
        jnp.einsum("rtkgd,rskd->rtkgs", grouped, tree_keys, preferred_element_type=jnp.float32)
        * scaling
    )
    live = (row_reach > 0.5)[:, :, None, None, :]
    scores = jnp.where(live, scores, -1e30)
    highest = jnp.max(scores, axis=-1)
    weights = jnp.where(live, jnp.exp(scores - highest[..., None]), 0.0)
    totals = jnp.sum(weights, axis=-1)
    weighted = jnp.einsum(
        "rtkgs,rskd->rtkgd",
        weights.astype(jnp.bfloat16),
        tree_values,
        preferred_element_type=jnp.float32,
    )
    return (
        highest.reshape(requests, rows, heads_dev),
        totals.reshape(requests, rows, heads_dev),
        weighted.reshape(requests, rows, heads_dev, head_dim),
    )


def context_kernel(use_ref, len_ref, q_ref, kp_ref, vp_ref, ko_ref, vo_ref, acc_ref):
    r = pl.program_id(1)
    scaling = 1.0 / math.sqrt(q_ref.shape[-1])
    q = q_ref[0].reshape(-1, q_ref.shape[-1])
    kp = kp_ref[0]
    ko = ko_ref[0, 0]
    dims = (((1,), (1,)), ((), ()))
    s_pre = lax.dot_general(kp, q, dims, preferred_element_type=jnp.float32) * scaling
    s_own = lax.dot_general(ko, q, dims, preferred_element_type=jnp.float32) * scaling
    n_pre = kp.shape[0]
    n_own = ko.shape[0]
    block_len = n_pre // use_ref.shape[1]
    block_id = lax.broadcasted_iota(jnp.int32, (n_pre, 1), 0) // block_len
    pre_live = jnp.zeros((n_pre, 1), jnp.bool_)
    for b in range(use_ref.shape[1]):
        pre_live = jnp.logical_or(pre_live, jnp.logical_and(block_id == b, use_ref[r, b] == 1))
    own_live = lax.broadcasted_iota(jnp.int32, (n_own, 1), 0) < len_ref[r]
    s_pre = jnp.where(pre_live, s_pre, -1e30)
    s_own = jnp.where(own_live, s_own, -1e30)
    top = jnp.maximum(
        jnp.max(s_pre, axis=0, keepdims=True), jnp.max(s_own, axis=0, keepdims=True)
    )
    top = jnp.maximum(top, -1e29).astype(jnp.bfloat16).astype(jnp.float32)
    w_pre = jnp.exp(s_pre - top)
    w_own = jnp.exp(s_own - top)
    totals = jnp.sum(w_pre, axis=0, keepdims=True) + jnp.sum(w_own, axis=0, keepdims=True)
    acc = jnp.dot(vp_ref[0], w_pre.astype(jnp.bfloat16), preferred_element_type=jnp.float32)
    acc = acc + jnp.dot(
        vo_ref[0, 0], w_own.astype(jnp.bfloat16), preferred_element_type=jnp.float32
    )
    head_dim = acc.shape[0]
    pieces = acc_ref.shape[0] * acc_ref.shape[2]
    width = acc_ref.shape[-1]
    extra = acc_ref.shape[-2] - head_dim
    high = totals.astype(jnp.bfloat16).astype(jnp.float32)
    low = totals - high
    row_id = lax.broadcasted_iota(jnp.int32, (extra, totals.shape[1]), 0)
    stats = jnp.where(row_id == 0, top, jnp.where(row_id == 1, high, jnp.where(row_id == 2, low, 0.0)))
    pair = acc_ref.shape[0]
    for c in range(pieces):
        spot = (c % pair, 0, c // pair, 0)
        acc_ref[spot + (slice(0, head_dim),)] = acc[:, c * width : (c + 1) * width].astype(
            acc_ref.dtype
        )
        acc_ref[spot + (slice(head_dim, None),)] = stats[:, c * width : (c + 1) * width].astype(
            acc_ref.dtype
        )


def context_part(queries, prefix_keys, prefix_values, use_rows, own_lengths, own_keys, own_values, pieces, pair):
    requests, tree_size, heads_dev, head_dim = queries.shape
    block_count, block_len, kv_dev, _ = prefix_keys.shape
    group_size = heads_dev // kv_dev
    private_dev = own_keys.shape[1]
    n_pre = block_count * block_len
    rows = tree_size * group_size
    width = rows // pieces
    kp = jnp.transpose(prefix_keys.reshape(n_pre, kv_dev, head_dim), (1, 0, 2))
    vp = jnp.transpose(prefix_values.reshape(n_pre, kv_dev, head_dim), (1, 2, 0))
    ko = jnp.transpose(own_keys, (0, 2, 1, 3))
    vo = jnp.transpose(own_values, (0, 2, 3, 1))
    grid_spec = pltpu.PrefetchScalarGridSpec(
        num_scalar_prefetch=2,
        grid=(kv_dev, requests),
        in_specs=[
            pl.BlockSpec((1, tree_size, group_size, head_dim), lambda k, r, u, n: (r, 0, k, 0)),
            pl.BlockSpec((1, n_pre, head_dim), lambda k, r, u, n: (k, 0, 0)),
            pl.BlockSpec((1, head_dim, n_pre), lambda k, r, u, n: (k, 0, 0)),
            pl.BlockSpec((1, 1, private_dev, head_dim), lambda k, r, u, n: (r, k, 0, 0)),
            pl.BlockSpec((1, 1, head_dim, private_dev), lambda k, r, u, n: (r, k, 0, 0)),
        ],
        out_specs=pl.BlockSpec(
            (pair, 1, pieces // pair, 1, head_dim + 16, width),
            lambda k, r, u, n: (0, r, 0, k, 0, 0),
        ),
    )
    return pl.pallas_call(
        context_kernel,
        grid_spec=grid_spec,
        out_shape=jax.ShapeDtypeStruct(
            (pair, requests, pieces // pair, kv_dev, head_dim + 16, width), jnp.bfloat16
        ),
    )(use_rows, own_lengths, queries, kp, vp, ko, vo)


SEQ = ("sx", "sy", "sc")


def pair_kernel(core_ref, keep_ref, recv_ref, out_ref):
    head_dim = out_ref.shape[-2] - 16
    for i in range(out_ref.shape[0]):
        for k in range(out_ref.shape[1]):
            keep = keep_ref[0, i, k].astype(jnp.float32)
            recv = recv_ref[0, i, k].astype(jnp.float32)
            keep_top = keep[head_dim : head_dim + 1]
            recv_top = recv[head_dim : head_dim + 1]
            pair_top = jnp.maximum(keep_top, recv_top)
            scaled = keep * jnp.exp(keep_top - pair_top) + recv * jnp.exp(recv_top - pair_top)
            totals = scaled[head_dim + 1 : head_dim + 2] + scaled[head_dim + 2 : head_dim + 3]
            high = totals.astype(jnp.bfloat16).astype(jnp.float32)
            low = totals - high
            row = lax.broadcasted_iota(jnp.int32, scaled.shape, 0)
            sent = jnp.where(
                row < head_dim,
                scaled,
                jnp.where(
                    row == head_dim,
                    pair_top,
                    jnp.where(row == head_dim + 1, high, jnp.where(row == head_dim + 2, low, 0.0)),
                ),
            )
            out_ref[i, k] = sent.astype(out_ref.dtype)


def pair_combine(core, parts, recv, steps):
    pair, chunks, kv_dev, rows, width = parts.shape
    per = chunks // steps
    block = (1, per, kv_dev, rows, width)
    grid_spec = pltpu.PrefetchScalarGridSpec(
        num_scalar_prefetch=1,
        grid=(steps,),
        in_specs=[
            pl.BlockSpec(block, lambda g, c: (c[0], g, 0, 0, 0)),
            pl.BlockSpec(block, lambda g, c: (c[0], g, 0, 0, 0)),
        ],
        out_specs=pl.BlockSpec((per, kv_dev, rows, width), lambda g, c: (g, 0, 0, 0)),
    )
    return pl.pallas_call(
        pair_kernel,
        grid_spec=grid_spec,
        out_shape=jax.ShapeDtypeStruct((chunks, kv_dev, rows, width), parts.dtype),
    )(core.reshape(1).astype(jnp.int32), parts, recv)


def unpack(parts, head_dim, axis):
    top = parts[:, :, :, head_dim] if axis == 1 else parts[:, :, head_dim]
    high = parts[:, :, :, head_dim + 1] if axis == 1 else parts[:, :, head_dim + 1]
    low = parts[:, :, :, head_dim + 2] if axis == 1 else parts[:, :, head_dim + 2]
    weighted = parts[:, :, :, :head_dim] if axis == 1 else parts[:, :, :head_dim]
    totals = high.astype(jnp.float32) + low.astype(jnp.float32)
    return top.astype(jnp.float32), totals, weighted.astype(jnp.float32)


def local(
    queries,
    prefix_keys,
    prefix_values,
    block_use,
    private_keys,
    private_values,
    private_lengths,
    draft_keys,
    draft_values,
    parents,
    out_weight,
):
    requests, tree_size, heads_dev, head_dim = queries.shape
    kv_dev = prefix_keys.shape[2]
    group_size = heads_dev // kv_dev
    private_dev = private_keys.shape[1]
    scaling = 1.0 / math.sqrt(head_dim)
    shard_index = lax.axis_index(SEQ)
    seq_size = lax.axis_size(SEQ)
    reach = ancestry(parents)
    row_count = requests * tree_size
    chunk = row_count // seq_size
    pieces = tree_size // chunk
    pair = lax.axis_size("sc")
    core = lax.axis_index("sc")
    own_lengths = jnp.clip(private_lengths - shard_index * private_dev, 0, private_dev)
    acc = context_part(
        queries, prefix_keys, prefix_values, block_use, own_lengths, private_keys, private_values, pieces, pair
    )
    width = chunk * group_size
    parts = acc.reshape(pair, seq_size // pair, kv_dev, head_dim + 16, width)
    recv = lax.ppermute(parts, "sc", [(i, (i + 1) % pair) for i in range(pair)])
    sent = pair_combine(core, parts, recv, 4)
    got = lax.all_to_all(sent, ("sx", "sy"), 0, 0, tiled=True)
    part_top, part_totals, part_weighted = unpack(got, head_dim, 0)
    top_all = jnp.max(part_top, axis=0)
    factor = jnp.exp(part_top - top_all[None])
    summed_totals = jnp.sum(part_totals * factor, axis=0)
    summed_weighted = jnp.sum(part_weighted * factor[:, :, None, :], axis=0)
    top_all = jnp.transpose(top_all.reshape(kv_dev, chunk, group_size), (1, 0, 2)).reshape(chunk, heads_dev)
    summed_totals = jnp.transpose(
        summed_totals.reshape(kv_dev, chunk, group_size), (1, 0, 2)
    ).reshape(chunk, heads_dev)
    summed_weighted = jnp.transpose(
        summed_weighted.reshape(kv_dev, head_dim, chunk, group_size), (2, 0, 3, 1)
    ).reshape(chunk, heads_dev, head_dim)
    row0 = shard_index * chunk
    request = row0 // tree_size
    token0 = row0 % tree_size
    my_queries = lax.dynamic_slice_in_dim(
        queries.reshape(row_count, heads_dev, head_dim), row0, chunk, 0
    )[None]
    my_keys = lax.dynamic_index_in_dim(draft_keys, request, 0, keepdims=True)
    my_values = lax.dynamic_index_in_dim(draft_values, request, 0, keepdims=True)
    my_reach = lax.dynamic_slice_in_dim(
        lax.dynamic_index_in_dim(reach, request, 0, keepdims=True), token0, chunk, 1
    )
    draft = draft_part(my_queries, my_keys, my_values, my_reach, scaling)
    draft = (draft[0][0], draft[1][0], draft[2][0])
    final_top, final_totals, final_weighted = combine(
        (top_all, summed_totals, summed_weighted), draft
    )
    attention = (final_weighted / final_totals[..., None]).astype(jnp.bfloat16)
    peers = seq_size // pair
    attention = jnp.broadcast_to(attention[None], (peers,) + attention.shape)
    attention = lax.all_to_all(attention, ("sx", "sy"), 0, 0, tiled=True)
    other = lax.ppermute(attention, "sc", [(i, (i + 1) % pair) for i in range(pair)])
    mine = jnp.einsum("xshd,hde->xse", attention, out_weight, preferred_element_type=jnp.float32)
    theirs = jnp.einsum("xshd,hde->xse", other, out_weight, preferred_element_type=jnp.float32)
    first = jnp.where(core == 0, mine, theirs)
    second = jnp.where(core == 0, theirs, mine)
    partial = jnp.stack([first, second], 1)
    heads_size = lax.axis_size("heads")
    partial = partial.reshape(heads_size, requests // heads_size, tree_size, partial.shape[-1])
    return jnp.sum(lax.all_to_all(partial, "heads", 0, 0, tiled=True), axis=0)


def solution(mesh):
    heads_size = mesh.shape["heads"]
    sizes = [mesh.shape["seq"] // 8, 4, 2]
    fine = Mesh(np.asarray(mesh.devices).reshape([heads_size] + sizes), ("heads",) + SEQ)
    return jax.shard_map(
        local,
        mesh=fine,
        in_specs=(
            P(None, None, "heads", None),
            P(SEQ, None, "heads", None),
            P(SEQ, None, "heads", None),
            P(None, SEQ),
            P(None, SEQ, "heads", None),
            P(None, SEQ, "heads", None),
            P(),
            P(None, None, "heads", None),
            P(None, None, "heads", None),
            P(),
            P("heads", None, SEQ),
        ),
        out_specs=P("heads", None, SEQ),
        check_vma=False,
    )
```

```python
import math

import jax
import jax.numpy as jnp
from jax import lax
from jax.experimental import pallas as pl
from jax.experimental.pallas import tpu as pltpu
from jax.sharding import Mesh, PartitionSpec as P
import numpy as np


def ancestry(parents):
    tree_size = parents.shape[-1]
    places = jnp.arange(tree_size, dtype=jnp.int32)
    onestep = (parents[..., None] == places).astype(jnp.float32)
    ident = (places[:, None] == places[None, :]).astype(jnp.float32)
    reach = jnp.maximum(onestep, ident)
    for level in range(max(1, (tree_size - 1).bit_length())):
        reach = jnp.minimum(
            jnp.einsum("rij,rjk->rik", reach, reach, precision=lax.Precision.HIGHEST), 1.0
        )
    return reach


def combine(first, second):
    top = jnp.maximum(first[0], second[0])
    first_factor = jnp.exp(first[0] - top)
    second_factor = jnp.exp(second[0] - top)
    totals = first[1] * first_factor + second[1] * second_factor
    weighted = first[2] * first_factor[..., None] + second[2] * second_factor[..., None]
    return (top, totals, weighted)


def draft_part(row_queries, tree_keys, tree_values, row_reach, scaling):
    requests, rows, heads_dev, head_dim = row_queries.shape
    kv_dev = tree_keys.shape[2]
    group_size = heads_dev // kv_dev
    grouped = row_queries.reshape(requests, rows, kv_dev, group_size, head_dim)
    scores = (
        jnp.einsum("rtkgd,rskd->rtkgs", grouped, tree_keys, preferred_element_type=jnp.float32)
        * scaling
    )
    live = (row_reach > 0.5)[:, :, None, None, :]
    scores = jnp.where(live, scores, -1e30)
    highest = jnp.max(scores, axis=-1)
    weights = jnp.where(live, jnp.exp(scores - highest[..., None]), 0.0)
    totals = jnp.sum(weights, axis=-1)
    weighted = jnp.einsum(
        "rtkgs,rskd->rtkgd",
        weights.astype(jnp.bfloat16),
        tree_values,
        preferred_element_type=jnp.float32,
    )
    return (
        highest.reshape(requests, rows, heads_dev),
        totals.reshape(requests, rows, heads_dev),
        weighted.reshape(requests, rows, heads_dev, head_dim),
    )


def context_kernel(use_ref, len_ref, core_ref, q_ref, kp_ref, vp_ref, ko_ref, vo_ref, mine_ref, theirs_ref):
    r = pl.program_id(1)
    scaling = 1.0 / math.sqrt(q_ref.shape[-1])
    q = q_ref[0].reshape(-1, q_ref.shape[-1])
    kp = kp_ref[0]
    ko = ko_ref[0, 0]
    dims = (((1,), (1,)), ((), ()))
    s_pre = lax.dot_general(kp, q, dims, preferred_element_type=jnp.float32) * scaling
    s_own = lax.dot_general(ko, q, dims, preferred_element_type=jnp.float32) * scaling
    n_pre = kp.shape[0]
    n_own = ko.shape[0]
    block_len = n_pre // use_ref.shape[1]
    block_id = lax.broadcasted_iota(jnp.int32, (n_pre, 1), 0) // block_len
    pre_live = jnp.zeros((n_pre, 1), jnp.bool_)
    for b in range(use_ref.shape[1]):
        pre_live = jnp.logical_or(pre_live, jnp.logical_and(block_id == b, use_ref[r, b] == 1))
    own_live = lax.broadcasted_iota(jnp.int32, (n_own, 1), 0) < len_ref[r]
    s_pre = jnp.where(pre_live, s_pre, -1e30)
    s_own = jnp.where(own_live, s_own, -1e30)
    top = jnp.maximum(
        jnp.max(s_pre, axis=0, keepdims=True), jnp.max(s_own, axis=0, keepdims=True)
    )
    top = jnp.maximum(top, -1e29).astype(jnp.bfloat16).astype(jnp.float32)
    w_pre = jnp.exp(s_pre - top)
    w_own = jnp.exp(s_own - top)
    totals = jnp.sum(w_pre, axis=0, keepdims=True) + jnp.sum(w_own, axis=0, keepdims=True)
    acc = jnp.dot(vp_ref[0], w_pre.astype(jnp.bfloat16), preferred_element_type=jnp.float32)
    acc = acc + jnp.dot(
        vo_ref[0, 0], w_own.astype(jnp.bfloat16), preferred_element_type=jnp.float32
    )
    head_dim = acc.shape[0]
    pair = 2
    pieces = mine_ref.shape[1] * pair
    width = mine_ref.shape[-1]
    extra = mine_ref.shape[-2] - head_dim
    high = totals.astype(jnp.bfloat16).astype(jnp.float32)
    low = totals - high
    row_id = lax.broadcasted_iota(jnp.int32, (extra, totals.shape[1]), 0)
    stats = jnp.where(row_id == 0, top, jnp.where(row_id == 1, high, jnp.where(row_id == 2, low, 0.0)))
    core = core_ref[0]
    for c in range(pieces):
        body = acc[:, c * width : (c + 1) * width].astype(mine_ref.dtype)
        tail = stats[:, c * width : (c + 1) * width].astype(mine_ref.dtype)
        for half, ref in ((0, mine_ref), (1, theirs_ref)):

            @pl.when((core == c % pair) == (half == 0))
            def _():
                ref[0, c // pair, 0, 0:head_dim, :] = body
                ref[0, c // pair, 0, head_dim:, :] = tail


def context_part(queries, prefix_keys, prefix_values, use_rows, own_lengths, own_keys, own_values, pieces, pair, core):
    requests, tree_size, heads_dev, head_dim = queries.shape
    block_count, block_len, kv_dev, _ = prefix_keys.shape
    group_size = heads_dev // kv_dev
    private_dev = own_keys.shape[1]
    n_pre = block_count * block_len
    rows = tree_size * group_size
    width = rows // pieces
    kp = jnp.transpose(prefix_keys.reshape(n_pre, kv_dev, head_dim), (1, 0, 2))
    vp = jnp.transpose(prefix_values.reshape(n_pre, kv_dev, head_dim), (1, 2, 0))
    ko = jnp.transpose(own_keys, (0, 2, 1, 3))
    vo = jnp.transpose(own_values, (0, 2, 3, 1))
    grid_spec = pltpu.PrefetchScalarGridSpec(
        num_scalar_prefetch=3,
        grid=(kv_dev, requests),
        in_specs=[
            pl.BlockSpec((1, tree_size, group_size, head_dim), lambda k, r, u, n, c: (r, 0, k, 0)),
            pl.BlockSpec((1, n_pre, head_dim), lambda k, r, u, n, c: (k, 0, 0)),
            pl.BlockSpec((1, head_dim, n_pre), lambda k, r, u, n, c: (k, 0, 0)),
            pl.BlockSpec((1, 1, private_dev, head_dim), lambda k, r, u, n, c: (r, k, 0, 0)),
            pl.BlockSpec((1, 1, head_dim, private_dev), lambda k, r, u, n, c: (r, k, 0, 0)),
        ],
        out_specs=[
            pl.BlockSpec((1, pieces // pair, 1, head_dim + 16, width), lambda k, r, u, n, c: (r, 0, k, 0, 0)),
            pl.BlockSpec((1, pieces // pair, 1, head_dim + 16, width), lambda k, r, u, n, c: (r, 0, k, 0, 0)),
        ],
    )
    return pl.pallas_call(
        context_kernel,
        grid_spec=grid_spec,
        out_shape=[
            jax.ShapeDtypeStruct((requests, pieces // pair, kv_dev, head_dim + 16, width), jnp.bfloat16)
        ]
        * 2,
    )(use_rows, own_lengths, core.reshape(1).astype(jnp.int32), queries, kp, vp, ko, vo)


SEQ = ("sx", "sy", "sc")


def pair_kernel(keep_ref, recv_ref, out_ref):
    head_dim = out_ref.shape[-2] - 16
    for i in range(out_ref.shape[0]):
        for k in range(out_ref.shape[1]):
            keep = keep_ref[i, k].astype(jnp.float32)
            recv = recv_ref[i, k].astype(jnp.float32)
            keep_top = keep[head_dim : head_dim + 1]
            recv_top = recv[head_dim : head_dim + 1]
            pair_top = jnp.maximum(keep_top, recv_top)
            keep_factor = jnp.exp(keep_top - pair_top)
            recv_factor = jnp.exp(recv_top - pair_top)
            out_ref[i, k, 0:head_dim] = (
                keep[0:head_dim] * keep_factor + recv[0:head_dim] * recv_factor
            ).astype(out_ref.dtype)
            scaled = keep[head_dim:] * keep_factor + recv[head_dim:] * recv_factor
            totals = scaled[1:2] + scaled[2:3]
            high = totals.astype(jnp.bfloat16).astype(jnp.float32)
            low = totals - high
            row = lax.broadcasted_iota(jnp.int32, scaled.shape, 0)
            sent = jnp.where(
                row == 0,
                pair_top,
                jnp.where(row == 1, high, jnp.where(row == 2, low, 0.0)),
            )
            out_ref[i, k, head_dim:] = sent.astype(out_ref.dtype)


def pair_combine(keep, recv, steps):
    chunks, kv_dev, rows, width = keep.shape
    per = chunks // steps
    block = (per, kv_dev, rows, width)
    return pl.pallas_call(
        pair_kernel,
        grid=(steps,),
        in_specs=[
            pl.BlockSpec(block, lambda g: (g, 0, 0, 0)),
            pl.BlockSpec(block, lambda g: (g, 0, 0, 0)),
        ],
        out_specs=pl.BlockSpec(block, lambda g: (g, 0, 0, 0)),
        out_shape=jax.ShapeDtypeStruct(keep.shape, keep.dtype),
    )(keep, recv)


def unpack(parts, head_dim, axis):
    top = parts[:, :, :, head_dim] if axis == 1 else parts[:, :, head_dim]
    high = parts[:, :, :, head_dim + 1] if axis == 1 else parts[:, :, head_dim + 1]
    low = parts[:, :, :, head_dim + 2] if axis == 1 else parts[:, :, head_dim + 2]
    weighted = parts[:, :, :, :head_dim] if axis == 1 else parts[:, :, :head_dim]
    totals = high.astype(jnp.float32) + low.astype(jnp.float32)
    return top.astype(jnp.float32), totals, weighted.astype(jnp.float32)


def local(
    queries,
    prefix_keys,
    prefix_values,
    block_use,
    private_keys,
    private_values,
    private_lengths,
    draft_keys,
    draft_values,
    parents,
    out_weight,
):
    requests, tree_size, heads_dev, head_dim = queries.shape
    kv_dev = prefix_keys.shape[2]
    group_size = heads_dev // kv_dev
    private_dev = private_keys.shape[1]
    scaling = 1.0 / math.sqrt(head_dim)
    shard_index = lax.axis_index(SEQ)
    seq_size = lax.axis_size(SEQ)
    reach = ancestry(parents)
    row_count = requests * tree_size
    chunk = row_count // seq_size
    pieces = tree_size // chunk
    pair = lax.axis_size("sc")
    core = lax.axis_index("sc")
    own_lengths = jnp.clip(private_lengths - shard_index * private_dev, 0, private_dev)
    mine, theirs = context_part(
        queries, prefix_keys, prefix_values, block_use, own_lengths, private_keys, private_values, pieces, pair, core
    )
    width = chunk * group_size
    keep = mine.reshape(seq_size // pair, kv_dev, head_dim + 16, width)
    recv = lax.ppermute(
        theirs.reshape(keep.shape), "sc", [(i, (i + 1) % pair) for i in range(pair)]
    )
    sent = pair_combine(keep, recv, 4)
    got = lax.all_to_all(sent, ("sx", "sy"), 0, 0, tiled=True)
    part_top, part_totals, part_weighted = unpack(got, head_dim, 0)
    top_all = jnp.max(part_top, axis=0)
    factor = jnp.exp(part_top - top_all[None])
    summed_totals = jnp.sum(part_totals * factor, axis=0)
    summed_weighted = jnp.sum(part_weighted * factor[:, :, None, :], axis=0)
    top_all = jnp.transpose(top_all.reshape(kv_dev, chunk, group_size), (1, 0, 2)).reshape(chunk, heads_dev)
    summed_totals = jnp.transpose(
        summed_totals.reshape(kv_dev, chunk, group_size), (1, 0, 2)
    ).reshape(chunk, heads_dev)
    summed_weighted = jnp.transpose(
        summed_weighted.reshape(kv_dev, head_dim, chunk, group_size), (2, 0, 3, 1)
    ).reshape(chunk, heads_dev, head_dim)
    row0 = shard_index * chunk
    request = row0 // tree_size
    token0 = row0 % tree_size
    my_queries = lax.dynamic_slice_in_dim(
        queries.reshape(row_count, heads_dev, head_dim), row0, chunk, 0
    )[None]
    my_keys = lax.dynamic_index_in_dim(draft_keys, request, 0, keepdims=True)
    my_values = lax.dynamic_index_in_dim(draft_values, request, 0, keepdims=True)
    my_reach = lax.dynamic_slice_in_dim(
        lax.dynamic_index_in_dim(reach, request, 0, keepdims=True), token0, chunk, 1
    )
    draft = draft_part(my_queries, my_keys, my_values, my_reach, scaling)
    draft = (draft[0][0], draft[1][0], draft[2][0])
    final_top, final_totals, final_weighted = combine(
        (top_all, summed_totals, summed_weighted), draft
    )
    attention = (final_weighted / final_totals[..., None]).astype(jnp.bfloat16)
    peers = seq_size // pair
    attention = jnp.broadcast_to(attention[None], (peers,) + attention.shape)
    attention = lax.all_to_all(attention, ("sx", "sy"), 0, 0, tiled=True)
    other = lax.ppermute(attention, "sc", [(i, (i + 1) % pair) for i in range(pair)])
    mine = jnp.einsum("xshd,hde->xse", attention, out_weight, preferred_element_type=jnp.float32)
    theirs = jnp.einsum("xshd,hde->xse", other, out_weight, preferred_element_type=jnp.float32)
    first = jnp.where(core == 0, mine, theirs)
    second = jnp.where(core == 0, theirs, mine)
    partial = jnp.stack([first, second], 1)
    heads_size = lax.axis_size("heads")
    partial = partial.reshape(heads_size, requests // heads_size, tree_size, partial.shape[-1])
    return jnp.sum(lax.all_to_all(partial, "heads", 0, 0, tiled=True), axis=0)


def solution(mesh):
    heads_size = mesh.shape["heads"]
    sizes = [mesh.shape["seq"] // 8, 4, 2]
    fine = Mesh(np.asarray(mesh.devices).reshape([heads_size] + sizes), ("heads",) + SEQ)
    return jax.shard_map(
        local,
        mesh=fine,
        in_specs=(
            P(None, None, "heads", None),
            P(SEQ, None, "heads", None),
            P(SEQ, None, "heads", None),
            P(None, SEQ),
            P(None, SEQ, "heads", None),
            P(None, SEQ, "heads", None),
            P(),
            P(None, None, "heads", None),
            P(None, None, "heads", None),
            P(),
            P("heads", None, SEQ),
        ),
        out_specs=P("heads", None, SEQ),
        check_vma=False,
    )
```

```python
import math

import jax
import jax.numpy as jnp
from jax import lax
from jax.experimental import pallas as pl
from jax.experimental.pallas import tpu as pltpu
from jax.sharding import Mesh, PartitionSpec as P
import numpy as np


def ancestry(parents):
    tree_size = parents.shape[-1]
    places = jnp.arange(tree_size, dtype=jnp.int32)
    onestep = (parents[..., None] == places).astype(jnp.float32)
    ident = (places[:, None] == places[None, :]).astype(jnp.float32)
    reach = jnp.maximum(onestep, ident)
    for level in range(max(1, (tree_size - 1).bit_length())):
        reach = jnp.minimum(
            jnp.einsum("rij,rjk->rik", reach, reach, precision=lax.Precision.HIGHEST), 1.0
        )
    return reach


def combine(first, second):
    top = jnp.maximum(first[0], second[0])
    first_factor = jnp.exp(first[0] - top)
    second_factor = jnp.exp(second[0] - top)
    totals = first[1] * first_factor + second[1] * second_factor
    weighted = first[2] * first_factor[..., None] + second[2] * second_factor[..., None]
    return (top, totals, weighted)


def draft_part(row_queries, tree_keys, tree_values, row_reach, scaling):
    requests, rows, heads_dev, head_dim = row_queries.shape
    kv_dev = tree_keys.shape[2]
    group_size = heads_dev // kv_dev
    grouped = row_queries.reshape(requests, rows, kv_dev, group_size, head_dim)
    scores = (
        jnp.einsum("rtkgd,rskd->rtkgs", grouped, tree_keys, preferred_element_type=jnp.float32)
        * scaling
    )
    live = (row_reach > 0.5)[:, :, None, None, :]
    scores = jnp.where(live, scores, -1e30)
    highest = jnp.max(scores, axis=-1)
    weights = jnp.where(live, jnp.exp(scores - highest[..., None]), 0.0)
    totals = jnp.sum(weights, axis=-1)
    weighted = jnp.einsum(
        "rtkgs,rskd->rtkgd",
        weights.astype(jnp.bfloat16),
        tree_values,
        preferred_element_type=jnp.float32,
    )
    return (
        highest.reshape(requests, rows, heads_dev),
        totals.reshape(requests, rows, heads_dev),
        weighted.reshape(requests, rows, heads_dev, head_dim),
    )


def context_kernel(use_ref, len_ref, core_ref, q_ref, kp_ref, vp_ref, ko_ref, vo_ref, mine_ref, theirs_ref):
    r = pl.program_id(1)
    scaling = 1.0 / math.sqrt(q_ref.shape[-1])
    q = q_ref[0].reshape(-1, q_ref.shape[-1])
    kp = kp_ref[0]
    ko = ko_ref[0, 0]
    dims = (((1,), (1,)), ((), ()))
    s_pre = lax.dot_general(kp, q, dims, preferred_element_type=jnp.float32) * scaling
    s_own = lax.dot_general(ko, q, dims, preferred_element_type=jnp.float32) * scaling
    n_pre = kp.shape[0]
    n_own = ko.shape[0]
    block_len = n_pre // use_ref.shape[1]
    block_id = lax.broadcasted_iota(jnp.int32, (n_pre, 1), 0) // block_len
    pre_live = jnp.zeros((n_pre, 1), jnp.bool_)
    for b in range(use_ref.shape[1]):
        pre_live = jnp.logical_or(pre_live, jnp.logical_and(block_id == b, use_ref[r, b] == 1))
    own_live = lax.broadcasted_iota(jnp.int32, (n_own, 1), 0) < len_ref[r]
    s_pre = jnp.where(pre_live, s_pre, -1e30)
    s_own = jnp.where(own_live, s_own, -1e30)
    top = jnp.maximum(
        jnp.max(s_pre, axis=0, keepdims=True), jnp.max(s_own, axis=0, keepdims=True)
    )
    top = jnp.maximum(top, -1e29).astype(jnp.bfloat16).astype(jnp.float32)
    w_pre = jnp.exp(s_pre - top)
    w_own = jnp.exp(s_own - top)
    totals = jnp.sum(w_pre, axis=0, keepdims=True) + jnp.sum(w_own, axis=0, keepdims=True)
    acc = jnp.dot(vp_ref[0], w_pre.astype(jnp.bfloat16), preferred_element_type=jnp.float32)
    acc = acc + jnp.dot(
        vo_ref[0, 0], w_own.astype(jnp.bfloat16), preferred_element_type=jnp.float32
    )
    head_dim = acc.shape[0]
    pair = 2
    pieces = mine_ref.shape[1] * pair
    width = mine_ref.shape[-1]
    extra = mine_ref.shape[-2] - head_dim
    high = totals.astype(jnp.bfloat16).astype(jnp.float32)
    low = totals - high
    row_id = lax.broadcasted_iota(jnp.int32, (extra, totals.shape[1]), 0)
    stats = jnp.where(row_id == 0, top, jnp.where(row_id == 1, high, jnp.where(row_id == 2, low, 0.0)))
    core = core_ref[0]
    for c in range(pieces):
        body = acc[:, c * width : (c + 1) * width].astype(mine_ref.dtype)
        tail = stats[:, c * width : (c + 1) * width].astype(mine_ref.dtype)
        for half, ref in ((0, mine_ref), (1, theirs_ref)):

            @pl.when((core == c % pair) == (half == 0))
            def _():
                ref[0, c // pair, 0, 0:head_dim, :] = body
                ref[0, c // pair, 0, head_dim:, :] = tail


def context_part(queries, prefix_keys, prefix_values, use_rows, own_lengths, own_keys, own_values, pieces, pair, core):
    requests, tree_size, heads_dev, head_dim = queries.shape
    block_count, block_len, kv_dev, _ = prefix_keys.shape
    group_size = heads_dev // kv_dev
    private_dev = own_keys.shape[1]
    n_pre = block_count * block_len
    rows = tree_size * group_size
    width = rows // pieces
    kp = jnp.transpose(prefix_keys.reshape(n_pre, kv_dev, head_dim), (1, 0, 2))
    vp = jnp.transpose(prefix_values.reshape(n_pre, kv_dev, head_dim), (1, 2, 0))
    ko = jnp.transpose(own_keys, (0, 2, 1, 3))
    vo = jnp.transpose(own_values, (0, 2, 3, 1))
    grid_spec = pltpu.PrefetchScalarGridSpec(
        num_scalar_prefetch=3,
        grid=(kv_dev, requests),
        in_specs=[
            pl.BlockSpec((1, tree_size, group_size, head_dim), lambda k, r, u, n, c: (r, 0, k, 0)),
            pl.BlockSpec((1, n_pre, head_dim), lambda k, r, u, n, c: (k, 0, 0)),
            pl.BlockSpec((1, head_dim, n_pre), lambda k, r, u, n, c: (k, 0, 0)),
            pl.BlockSpec((1, 1, private_dev, head_dim), lambda k, r, u, n, c: (r, k, 0, 0)),
            pl.BlockSpec((1, 1, head_dim, private_dev), lambda k, r, u, n, c: (r, k, 0, 0)),
        ],
        out_specs=[
            pl.BlockSpec((1, pieces // pair, 1, head_dim + 16, width), lambda k, r, u, n, c: (r, 0, k, 0, 0)),
            pl.BlockSpec((1, pieces // pair, 1, head_dim + 16, width), lambda k, r, u, n, c: (r, 0, k, 0, 0)),
        ],
    )
    return pl.pallas_call(
        context_kernel,
        grid_spec=grid_spec,
        out_shape=[
            jax.ShapeDtypeStruct((requests, pieces // pair, kv_dev, head_dim + 16, width), jnp.bfloat16)
        ]
        * 2,
    )(use_rows, own_lengths, core.reshape(1).astype(jnp.int32), queries, kp, vp, ko, vo)


SEQ = ("sx", "sy", "sc")


def pair_kernel(keep_ref, recv_ref, out_ref):
    head_dim = out_ref.shape[-2] - 16
    for i in range(out_ref.shape[0]):
        for k in range(out_ref.shape[1]):
            keep = keep_ref[i, k].astype(jnp.float32)
            recv = recv_ref[i, k].astype(jnp.float32)
            keep_top = keep[head_dim : head_dim + 1]
            recv_top = recv[head_dim : head_dim + 1]
            pair_top = jnp.maximum(keep_top, recv_top)
            keep_factor = jnp.exp(keep_top - pair_top)
            recv_factor = jnp.exp(recv_top - pair_top)
            out_ref[i, k, 0:head_dim] = (
                keep[0:head_dim] * keep_factor + recv[0:head_dim] * recv_factor
            ).astype(out_ref.dtype)
            scaled = keep[head_dim:] * keep_factor + recv[head_dim:] * recv_factor
            totals = scaled[1:2] + scaled[2:3]
            high = totals.astype(jnp.bfloat16).astype(jnp.float32)
            low = totals - high
            row = lax.broadcasted_iota(jnp.int32, scaled.shape, 0)
            sent = jnp.where(
                row == 0,
                pair_top,
                jnp.where(row == 1, high, jnp.where(row == 2, low, 0.0)),
            )
            out_ref[i, k, head_dim:] = sent.astype(out_ref.dtype)


def pair_combine(keep, recv, steps):
    chunks, kv_dev, rows, width = keep.shape
    per = chunks // steps
    block = (per, kv_dev, rows, width)
    return pl.pallas_call(
        pair_kernel,
        grid=(steps,),
        in_specs=[
            pl.BlockSpec(block, lambda g: (g, 0, 0, 0)),
            pl.BlockSpec(block, lambda g: (g, 0, 0, 0)),
        ],
        out_specs=pl.BlockSpec(block, lambda g: (g, 0, 0, 0)),
        out_shape=jax.ShapeDtypeStruct(keep.shape, keep.dtype),
    )(keep, recv)


def unpack(parts, head_dim, axis):
    top = parts[:, :, :, head_dim] if axis == 1 else parts[:, :, head_dim]
    high = parts[:, :, :, head_dim + 1] if axis == 1 else parts[:, :, head_dim + 1]
    low = parts[:, :, :, head_dim + 2] if axis == 1 else parts[:, :, head_dim + 2]
    weighted = parts[:, :, :, :head_dim] if axis == 1 else parts[:, :, :head_dim]
    totals = high.astype(jnp.float32) + low.astype(jnp.float32)
    return top.astype(jnp.float32), totals, weighted.astype(jnp.float32)


def local(
    queries,
    prefix_keys,
    prefix_values,
    block_use,
    private_keys,
    private_values,
    private_lengths,
    draft_keys,
    draft_values,
    parents,
    out_weight,
):
    requests, tree_size, heads_dev, head_dim = queries.shape
    kv_dev = prefix_keys.shape[2]
    group_size = heads_dev // kv_dev
    private_dev = private_keys.shape[1]
    scaling = 1.0 / math.sqrt(head_dim)
    shard_index = lax.axis_index(SEQ)
    seq_size = lax.axis_size(SEQ)
    reach = ancestry(parents)
    row_count = requests * tree_size
    chunk = row_count // seq_size
    pieces = tree_size // chunk
    pair = lax.axis_size("sc")
    core = lax.axis_index("sc")
    own_lengths = jnp.clip(private_lengths - shard_index * private_dev, 0, private_dev)
    mine, theirs = context_part(
        queries, prefix_keys, prefix_values, block_use, own_lengths, private_keys, private_values, pieces, pair, core
    )
    width = chunk * group_size
    keep = mine.reshape(seq_size // pair, kv_dev, head_dim + 16, width)
    recv = lax.ppermute(
        theirs.reshape(keep.shape), "sc", [(i, (i + 1) % pair) for i in range(pair)]
    )
    sent = pair_combine(keep, recv, 2)
    got = lax.all_to_all(sent, ("sx", "sy"), 0, 0, tiled=True)
    part_top, part_totals, part_weighted = unpack(got, head_dim, 0)
    top_all = jnp.max(part_top, axis=0)
    factor = jnp.exp(part_top - top_all[None])
    summed_totals = jnp.sum(part_totals * factor, axis=0)
    summed_weighted = jnp.sum(part_weighted * factor[:, :, None, :], axis=0)
    top_all = jnp.transpose(top_all.reshape(kv_dev, chunk, group_size), (1, 0, 2)).reshape(chunk, heads_dev)
    summed_totals = jnp.transpose(
        summed_totals.reshape(kv_dev, chunk, group_size), (1, 0, 2)
    ).reshape(chunk, heads_dev)
    summed_weighted = jnp.transpose(
        summed_weighted.reshape(kv_dev, head_dim, chunk, group_size), (2, 0, 3, 1)
    ).reshape(chunk, heads_dev, head_dim)
    row0 = shard_index * chunk
    request = row0 // tree_size
    token0 = row0 % tree_size
    my_queries = lax.dynamic_slice_in_dim(
        queries.reshape(row_count, heads_dev, head_dim), row0, chunk, 0
    )[None]
    my_keys = lax.dynamic_index_in_dim(draft_keys, request, 0, keepdims=True)
    my_values = lax.dynamic_index_in_dim(draft_values, request, 0, keepdims=True)
    my_reach = lax.dynamic_slice_in_dim(
        lax.dynamic_index_in_dim(reach, request, 0, keepdims=True), token0, chunk, 1
    )
    draft = draft_part(my_queries, my_keys, my_values, my_reach, scaling)
    draft = (draft[0][0], draft[1][0], draft[2][0])
    final_top, final_totals, final_weighted = combine(
        (top_all, summed_totals, summed_weighted), draft
    )
    attention = (final_weighted / final_totals[..., None]).astype(jnp.bfloat16)
    peers = seq_size // pair
    attention = jnp.broadcast_to(attention[None], (peers,) + attention.shape)
    attention = lax.all_to_all(attention, ("sx", "sy"), 0, 0, tiled=True)
    other = lax.ppermute(attention, "sc", [(i, (i + 1) % pair) for i in range(pair)])
    mine = jnp.einsum("xshd,hde->xse", attention, out_weight, preferred_element_type=jnp.float32)
    theirs = jnp.einsum("xshd,hde->xse", other, out_weight, preferred_element_type=jnp.float32)
    partial = jnp.zeros((mine.shape[0], pair) + mine.shape[1:], mine.dtype)
    partial = lax.dynamic_update_index_in_dim(partial, mine, core, 1)
    partial = lax.dynamic_update_index_in_dim(partial, theirs, pair - 1 - core, 1)
    heads_size = lax.axis_size("heads")
    partial = partial.reshape(heads_size, requests // heads_size, tree_size, partial.shape[-1])
    return jnp.sum(lax.all_to_all(partial, "heads", 0, 0, tiled=True), axis=0)


def solution(mesh):
    heads_size = mesh.shape["heads"]
    sizes = [mesh.shape["seq"] // 8, 4, 2]
    fine = Mesh(np.asarray(mesh.devices).reshape([heads_size] + sizes), ("heads",) + SEQ)
    return jax.shard_map(
        local,
        mesh=fine,
        in_specs=(
            P(None, None, "heads", None),
            P(SEQ, None, "heads", None),
            P(SEQ, None, "heads", None),
            P(None, SEQ),
            P(None, SEQ, "heads", None),
            P(None, SEQ, "heads", None),
            P(),
            P(None, None, "heads", None),
            P(None, None, "heads", None),
            P(),
            P("heads", None, SEQ),
        ),
        out_specs=P("heads", None, SEQ),
        check_vma=False,
    )
```

```python
import math

import jax
import jax.numpy as jnp
from jax import lax
from jax.experimental import pallas as pl
from jax.experimental.pallas import tpu as pltpu
from jax.sharding import Mesh, PartitionSpec as P
import numpy as np


def ancestry(parents):
    tree_size = parents.shape[-1]
    places = jnp.arange(tree_size, dtype=jnp.int32)
    onestep = (parents[..., None] == places).astype(jnp.float32)
    ident = (places[:, None] == places[None, :]).astype(jnp.float32)
    reach = jnp.maximum(onestep, ident)
    for level in range(max(1, (tree_size - 1).bit_length())):
        reach = jnp.minimum(
            jnp.einsum("rij,rjk->rik", reach, reach, precision=lax.Precision.HIGHEST), 1.0
        )
    return reach


def combine(first, second):
    top = jnp.maximum(first[0], second[0])
    first_factor = jnp.exp(first[0] - top)
    second_factor = jnp.exp(second[0] - top)
    totals = first[1] * first_factor + second[1] * second_factor
    weighted = first[2] * first_factor[..., None] + second[2] * second_factor[..., None]
    return (top, totals, weighted)


def draft_part(row_queries, tree_keys, tree_values, row_reach, scaling):
    requests, rows, heads_dev, head_dim = row_queries.shape
    kv_dev = tree_keys.shape[2]
    group_size = heads_dev // kv_dev
    grouped = row_queries.reshape(requests, rows, kv_dev, group_size, head_dim)
    scores = (
        jnp.einsum("rtkgd,rskd->rtkgs", grouped, tree_keys, preferred_element_type=jnp.float32)
        * scaling
    )
    live = (row_reach > 0.5)[:, :, None, None, :]
    scores = jnp.where(live, scores, -1e30)
    highest = jnp.max(scores, axis=-1)
    weights = jnp.where(live, jnp.exp(scores - highest[..., None]), 0.0)
    totals = jnp.sum(weights, axis=-1)
    weighted = jnp.einsum(
        "rtkgs,rskd->rtkgd",
        weights.astype(jnp.bfloat16),
        tree_values,
        preferred_element_type=jnp.float32,
    )
    return (
        highest.reshape(requests, rows, heads_dev),
        totals.reshape(requests, rows, heads_dev),
        weighted.reshape(requests, rows, heads_dev, head_dim),
    )


def context_kernel(use_ref, len_ref, core_ref, q_ref, kp_ref, vp_ref, ko_ref, vo_ref, mine_ref, theirs_ref):
    r = pl.program_id(1)
    scaling = 1.0 / math.sqrt(q_ref.shape[-1])
    q = q_ref[0].reshape(-1, q_ref.shape[-1])
    kp = kp_ref[0]
    ko = ko_ref[0, 0]
    dims = (((1,), (1,)), ((), ()))
    s_pre = lax.dot_general(kp, q, dims, preferred_element_type=jnp.float32) * scaling
    s_own = lax.dot_general(ko, q, dims, preferred_element_type=jnp.float32) * scaling
    n_pre = kp.shape[0]
    n_own = ko.shape[0]
    block_len = n_pre // use_ref.shape[1]
    block_id = lax.broadcasted_iota(jnp.int32, (n_pre, 1), 0) // block_len
    pre_live = jnp.zeros((n_pre, 1), jnp.bool_)
    for b in range(use_ref.shape[1]):
        pre_live = jnp.logical_or(pre_live, jnp.logical_and(block_id == b, use_ref[r, b] == 1))
    own_live = lax.broadcasted_iota(jnp.int32, (n_own, 1), 0) < len_ref[r]
    s_pre = jnp.where(pre_live, s_pre, -1e30)
    s_own = jnp.where(own_live, s_own, -1e30)
    top = jnp.maximum(
        jnp.max(s_pre, axis=0, keepdims=True), jnp.max(s_own, axis=0, keepdims=True)
    )
    top = jnp.maximum(top, -1e29).astype(jnp.bfloat16).astype(jnp.float32)
    w_pre = jnp.exp(s_pre - top)
    w_own = jnp.exp(s_own - top)
    totals = jnp.sum(w_pre, axis=0, keepdims=True) + jnp.sum(w_own, axis=0, keepdims=True)
    acc = jnp.dot(vp_ref[0], w_pre.astype(jnp.bfloat16), preferred_element_type=jnp.float32)
    acc = acc + jnp.dot(
        vo_ref[0, 0], w_own.astype(jnp.bfloat16), preferred_element_type=jnp.float32
    )
    head_dim = acc.shape[0]
    pair = 2
    pieces = mine_ref.shape[1] * pair
    width = mine_ref.shape[-1]
    extra = mine_ref.shape[-2] - head_dim
    high = totals.astype(jnp.bfloat16).astype(jnp.float32)
    low = totals - high
    row_id = lax.broadcasted_iota(jnp.int32, (extra, totals.shape[1]), 0)
    stats = jnp.where(row_id == 0, top, jnp.where(row_id == 1, high, jnp.where(row_id == 2, low, 0.0)))
    core = core_ref[0]
    for c in range(pieces):
        body = acc[:, c * width : (c + 1) * width].astype(mine_ref.dtype)
        tail = stats[:, c * width : (c + 1) * width].astype(mine_ref.dtype)
        for half, ref in ((0, mine_ref), (1, theirs_ref)):

            @pl.when((core == c % pair) == (half == 0))
            def _():
                ref[0, c // pair, 0, 0:head_dim, :] = body
                ref[0, c // pair, 0, head_dim:, :] = tail


def context_part(queries, prefix_keys, prefix_values, use_rows, own_lengths, own_keys, own_values, pieces, pair, core):
    requests, tree_size, heads_dev, head_dim = queries.shape
    block_count, block_len, kv_dev, _ = prefix_keys.shape
    group_size = heads_dev // kv_dev
    private_dev = own_keys.shape[1]
    n_pre = block_count * block_len
    rows = tree_size * group_size
    width = rows // pieces
    kp = jnp.transpose(prefix_keys.reshape(n_pre, kv_dev, head_dim), (1, 0, 2))
    vp = jnp.transpose(prefix_values.reshape(n_pre, kv_dev, head_dim), (1, 2, 0))
    ko = jnp.transpose(own_keys, (0, 2, 1, 3))
    vo = jnp.transpose(own_values, (0, 2, 3, 1))
    grid_spec = pltpu.PrefetchScalarGridSpec(
        num_scalar_prefetch=3,
        grid=(kv_dev, requests),
        in_specs=[
            pl.BlockSpec((1, tree_size, group_size, head_dim), lambda k, r, u, n, c: (r, 0, k, 0)),
            pl.BlockSpec((1, n_pre, head_dim), lambda k, r, u, n, c: (k, 0, 0)),
            pl.BlockSpec((1, head_dim, n_pre), lambda k, r, u, n, c: (k, 0, 0)),
            pl.BlockSpec((1, 1, private_dev, head_dim), lambda k, r, u, n, c: (r, k, 0, 0)),
            pl.BlockSpec((1, 1, head_dim, private_dev), lambda k, r, u, n, c: (r, k, 0, 0)),
        ],
        out_specs=[
            pl.BlockSpec((1, pieces // pair, 1, head_dim + 16, width), lambda k, r, u, n, c: (r, 0, k, 0, 0)),
            pl.BlockSpec((1, pieces // pair, 1, head_dim + 16, width), lambda k, r, u, n, c: (r, 0, k, 0, 0)),
        ],
    )
    return pl.pallas_call(
        context_kernel,
        grid_spec=grid_spec,
        out_shape=[
            jax.ShapeDtypeStruct((requests, pieces // pair, kv_dev, head_dim + 16, width), jnp.bfloat16)
        ]
        * 2,
    )(use_rows, own_lengths, core.reshape(1).astype(jnp.int32), queries, kp, vp, ko, vo)


SEQ = ("sx", "sy", "sc")


def pair_kernel(keep_ref, recv_ref, out_ref):
    head_dim = out_ref.shape[-2] - 16
    for i in range(out_ref.shape[0]):
        for k in range(out_ref.shape[1]):
            keep = keep_ref[i, k].astype(jnp.float32)
            recv = recv_ref[i, k].astype(jnp.float32)
            keep_top = keep[head_dim : head_dim + 1]
            recv_top = recv[head_dim : head_dim + 1]
            pair_top = jnp.maximum(keep_top, recv_top)
            keep_factor = jnp.exp(keep_top - pair_top)
            recv_factor = jnp.exp(recv_top - pair_top)
            out_ref[i, k, 0:head_dim] = (
                keep[0:head_dim] * keep_factor + recv[0:head_dim] * recv_factor
            ).astype(out_ref.dtype)
            scaled = keep[head_dim:] * keep_factor + recv[head_dim:] * recv_factor
            totals = scaled[1:2] + scaled[2:3]
            high = totals.astype(jnp.bfloat16).astype(jnp.float32)
            low = totals - high
            row = lax.broadcasted_iota(jnp.int32, scaled.shape, 0)
            sent = jnp.where(
                row == 0,
                pair_top,
                jnp.where(row == 1, high, jnp.where(row == 2, low, 0.0)),
            )
            out_ref[i, k, head_dim:] = sent.astype(out_ref.dtype)


def pair_combine(keep, recv, steps):
    chunks, kv_dev, rows, width = keep.shape
    per = chunks // steps
    block = (per, kv_dev, rows, width)
    return pl.pallas_call(
        pair_kernel,
        grid=(steps,),
        in_specs=[
            pl.BlockSpec(block, lambda g: (g, 0, 0, 0)),
            pl.BlockSpec(block, lambda g: (g, 0, 0, 0)),
        ],
        out_specs=pl.BlockSpec(block, lambda g: (g, 0, 0, 0)),
        out_shape=jax.ShapeDtypeStruct(keep.shape, keep.dtype),
    )(keep, recv)


def unpack(parts, head_dim, axis):
    top = parts[:, :, :, head_dim] if axis == 1 else parts[:, :, head_dim]
    high = parts[:, :, :, head_dim + 1] if axis == 1 else parts[:, :, head_dim + 1]
    low = parts[:, :, :, head_dim + 2] if axis == 1 else parts[:, :, head_dim + 2]
    weighted = parts[:, :, :, :head_dim] if axis == 1 else parts[:, :, :head_dim]
    totals = high.astype(jnp.float32) + low.astype(jnp.float32)
    return top.astype(jnp.float32), totals, weighted.astype(jnp.float32)


def local(
    queries,
    prefix_keys,
    prefix_values,
    block_use,
    private_keys,
    private_values,
    private_lengths,
    draft_keys,
    draft_values,
    parents,
    out_weight,
):
    requests, tree_size, heads_dev, head_dim = queries.shape
    kv_dev = prefix_keys.shape[2]
    group_size = heads_dev // kv_dev
    private_dev = private_keys.shape[1]
    scaling = 1.0 / math.sqrt(head_dim)
    shard_index = lax.axis_index(SEQ)
    seq_size = lax.axis_size(SEQ)
    reach = ancestry(parents)
    row_count = requests * tree_size
    chunk = row_count // seq_size
    pieces = tree_size // chunk
    pair = lax.axis_size("sc")
    core = lax.axis_index("sc")
    own_lengths = jnp.clip(private_lengths - shard_index * private_dev, 0, private_dev)
    mine, theirs = context_part(
        queries, prefix_keys, prefix_values, block_use, own_lengths, private_keys, private_values, pieces, pair, core
    )
    width = chunk * group_size
    keep = mine.reshape(seq_size // pair, kv_dev, head_dim + 16, width)
    recv = lax.ppermute(
        theirs.reshape(keep.shape), "sc", [(i, (i + 1) % pair) for i in range(pair)]
    )
    sent = pair_combine(keep, recv, 1)
    got = lax.all_to_all(sent, ("sx", "sy"), 0, 0, tiled=True)
    part_top, part_totals, part_weighted = unpack(got, head_dim, 0)
    top_all = jnp.max(part_top, axis=0)
    factor = jnp.exp(part_top - top_all[None])
    summed_totals = jnp.sum(part_totals * factor, axis=0)
    summed_weighted = jnp.sum(part_weighted * factor[:, :, None, :], axis=0)
    top_all = jnp.transpose(top_all.reshape(kv_dev, chunk, group_size), (1, 0, 2)).reshape(chunk, heads_dev)
    summed_totals = jnp.transpose(
        summed_totals.reshape(kv_dev, chunk, group_size), (1, 0, 2)
    ).reshape(chunk, heads_dev)
    summed_weighted = jnp.transpose(
        summed_weighted.reshape(kv_dev, head_dim, chunk, group_size), (2, 0, 3, 1)
    ).reshape(chunk, heads_dev, head_dim)
    row0 = shard_index * chunk
    request = row0 // tree_size
    token0 = row0 % tree_size
    my_queries = lax.dynamic_slice_in_dim(
        queries.reshape(row_count, heads_dev, head_dim), row0, chunk, 0
    )[None]
    my_keys = lax.dynamic_index_in_dim(draft_keys, request, 0, keepdims=True)
    my_values = lax.dynamic_index_in_dim(draft_values, request, 0, keepdims=True)
    my_reach = lax.dynamic_slice_in_dim(
        lax.dynamic_index_in_dim(reach, request, 0, keepdims=True), token0, chunk, 1
    )
    draft = draft_part(my_queries, my_keys, my_values, my_reach, scaling)
    draft = (draft[0][0], draft[1][0], draft[2][0])
    final_top, final_totals, final_weighted = combine(
        (top_all, summed_totals, summed_weighted), draft
    )
    attention = (final_weighted / final_totals[..., None]).astype(jnp.bfloat16)
    peers = seq_size // pair
    attention = jnp.broadcast_to(attention[None], (peers,) + attention.shape)
    attention = lax.all_to_all(attention, ("sx", "sy"), 0, 0, tiled=True)
    other = lax.ppermute(attention, "sc", [(i, (i + 1) % pair) for i in range(pair)])
    mine = jnp.einsum("xshd,hde->xse", attention, out_weight, preferred_element_type=jnp.float32)
    theirs = jnp.einsum("xshd,hde->xse", other, out_weight, preferred_element_type=jnp.float32)
    partial = jnp.zeros((mine.shape[0], pair) + mine.shape[1:], mine.dtype)
    partial = lax.dynamic_update_index_in_dim(partial, mine, core, 1)
    partial = lax.dynamic_update_index_in_dim(partial, theirs, pair - 1 - core, 1)
    heads_size = lax.axis_size("heads")
    partial = partial.reshape(heads_size, requests // heads_size, tree_size, partial.shape[-1])
    return jnp.sum(lax.all_to_all(partial, "heads", 0, 0, tiled=True), axis=0)


def solution(mesh):
    heads_size = mesh.shape["heads"]
    sizes = [mesh.shape["seq"] // 8, 4, 2]
    fine = Mesh(np.asarray(mesh.devices).reshape([heads_size] + sizes), ("heads",) + SEQ)
    return jax.shard_map(
        local,
        mesh=fine,
        in_specs=(
            P(None, None, "heads", None),
            P(SEQ, None, "heads", None),
            P(SEQ, None, "heads", None),
            P(None, SEQ),
            P(None, SEQ, "heads", None),
            P(None, SEQ, "heads", None),
            P(),
            P(None, None, "heads", None),
            P(None, None, "heads", None),
            P(),
            P("heads", None, SEQ),
        ),
        out_specs=P("heads", None, SEQ),
        check_vma=False,
    )
```

```python
import math

import jax
import jax.numpy as jnp
from jax import lax
from jax.experimental import pallas as pl
from jax.experimental.pallas import tpu as pltpu
from jax.sharding import Mesh, PartitionSpec as P
import numpy as np


def ancestry(parents):
    tree_size = parents.shape[-1]
    places = jnp.arange(tree_size, dtype=jnp.int32)
    onestep = (parents[..., None] == places).astype(jnp.float32)
    ident = (places[:, None] == places[None, :]).astype(jnp.float32)
    reach = jnp.maximum(onestep, ident)
    for level in range(max(1, (tree_size - 1).bit_length())):
        reach = jnp.minimum(
            jnp.einsum("rij,rjk->rik", reach, reach, precision=lax.Precision.HIGHEST), 1.0
        )
    return reach


def combine(first, second):
    top = jnp.maximum(first[0], second[0])
    first_factor = jnp.exp(first[0] - top)
    second_factor = jnp.exp(second[0] - top)
    totals = first[1] * first_factor + second[1] * second_factor
    weighted = first[2] * first_factor[..., None] + second[2] * second_factor[..., None]
    return (top, totals, weighted)


def draft_part(row_queries, tree_keys, tree_values, row_reach, scaling):
    requests, rows, heads_dev, head_dim = row_queries.shape
    kv_dev = tree_keys.shape[2]
    group_size = heads_dev // kv_dev
    grouped = row_queries.reshape(requests, rows, kv_dev, group_size, head_dim)
    scores = (
        jnp.einsum("rtkgd,rskd->rtkgs", grouped, tree_keys, preferred_element_type=jnp.float32)
        * scaling
    )
    live = (row_reach > 0.5)[:, :, None, None, :]
    scores = jnp.where(live, scores, -1e30)
    highest = jnp.max(scores, axis=-1)
    weights = jnp.where(live, jnp.exp(scores - highest[..., None]), 0.0)
    totals = jnp.sum(weights, axis=-1)
    weighted = jnp.einsum(
        "rtkgs,rskd->rtkgd",
        weights.astype(jnp.bfloat16),
        tree_values,
        preferred_element_type=jnp.float32,
    )
    return (
        highest.reshape(requests, rows, heads_dev),
        totals.reshape(requests, rows, heads_dev),
        weighted.reshape(requests, rows, heads_dev, head_dim),
    )


def context_kernel(use_ref, len_ref, core_ref, q_ref, kp_ref, vp_ref, ko_ref, vo_ref, mine_ref, theirs_ref):
    r = pl.program_id(1)
    scaling = 1.0 / math.sqrt(q_ref.shape[-1])
    q = q_ref[0].reshape(-1, q_ref.shape[-1])
    kp = kp_ref[0]
    ko = ko_ref[0, 0]
    dims = (((1,), (1,)), ((), ()))
    s_pre = lax.dot_general(kp, q, dims, preferred_element_type=jnp.float32) * scaling
    s_own = lax.dot_general(ko, q, dims, preferred_element_type=jnp.float32) * scaling
    n_pre = kp.shape[0]
    n_own = ko.shape[0]
    block_len = n_pre // use_ref.shape[1]
    block_id = lax.broadcasted_iota(jnp.int32, (n_pre, 1), 0) // block_len
    pre_live = jnp.zeros((n_pre, 1), jnp.bool_)
    for b in range(use_ref.shape[1]):
        pre_live = jnp.logical_or(pre_live, jnp.logical_and(block_id == b, use_ref[r, b] == 1))
    own_live = lax.broadcasted_iota(jnp.int32, (n_own, 1), 0) < len_ref[r]
    s_pre = jnp.where(pre_live, s_pre, -1e30)
    s_own = jnp.where(own_live, s_own, -1e30)
    top = jnp.maximum(
        jnp.max(s_pre, axis=0, keepdims=True), jnp.max(s_own, axis=0, keepdims=True)
    )
    top = jnp.maximum(top, -1e29).astype(jnp.bfloat16).astype(jnp.float32)
    w_pre = jnp.exp(s_pre - top)
    w_own = jnp.exp(s_own - top)
    totals = jnp.sum(w_pre, axis=0, keepdims=True) + jnp.sum(w_own, axis=0, keepdims=True)
    acc = jnp.dot(vp_ref[0], w_pre.astype(jnp.bfloat16), preferred_element_type=jnp.float32)
    acc = acc + jnp.dot(
        vo_ref[0, 0], w_own.astype(jnp.bfloat16), preferred_element_type=jnp.float32
    )
    head_dim = acc.shape[0]
    pair = 2
    pieces = mine_ref.shape[1] * pair
    width = mine_ref.shape[-1]
    extra = mine_ref.shape[-2] - head_dim
    high = totals.astype(jnp.bfloat16).astype(jnp.float32)
    low = totals - high
    row_id = lax.broadcasted_iota(jnp.int32, (extra, totals.shape[1]), 0)
    stats = jnp.where(row_id == 0, top, jnp.where(row_id == 1, high, jnp.where(row_id == 2, low, 0.0)))
    core = core_ref[0]
    for c in range(pieces):
        body = acc[:, c * width : (c + 1) * width].astype(mine_ref.dtype)
        tail = stats[:, c * width : (c + 1) * width].astype(mine_ref.dtype)
        for half, ref in ((0, mine_ref), (1, theirs_ref)):

            @pl.when((core == c % pair) == (half == 0))
            def _():
                ref[0, c // pair, 0, 0:head_dim, :] = body
                ref[0, c // pair, 0, head_dim:, :] = tail


def context_part(queries, prefix_keys, prefix_values, use_rows, own_lengths, own_keys, own_values, pieces, pair, core):
    requests, tree_size, heads_dev, head_dim = queries.shape
    block_count, block_len, kv_dev, _ = prefix_keys.shape
    group_size = heads_dev // kv_dev
    private_dev = own_keys.shape[1]
    n_pre = block_count * block_len
    rows = tree_size * group_size
    width = rows // pieces
    kp = jnp.transpose(prefix_keys.reshape(n_pre, kv_dev, head_dim), (1, 0, 2))
    vp = jnp.transpose(prefix_values.reshape(n_pre, kv_dev, head_dim), (1, 2, 0))
    ko = jnp.transpose(own_keys, (0, 2, 1, 3))
    vo = jnp.transpose(own_values, (0, 2, 3, 1))
    grid_spec = pltpu.PrefetchScalarGridSpec(
        num_scalar_prefetch=3,
        grid=(kv_dev, requests),
        in_specs=[
            pl.BlockSpec((1, tree_size, group_size, head_dim), lambda k, r, u, n, c: (r, 0, k, 0)),
            pl.BlockSpec((1, n_pre, head_dim), lambda k, r, u, n, c: (k, 0, 0)),
            pl.BlockSpec((1, head_dim, n_pre), lambda k, r, u, n, c: (k, 0, 0)),
            pl.BlockSpec((1, 1, private_dev, head_dim), lambda k, r, u, n, c: (r, k, 0, 0)),
            pl.BlockSpec((1, 1, head_dim, private_dev), lambda k, r, u, n, c: (r, k, 0, 0)),
        ],
        out_specs=[
            pl.BlockSpec((1, pieces // pair, 1, head_dim + 16, width), lambda k, r, u, n, c: (r, 0, k, 0, 0)),
            pl.BlockSpec((1, pieces // pair, 1, head_dim + 16, width), lambda k, r, u, n, c: (r, 0, k, 0, 0)),
        ],
    )
    return pl.pallas_call(
        context_kernel,
        grid_spec=grid_spec,
        out_shape=[
            jax.ShapeDtypeStruct((requests, pieces // pair, kv_dev, head_dim + 16, width), jnp.bfloat16)
        ]
        * 2,
    )(use_rows, own_lengths, core.reshape(1).astype(jnp.int32), queries, kp, vp, ko, vo)


SEQ = ("sx", "sy", "sc")


def pair_kernel(keep_ref, recv_ref, out_ref):
    head_dim = out_ref.shape[-2] - 16
    for i in range(out_ref.shape[0]):
        for k in range(out_ref.shape[1]):
            keep = keep_ref[i, k].astype(jnp.float32)
            recv = recv_ref[i, k].astype(jnp.float32)
            keep_top = keep[head_dim : head_dim + 1]
            recv_top = recv[head_dim : head_dim + 1]
            pair_top = jnp.maximum(keep_top, recv_top)
            keep_factor = jnp.exp(keep_top - pair_top)
            recv_factor = jnp.exp(recv_top - pair_top)
            out_ref[i, k, 0:head_dim] = (
                keep[0:head_dim] * keep_factor + recv[0:head_dim] * recv_factor
            ).astype(out_ref.dtype)
            scaled = keep[head_dim:] * keep_factor + recv[head_dim:] * recv_factor
            totals = scaled[1:2] + scaled[2:3]
            high = totals.astype(jnp.bfloat16).astype(jnp.float32)
            low = totals - high
            row = lax.broadcasted_iota(jnp.int32, scaled.shape, 0)
            sent = jnp.where(
                row == 0,
                pair_top,
                jnp.where(row == 1, high, jnp.where(row == 2, low, 0.0)),
            )
            out_ref[i, k, head_dim:] = sent.astype(out_ref.dtype)


def pair_combine(keep, recv, steps):
    chunks, kv_dev, rows, width = keep.shape
    per = chunks // steps
    block = (per, kv_dev, rows, width)
    return pl.pallas_call(
        pair_kernel,
        grid=(steps,),
        in_specs=[
            pl.BlockSpec(block, lambda g: (g, 0, 0, 0)),
            pl.BlockSpec(block, lambda g: (g, 0, 0, 0)),
        ],
        out_specs=pl.BlockSpec(block, lambda g: (g, 0, 0, 0)),
        out_shape=jax.ShapeDtypeStruct(keep.shape, keep.dtype),
    )(keep, recv)


def unpack(parts, head_dim, axis):
    top = parts[:, :, :, head_dim] if axis == 1 else parts[:, :, head_dim]
    high = parts[:, :, :, head_dim + 1] if axis == 1 else parts[:, :, head_dim + 1]
    low = parts[:, :, :, head_dim + 2] if axis == 1 else parts[:, :, head_dim + 2]
    weighted = parts[:, :, :, :head_dim] if axis == 1 else parts[:, :, :head_dim]
    totals = high.astype(jnp.float32) + low.astype(jnp.float32)
    return top.astype(jnp.float32), totals, weighted.astype(jnp.float32)


def local(
    queries,
    prefix_keys,
    prefix_values,
    block_use,
    private_keys,
    private_values,
    private_lengths,
    draft_keys,
    draft_values,
    parents,
    out_weight,
):
    requests, tree_size, heads_dev, head_dim = queries.shape
    kv_dev = prefix_keys.shape[2]
    group_size = heads_dev // kv_dev
    private_dev = private_keys.shape[1]
    scaling = 1.0 / math.sqrt(head_dim)
    shard_index = lax.axis_index(SEQ)
    seq_size = lax.axis_size(SEQ)
    reach = ancestry(parents)
    row_count = requests * tree_size
    chunk = row_count // seq_size
    pieces = tree_size // chunk
    pair = lax.axis_size("sc")
    core = lax.axis_index("sc")
    own_lengths = jnp.clip(private_lengths - shard_index * private_dev, 0, private_dev)
    mine, theirs = context_part(
        queries, prefix_keys, prefix_values, block_use, own_lengths, private_keys, private_values, pieces, pair, core
    )
    width = chunk * group_size
    keep = mine.reshape(seq_size // pair, kv_dev, head_dim + 16, width)
    recv = lax.ppermute(
        theirs.reshape(keep.shape), "sc", [(i, (i + 1) % pair) for i in range(pair)]
    )
    sent = pair_combine(keep, recv, 2)
    got = lax.all_to_all(sent, ("sx", "sy"), 0, 0, tiled=True)
    part_top, part_totals, part_weighted = unpack(got, head_dim, 0)
    top_all = jnp.max(part_top, axis=0)
    factor = jnp.exp(part_top - top_all[None])
    summed_totals = jnp.sum(part_totals * factor, axis=0)
    summed_weighted = jnp.sum(part_weighted * factor[:, :, None, :], axis=0)
    top_all = jnp.transpose(top_all.reshape(kv_dev, chunk, group_size), (1, 0, 2)).reshape(chunk, heads_dev)
    summed_totals = jnp.transpose(
        summed_totals.reshape(kv_dev, chunk, group_size), (1, 0, 2)
    ).reshape(chunk, heads_dev)
    summed_weighted = jnp.transpose(
        summed_weighted.reshape(kv_dev, head_dim, chunk, group_size), (2, 0, 3, 1)
    ).reshape(chunk, heads_dev, head_dim)
    row0 = shard_index * chunk
    request = row0 // tree_size
    token0 = row0 % tree_size
    my_queries = lax.dynamic_slice_in_dim(
        queries.reshape(row_count, heads_dev, head_dim), row0, chunk, 0
    )[None]
    my_keys = lax.dynamic_index_in_dim(draft_keys, request, 0, keepdims=True)
    my_values = lax.dynamic_index_in_dim(draft_values, request, 0, keepdims=True)
    my_reach = lax.dynamic_slice_in_dim(
        lax.dynamic_index_in_dim(reach, request, 0, keepdims=True), token0, chunk, 1
    )
    draft = draft_part(my_queries, my_keys, my_values, my_reach, scaling)
    draft = (draft[0][0], draft[1][0], draft[2][0])
    final_top, final_totals, final_weighted = combine(
        (top_all, summed_totals, summed_weighted), draft
    )
    attention = (final_weighted / final_totals[..., None]).astype(jnp.bfloat16)
    peers = seq_size // pair
    attention = jnp.broadcast_to(attention[None], (peers,) + attention.shape)
    attention = lax.all_to_all(attention, ("sx", "sy"), 0, 0, tiled=True)
    other = lax.ppermute(attention, "sc", [(i, (i + 1) % pair) for i in range(pair)])
    mine = jnp.einsum("xshd,hde->xse", attention, out_weight, preferred_element_type=jnp.float32)
    theirs = jnp.einsum("xshd,hde->xse", other, out_weight, preferred_element_type=jnp.float32)
    partial = jnp.broadcast_to(mine[:, None], (mine.shape[0], pair) + mine.shape[1:])
    partial = lax.dynamic_update_index_in_dim(partial, theirs, pair - 1 - core, 1)
    heads_size = lax.axis_size("heads")
    partial = partial.reshape(heads_size, requests // heads_size, tree_size, partial.shape[-1])
    return jnp.sum(lax.all_to_all(partial, "heads", 0, 0, tiled=True), axis=0)


def solution(mesh):
    heads_size = mesh.shape["heads"]
    sizes = [mesh.shape["seq"] // 8, 4, 2]
    fine = Mesh(np.asarray(mesh.devices).reshape([heads_size] + sizes), ("heads",) + SEQ)
    return jax.shard_map(
        local,
        mesh=fine,
        in_specs=(
            P(None, None, "heads", None),
            P(SEQ, None, "heads", None),
            P(SEQ, None, "heads", None),
            P(None, SEQ),
            P(None, SEQ, "heads", None),
            P(None, SEQ, "heads", None),
            P(),
            P(None, None, "heads", None),
            P(None, None, "heads", None),
            P(),
            P("heads", None, SEQ),
        ),
        out_specs=P("heads", None, SEQ),
        check_vma=False,
    )
```
